32 devices in a mesh: groups: 2 (over y), row: 4 (over z), col: 2 (over x), sub: 2 (over core).
Axes of the slice: x: 2, y: 2, z: 4, core: 2. Of those that a mesh axis runs over, the one named last changes fastest.
Arguments:
- pixels: bfloat16 [4, 4096, 2048], P('groups', ('row', 'col', 'sub')), parts along dimension 0, may hold values from 0.019897461 to 1
Outputs:
- phase: float32 [4, 512, 256], P(('groups', 'sub'), 'row', 'col'), parts along dimension 0
- mean_flux: float32 [4, 512, 256], P(('groups', 'sub'), 'row', 'col'), parts along dimension 0
- spot_size: float32 [4, 512, 256], P(('groups', 'sub'), 'row', 'col'), parts along dimension 0
The draws below stay inside these ranges and needn't reach their ends.
There are 2 independent parts, one for each index of `groups`. The reference program is written for one: setup_inputs(seed, part) draws one part's arguments, and reference() takes and returns one part's arrays. A program takes and returns all parts, laid end to end along the dimension named above; each array names one. Nothing has to cross between parts.
All inputs are finite; a program needn't handle non-finite values.
Results may differ from the reference program's by a relative error of at most 0.0011.
Values sent between devices are 32-bit elements; how exact they have to be, the bound alone decides.
No kernel may reach another device: no remote copies, remote signals or barrier semaphores. Data moves between devices by JAX's collectives and lax.ppermute only.
A program may use at most 128 MiB of HBM per device.

```python
import math
import jax
import jax.numpy as jnp
from jax import lax

PIX = 8
SUBN = 128
MARGIN = 8
FRAMES = 2
NR = 512
NC = 256
N_ROW = 4
N_COL = 2


def steps_of(stream_key, extent, cuts, least, high):
    factor_of = 1.0
    for position, shards_of in cuts:
        heights = jax.random.uniform(jax.random.fold_in(jax.random.fold_in(stream_key, 6), position), (shards_of,), jnp.float32, least / len(cuts), high / len(cuts))
        factor_of = factor_of * jnp.repeat(jnp.exp(heights), extent[position] // shards_of).reshape((-1,) + (1,) * (len(extent) - 1 - position))
    return factor_of


def setup_inputs(seed: int = 0, part: int = 0) -> dict:
    splits = jax.random.split(jax.random.key(seed), 2)
    part_keys = jax.random.split(jax.random.fold_in(splits[1], part), 2)
    pixels = jnp.clip(jnp.exp(math.log(1.0) - 3.9171631 * jax.random.uniform(part_keys[0], (FRAMES, NR * PIX, NC * PIX), jnp.float32) ** steps_of(part_keys[0], (FRAMES, NR * PIX, NC * PIX), ((1, 16),), -0.2, 0.2)), 0.019897461, 1.0).astype(jnp.bfloat16)
    return {"pixels": pixels}


damping = 2e-05

def moment_table():
    offset = jnp.arange(PIX, dtype=jnp.float32) - (PIX - 1) / 2.0
    table = jnp.stack([jnp.ones_like(offset), offset, offset * offset], 1)
    return (table, offset)

def make_basis(count):
    order = jnp.arange(1, count + 1, dtype=jnp.float32)
    angles = math.pi * order[:, None] * order[None, :] / (count + 1)
    vectors = jnp.sqrt(2.0 / (count + 1)) * jnp.sin(angles)
    spectrum = 2.0 - 2.0 * jnp.cos(math.pi * order / (count + 1))
    return (vectors, spectrum[:, None] + spectrum[None, :] + damping)

def coarse_matrix(blocks_down, blocks_across):
    number = blocks_down * blocks_across
    labels = jnp.arange(number, dtype=jnp.int32)
    block_row = labels // blocks_across
    block_col = labels % blocks_across
    apart = jnp.abs(block_row[:, None] - block_row[None, :]) + jnp.abs(block_col[:, None] - block_col[None, :])
    touching = (apart == 1).astype(jnp.float32)
    laplace = jnp.diag(lax.optimization_barrier(jnp.sum(touching, 1))) - touching
    return SUBN * laplace + damping * SUBN * SUBN * jnp.eye(number, dtype=jnp.float32)

def solve_window(window, vectors, denominator):
    highest = lax.Precision.HIGHEST
    inner = jnp.dot(jnp.dot(vectors, window, precision=highest), vectors, precision=highest)
    inner = inner / denominator
    return jnp.dot(jnp.dot(vectors, inner, precision=highest), vectors, precision=highest)

def divergence(flow_x, flow_y):
    from_left = jnp.pad(flow_x, ((0, 0), (1, 0)))[:, :-1]
    from_above = jnp.pad(flow_y, ((1, 0), (0, 0)))[:-1, :]
    return from_left - flow_x + from_above - flow_y

def one_frame(readout):
    table, offset = moment_table()
    blocks = readout.astype(jnp.float32).reshape(NR, PIX, NC, PIX)
    partial_value = jnp.einsum('iajb,bk->kiaj', blocks, table)
    intensity = lax.optimization_barrier(jnp.sum(partial_value[0], 1))
    moment_x = lax.optimization_barrier(jnp.sum(partial_value[1], 1))
    moment_y = lax.optimization_barrier(jnp.sum(partial_value[0] * offset[None, :, None], 1))
    moment_two = lax.optimization_barrier(jnp.sum(partial_value[2], 1)) + lax.optimization_barrier(jnp.sum(partial_value[0] * (offset * offset)[None, :, None], 1))
    slope_x = moment_x / intensity
    slope_y = moment_y / intensity
    spot_size = moment_two / intensity - slope_x * slope_x - slope_y * slope_y
    mean_flux = intensity / (PIX * PIX)
    column = jnp.arange(NC, dtype=jnp.int32)
    rowline = jnp.arange(NR, dtype=jnp.int32)
    flow_x = jnp.where(column[None, :] < NC - 1, slope_x, 0.0)
    flow_y = jnp.where(rowline[:, None] < NR - 1, slope_y, 0.0)
    source = divergence(flow_x, flow_y)
    coarse_rhs = lax.optimization_barrier(jnp.sum(source.reshape(N_ROW, SUBN, N_COL, SUBN), (1, 3))).reshape(-1)
    factor = jnp.linalg.cholesky(coarse_matrix(N_ROW, N_COL))
    coarse_phase = jax.scipy.linalg.cho_solve((factor, True), coarse_rhs)
    count = SUBN + 2 * MARGIN
    vectors, denominator = make_basis(count)
    padded = jnp.pad(source, MARGIN)

    def add_block(label, summed):
        start_row = (label // N_COL * SUBN).astype(jnp.int32)
        start_col = (label % N_COL * SUBN).astype(jnp.int32)
        window = lax.dynamic_slice(padded, (start_row, start_col), (count, count))
        solved = solve_window(window, vectors, denominator)
        current = lax.dynamic_slice(summed, (start_row, start_col), (count, count))
        return lax.dynamic_update_slice(summed, current + solved, (start_row, start_col))
    summed = lax.fori_loop(0, N_ROW * N_COL, add_block, jnp.zeros(padded.shape, jnp.float32))
    coarse_field = jnp.repeat(jnp.repeat(coarse_phase.reshape(N_ROW, N_COL), SUBN, 0), SUBN, 1)
    phase = summed[MARGIN:MARGIN + NR, MARGIN:MARGIN + NC] + coarse_field
    return (phase, mean_flux, spot_size)

def reference(pixels):
    phase, mean_flux, spot_size = lax.map(one_frame, pixels)
    return (phase, mean_flux, spot_size)
```

```python
import functools
import math

import jax
import jax.numpy as jnp
import numpy as np
from jax import lax
from jax.experimental import pallas as pl
from jax.experimental.pallas import tpu as pltpu
from jax.sharding import PartitionSpec as P

PIX = 8
SUBN = 128
MARGIN = 8
WIN = SUBN + 2 * MARGIN
CHUNK = 256
LANES = 128
GROUP = CHUNK // PIX
DAMPING = 2e-05
F32 = jnp.float32
BF16 = jnp.bfloat16


def split_const(values):
    high = np.asarray(values).astype(jnp.bfloat16)
    return high, (values - high.astype(np.float64)).astype(jnp.bfloat16)


def sine_basis():
    order = np.arange(1, WIN + 1, dtype=np.float64)
    vectors = np.sqrt(2.0 / (WIN + 1)) * np.sin(math.pi * order[:, None] * order[None, :] / (WIN + 1))
    spectrum = 2.0 - 2.0 * np.cos(math.pi * order / (WIN + 1))
    return vectors, 1.0 / (spectrum[:, None] + spectrum[None, :] + DAMPING)


def column_basis(blocks):
    vectors, _ = sine_basis()
    table = np.zeros((blocks * SUBN, blocks * WIN))
    for block in range(blocks):
        low = max(block * SUBN - MARGIN, 0)
        high = min((block + 1) * SUBN + MARGIN, blocks * SUBN)
        start = low - (block * SUBN - MARGIN)
        table[low:high, block * WIN : (block + 1) * WIN] = vectors[start : start + high - low]
    return table


def coarse_inverse(blocks_down, blocks_across):
    number = blocks_down * blocks_across
    row, col = np.divmod(np.arange(number), blocks_across)
    apart = np.abs(row[:, None] - row[None, :]) + np.abs(col[:, None] - col[None, :])
    touching = (apart == 1).astype(np.float64)
    laplace = np.diag(touching.sum(1)) - touching
    return np.linalg.inv(SUBN * laplace + DAMPING * SUBN * SUBN * np.eye(number))


def row_moments(stripe):
    offset = np.arange(PIX) - (PIX - 1) / 2.0
    table = np.zeros((3, stripe, stripe * PIX))
    for row in range(stripe):
        for kind in range(3):
            table[kind, row, row * PIX : (row + 1) * PIX] = offset**kind
    return table.reshape(3 * stripe, stripe * PIX).astype(jnp.bfloat16)


def column_moments():
    offset = np.arange(PIX) - (PIX - 1) / 2.0
    places = LANES // GROUP
    table = np.zeros((places, CHUNK, LANES))
    for chunk in range(places):
        for kind in range(3):
            lane = GROUP * ((kind + chunk) % places)
            for cell in range(GROUP):
                table[chunk, cell * PIX : (cell + 1) * PIX, lane + cell] = offset**kind
    return table.astype(jnp.bfloat16)


def halves(values):
    high = values.astype(BF16)
    return high, (values - high.astype(F32)).astype(BF16)


def dot(left, right):
    return jnp.dot(left, right, preferred_element_type=F32)


def dot_three(left, right):
    return dot(left[0], right[0]) + (dot(left[0], right[1]) + dot(left[1], right[0]))


def iota(shape, axis):
    return lax.broadcasted_iota(jnp.int32, shape, axis)


def moments_kernel(sizes, pixels, row_table, col_table, field, extras, held, arrived):
    frames, stripe, blocks, cores, stripes = sizes
    width = blocks * SUBN
    places = LANES // GROUP
    span = LANES * PIX

    def copy(frame, part):
        where = (frame, slice(None), pl.ds(part * span, span))
        return pltpu.make_async_copy(pixels.at[where], held.at[where], arrived.at[frame, part])

    for frame in range(frames):
        for part in range(blocks):
            copy(frame, part).start()
    position = (lax.axis_index("row") * blocks + lax.axis_index("col")) * cores + lax.axis_index("sub")
    group = iota((stripe, LANES), 1) // GROUP

    def gather(pieces, kind):
        total = pieces[-1]
        for chunk in range(places - 1):
            total = jnp.where(group == (kind + chunk) % places, pieces[chunk], total)
        return pltpu.roll(total, LANES - GROUP * kind, 1) if kind else total

    row = iota((stripe, width), 0)
    column = iota((stripe, width), 1)
    for frame in range(frames):
        intensity, moment_x, moment_y, moment_two = [], [], [], []
        for part in range(blocks):
            copy(frame, part).wait()
            lines = dot(row_table[...], held[frame, :, pl.ds(part * span, span)])
            high, low = halves(lines)
            pieces = []
            for chunk in range(places):
                cut = slice(chunk * CHUNK, (chunk + 1) * CHUNK)
                weights = col_table[chunk]
                pieces.append(dot(high[:, cut], weights) + dot(low[:, cut], weights))
            plain = [piece[:stripe] for piece in pieces]
            tilted = [piece[stripe : 2 * stripe] for piece in pieces]
            bent = [piece[2 * stripe :] for piece in pieces]
            intensity.append(gather(plain, 0))
            moment_x.append(gather(plain, 1))
            moment_y.append(gather(tilted, 0))
            moment_two.append(gather(plain, 2) + gather(bent, 0))
        intensity = jnp.concatenate(intensity, 1)
        inverse = 1.0 / intensity
        slope_x = jnp.concatenate(moment_x, 1) * inverse
        slope_y = jnp.concatenate(moment_y, 1) * inverse
        spot_size = jnp.concatenate(moment_two, 1) * inverse - slope_x * slope_x - slope_y * slope_y
        mean_flux = intensity * (1.0 / (PIX * PIX))
        flow_x = jnp.where(column < width - 1, slope_x, 0.0)
        flow_y = jnp.where(position * stripe + row < stripes * stripe - 1, slope_y, 0.0)
        left = jnp.where(column > 0, pltpu.roll(flow_x, 1, 1), 0.0)
        above = pltpu.roll(flow_y, 1, 0)
        source = left - flow_x + jnp.where(row > 0, above, 0.0) - flow_y
        spill = jnp.where(row[:8] == 0, above[:8], 0.0)
        for block in range(blocks):
            target = block * cores + frame
            own = slice(block * SUBN, (block + 1) * SUBN)
            field[target, :stripe, :] = source
            field[target, stripe:, :] = spill
            extras[target, :stripe, :] = mean_flux[:, own]
            extras[target, stripe:, :] = spot_size[:, own]


def rims_kernel(
    sizes, field, basis_high, basis_low, back_high, back_low, drive_high, drive_low, edge_high, edge_low, scale,
    sent, spread, near,
):
    stripe, pieces, blocks, rows = sizes
    width = blocks * SUBN
    mine = lax.axis_index("row")
    side = lax.axis_index("col")
    parts = []
    for piece in range(pieces):
        block = field[piece, :stripe, :]
        if piece:
            head = block[:8] + field[piece - 1, stripe:, :]
            block = head if stripe == 8 else jnp.concatenate([head, block[8:]], 0)
        parts.append(block)
    spill = field[pieces - 1, stripe:, :]
    parts.append(spill)
    source = jnp.concatenate(parts, 0)
    across = dot_three(halves(source), (basis_high[...], basis_low[...]))
    driven = dot_three((drive_high[...], drive_low[...]), halves(across))
    factor = scale[...]
    responses = [driven[k * WIN : (k + 1) * WIN] * factor for k in range(3)]
    response = jnp.concatenate(responses, 0)
    back = (back_high[side], back_low[side])
    reach = dot_three(halves(response), back)
    spread[...] = reach[:WIN]
    edge = (edge_high[...], edge_low[...])
    high, low = halves(reach)
    rims = [
        dot_three(edge, (high[k * WIN : (k + 1) * WIN], low[k * WIN : (k + 1) * WIN])) for k in range(3)
    ]
    near[:8, :] = jnp.where(mine > 0, rims[1][8:], 0.0)
    near[8:, :] = jnp.where(mine < rows - 1, rims[2][:8], 0.0)
    base = 8 * blocks
    tail = sent.shape[1] - base - 8
    total = jnp.sum(source[:SUBN], 0, keepdims=True)
    place = iota((tail, LANES), 0)
    sums = jnp.zeros((tail, LANES), F32)
    for block in range(blocks):
        cut = slice(block * SUBN, (block + 1) * SUBN)
        sums = jnp.where(place == block, total[:, cut], sums)
        sums = jnp.where(place == blocks + block, spill[:1, cut], sums)
    for target in range(rows):
        sent[target, : base + 8, :] = jnp.zeros((base + 8, LANES), F32)
        sent[target, base + 8 :, :] = sums

    def put(target, rim, raw):
        sent[target, base : base + 8, :] = rim
        if raw is not None:
            for block in range(blocks):
                sent[target, 8 * block : 8 * block + 8, :] = raw[:, block * SUBN : (block + 1) * SUBN]

    @pl.when(mine >= 1)
    def _():
        put(mine - 1, rims[0][:8], source[:8])

    @pl.when(mine >= 2)
    def _():
        put(mine - 2, rims[1][:8], None)

    @pl.when(mine + 1 < rows)
    def _():
        put(mine + 1, rims[0][8:], source[SUBN - 8 : SUBN])

    @pl.when(mine + 2 < rows)
    def _():
        put(mine + 2, rims[2][8:], None)


def phase_kernel(
    sizes, received, spread, near, basis_high, basis_low, back_high, back_low, halo_high, halo_low,
    out_high, out_low, scale, coarse, phase,
):
    blocks, rows = sizes
    mine = lax.axis_index("row")
    side = lax.axis_index("col")
    base = 8 * blocks
    tail = received.shape[1] - base - 8
    above = jnp.maximum(mine - 1, 0)
    below = jnp.minimum(mine + 1, rows - 1)
    has_above = mine > 0
    has_below = mine < rows - 1
    first = iota((8, LANES), 0) == 0
    top, bottom, spilt = [], [], []
    for block in range(blocks):
        top.append(jnp.where(has_above, received[above, 8 * block : 8 * block + 8, :], 0.0))
        bottom.append(jnp.where(has_below, received[below, 8 * block : 8 * block + 8, :], 0.0))
        line = received[above, pl.ds(base + 8 + blocks + block, 1), :]
        spilt.append(jnp.where(jnp.logical_and(first, has_above), line, 0.0))
    halo = jnp.concatenate(
        [jnp.concatenate(top, 1), jnp.concatenate(spilt, 1), jnp.concatenate(bottom, 1)], 0
    )
    across = dot_three(halves(halo), (basis_high[...], basis_low[...]))
    driven = dot_three((halo_high[...], halo_low[...]), halves(across))
    reach = dot_three(halves(driven * scale[...]), (back_high[side], back_low[side]))
    solved = dot_three((out_high[...], out_low[...]), halves(spread[...] + reach))
    weighted = jnp.zeros((tail, LANES), F32)
    for origin in range(rows):
        count = jnp.sum(received[origin, base + 8 :, :], 1, keepdims=True)
        weighted = weighted + count * coarse[origin]
    own = iota((tail, LANES), 1) == mine * blocks + side
    level = jnp.sum(jnp.where(own, weighted, 0.0), keepdims=True)
    solved = solved + level
    head = near[:8, :] + jnp.where(has_above, received[above, base : base + 8, :], 0.0)
    head = head + jnp.where(mine > 1, received[jnp.maximum(mine - 2, 0), base : base + 8, :], 0.0)
    foot = near[8:, :] + jnp.where(has_below, received[below, base : base + 8, :], 0.0)
    foot = foot + jnp.where(
        mine < rows - 2, received[jnp.minimum(mine + 2, rows - 1), base : base + 8, :], 0.0
    )
    phase[0, :8, :] = solved[:8] + head
    phase[0, 8 : SUBN - 8, :] = solved[8 : SUBN - 8]
    phase[0, SUBN - 8 :, :] = solved[SUBN - 8 :] + foot


def coarse_table(blocks_down, blocks_across, tail):
    inverse = coarse_inverse(blocks_down, blocks_across)
    number = blocks_down * blocks_across
    lanes = -(-number // LANES) * LANES
    table = np.zeros((blocks_down, tail, lanes), np.float32)
    for row in range(blocks_down):
        for block in range(blocks_across):
            table[row, block, :number] = inverse[row * blocks_across + block]
            if row + 1 < blocks_down:
                table[row, blocks_across + block, :number] = inverse[(row + 1) * blocks_across + block]
    return table


def in_vmem(count):
    return [pl.BlockSpec(memory_space=pltpu.VMEM)] * count


PARAMS = pltpu.CompilerParams(vmem_limit_bytes=48 * 1024 * 1024)


def body(pixels):
    frames, pixel_rows, pixel_cols = pixels.shape
    stripe = pixel_rows // PIX
    width = pixel_cols // PIX
    rows = lax.axis_size("row")
    blocks = lax.axis_size("col")
    cores = lax.axis_size("sub")
    pieces = blocks * cores
    assert frames == cores and width == blocks * SUBN and stripe * pieces == SUBN

    field, extras = pl.pallas_call(
        functools.partial(moments_kernel, (frames, stripe, blocks, cores, rows * pieces)),
        out_shape=(
            jax.ShapeDtypeStruct((pieces, stripe + 8, width), F32),
            jax.ShapeDtypeStruct((pieces, 2 * stripe, SUBN), F32),
        ),
        in_specs=[pl.BlockSpec(memory_space=pl.ANY)] + in_vmem(2),
        out_specs=tuple(in_vmem(2)),
        scratch_shapes=[
            pltpu.VMEM((frames, pixel_rows, pixel_cols), BF16),
            pltpu.SemaphoreType.DMA((frames, blocks)),
        ],
        compiler_params=PARAMS,
        name="moments",
    )(pixels, jnp.asarray(row_moments(stripe)), jnp.asarray(column_moments()))

    field = lax.all_to_all(field, ("col", "sub"), split_axis=0, concat_axis=0, tiled=True)
    extras = lax.all_to_all(extras, ("col", "sub"), split_axis=0, concat_axis=0, tiled=True)

    vectors, scale = sine_basis()
    basis = column_basis(blocks)
    basis_pair = [jnp.asarray(part) for part in split_const(basis)]
    back = basis.T.reshape(blocks * WIN, blocks, SUBN).transpose(1, 0, 2)
    back_pair = [jnp.asarray(part) for part in split_const(back)]
    scale_wide = jnp.asarray(np.tile(scale, (1, blocks)).astype(np.float32))
    reached = SUBN + 8
    drive = np.zeros((3, WIN, reached))
    drive[0] = vectors[:, MARGIN:]
    drive[1, :, :8] = vectors[:, WIN - 8 :]
    drive[2, :, SUBN - 8 : SUBN + 1] = vectors[:, :9]
    drive_pair = [jnp.asarray(part) for part in split_const(drive.reshape(3 * WIN, reached))]
    edge = np.concatenate([vectors[:8], vectors[WIN - 8 :]], 0)
    edge_pair = [jnp.asarray(part) for part in split_const(edge)]
    tail = -(-2 * blocks // 8) * 8
    height = 8 * blocks + 8 + tail

    sent, spread, near = pl.pallas_call(
        functools.partial(rims_kernel, (stripe, pieces, blocks, rows)),
        out_shape=(
            jax.ShapeDtypeStruct((rows, height, LANES), F32),
            jax.ShapeDtypeStruct((WIN, SUBN), F32),
            jax.ShapeDtypeStruct((16, SUBN), F32),
        ),
        in_specs=in_vmem(10),
        out_specs=tuple(in_vmem(3)),
        compiler_params=PARAMS,
        name="rims",
    )(field, *basis_pair, *back_pair, *drive_pair, *edge_pair, scale_wide)

    received = lax.all_to_all(sent, "row", split_axis=0, concat_axis=0, tiled=True)

    halo = np.zeros((WIN, 24))
    halo[:, :9] = vectors[:, :9]
    halo[:, 16:] = vectors[:, WIN - 8 :]
    halo_pair = [jnp.asarray(part) for part in split_const(halo)]
    out_pair = [jnp.asarray(part) for part in split_const(vectors[MARGIN : MARGIN + SUBN])]
    phase = pl.pallas_call(
        functools.partial(phase_kernel, (blocks, rows)),
        out_shape=jax.ShapeDtypeStruct((1, SUBN, SUBN), F32),
        in_specs=in_vmem(13),
        out_specs=pl.BlockSpec(memory_space=pltpu.VMEM),
        compiler_params=PARAMS,
        name="phase",
    )(
        received, spread, near, *basis_pair, *back_pair, *halo_pair, *out_pair, scale_wide,
        jnp.asarray(coarse_table(rows, blocks, tail)),
    )
    mean_flux = extras[:, :stripe].reshape(1, SUBN, SUBN)
    spot_size = extras[:, stripe:].reshape(1, SUBN, SUBN)
    return phase, mean_flux, spot_size


def solution(mesh):
    placed = P(("groups", "sub"), "row", "col")
    return jax.shard_map(
        body,
        mesh=mesh,
        in_specs=(P("groups", ("row", "col", "sub"), None),),
        out_specs=(placed, placed, placed),
        check_vma=False,
    )
```

```python
import functools
import math

import jax
import jax.numpy as jnp
import numpy as np
from jax import lax
from jax.experimental import pallas as pl
from jax.experimental.pallas import tpu as pltpu
from jax.sharding import PartitionSpec as P

PIX = 8
SUBN = 128
MARGIN = 8
WIN = SUBN + 2 * MARGIN
CHUNK = 256
LANES = 128
GROUP = CHUNK // PIX
DAMPING = 2e-05
F32 = jnp.float32
BF16 = jnp.bfloat16


def split_const(values):
    high = np.asarray(values).astype(jnp.bfloat16)
    return high, (values - high.astype(np.float64)).astype(jnp.bfloat16)


def sine_basis():
    order = np.arange(1, WIN + 1, dtype=np.float64)
    vectors = np.sqrt(2.0 / (WIN + 1)) * np.sin(math.pi * order[:, None] * order[None, :] / (WIN + 1))
    spectrum = 2.0 - 2.0 * np.cos(math.pi * order / (WIN + 1))
    return vectors, 1.0 / (spectrum[:, None] + spectrum[None, :] + DAMPING)


def column_basis(blocks):
    vectors, _ = sine_basis()
    table = np.zeros((blocks * SUBN, blocks * WIN))
    for block in range(blocks):
        low = max(block * SUBN - MARGIN, 0)
        high = min((block + 1) * SUBN + MARGIN, blocks * SUBN)
        start = low - (block * SUBN - MARGIN)
        table[low:high, block * WIN : (block + 1) * WIN] = vectors[start : start + high - low]
    return table


def coarse_inverse(blocks_down, blocks_across):
    number = blocks_down * blocks_across
    row, col = np.divmod(np.arange(number), blocks_across)
    apart = np.abs(row[:, None] - row[None, :]) + np.abs(col[:, None] - col[None, :])
    touching = (apart == 1).astype(np.float64)
    laplace = np.diag(touching.sum(1)) - touching
    return np.linalg.inv(SUBN * laplace + DAMPING * SUBN * SUBN * np.eye(number))


def halves(values):
    high = values.astype(BF16)
    return high, (values - high.astype(F32)).astype(BF16)


def dot(left, right):
    return jnp.dot(left, right, preferred_element_type=F32)


def dot_three(left, right):
    return dot(left[0], right[0]) + (dot(left[0], right[1]) + dot(left[1], right[0]))


def iota(shape, axis):
    return lax.broadcasted_iota(jnp.int32, shape, axis)


def power(offset, kind):
    return jnp.where(kind == 0, 1.0, jnp.where(kind == 1, offset, offset * offset))


def offset_of(place):
    return (place % PIX).astype(F32) - (PIX - 1) / 2.0


def row_moments(stripe):
    shape = (3 * stripe, stripe * PIX)
    row, place = iota(shape, 0), iota(shape, 1)
    hit = place // PIX == row % stripe
    return jnp.where(hit, power(offset_of(place), row // stripe), 0.0).astype(BF16)


def column_moments(chunk):
    places = LANES // GROUP
    shape = (CHUNK, LANES)
    place, lane = iota(shape, 0), iota(shape, 1)
    kind = (lane // GROUP + (places - chunk)) % places
    hit = jnp.logical_and(place // PIX == lane % GROUP, kind < 3)
    return jnp.where(hit, power(offset_of(place), kind), 0.0).astype(BF16)


def moments_kernel(sizes, pixels, field, held, arrived):
    frames, stripe, blocks, cores, stripes = sizes
    width = blocks * SUBN
    places = LANES // GROUP
    span = LANES * PIX

    def copy(frame, part):
        where = (frame, slice(None), pl.ds(part * span, span))
        return pltpu.make_async_copy(pixels.at[where], held.at[where], arrived.at[frame, part])

    for frame in range(frames):
        for part in range(blocks):
            copy(frame, part).start()
    row_table = row_moments(stripe)
    col_tables = [column_moments(chunk) for chunk in range(places)]
    position = (lax.axis_index("row") * blocks + lax.axis_index("col")) * cores + lax.axis_index("sub")
    group = iota((stripe, LANES), 1) // GROUP

    def gather(pieces, kind):
        total = pieces[-1]
        for chunk in range(places - 1):
            total = jnp.where(group == (kind + chunk) % places, pieces[chunk], total)
        return pltpu.roll(total, LANES - GROUP * kind, 1) if kind else total

    row = iota((stripe, width), 0)
    column = iota((stripe, width), 1)
    for frame in range(frames):
        intensity, moment_x, moment_y, moment_two = [], [], [], []
        for part in range(blocks):
            copy(frame, part).wait()
            lines = dot(row_table, held[frame, :, pl.ds(part * span, span)])
            high, low = halves(lines)
            pieces = []
            for chunk in range(places):
                cut = slice(chunk * CHUNK, (chunk + 1) * CHUNK)
                weights = col_tables[chunk]
                pieces.append(dot(high[:, cut], weights) + dot(low[:, cut], weights))
            plain = [piece[:stripe] for piece in pieces]
            tilted = [piece[stripe : 2 * stripe] for piece in pieces]
            bent = [piece[2 * stripe :] for piece in pieces]
            intensity.append(gather(plain, 0))
            moment_x.append(gather(plain, 1))
            moment_y.append(gather(tilted, 0))
            moment_two.append(gather(plain, 2) + gather(bent, 0))
        intensity = jnp.concatenate(intensity, 1)
        inverse = 1.0 / intensity
        slope_x = jnp.concatenate(moment_x, 1) * inverse
        slope_y = jnp.concatenate(moment_y, 1) * inverse
        spot_size = jnp.concatenate(moment_two, 1) * inverse - slope_x * slope_x - slope_y * slope_y
        mean_flux = intensity * (1.0 / (PIX * PIX))
        flow_x = jnp.where(column < width - 1, slope_x, 0.0)
        flow_y = jnp.where(position * stripe + row < stripes * stripe - 1, slope_y, 0.0)
        left = jnp.where(column > 0, pltpu.roll(flow_x, 1, 1), 0.0)
        above = pltpu.roll(flow_y, 1, 0)
        source = left - flow_x + jnp.where(row > 0, above, 0.0) - flow_y
        spill = jnp.where(row[:8] == 0, above[:8], 0.0)
        for block in range(blocks):
            target = block * cores + frame
            own = slice(block * SUBN, (block + 1) * SUBN)
            field[target, :stripe, :] = source
            field[target, stripe : stripe + 8, :] = spill
            field[target, stripe + 8 :, :SUBN] = mean_flux[:, own]
            field[target, stripe + 8 :, SUBN : 2 * SUBN] = spot_size[:, own]


def rims_kernel(
    sizes, field, basis_high, basis_low, back_high, back_low, drive_high, drive_low, edge_high, edge_low, scale,
    sent, spread, near,
):
    stripe, pieces, blocks, rows = sizes
    width = blocks * SUBN
    mine = lax.axis_index("row")
    side = lax.axis_index("col")
    parts = []
    for piece in range(pieces):
        block = field[piece, :stripe, :]
        if piece:
            head = block[:8] + field[piece - 1, stripe : stripe + 8, :]
            block = head if stripe == 8 else jnp.concatenate([head, block[8:]], 0)
        parts.append(block)
    spill = field[pieces - 1, stripe : stripe + 8, :]
    parts.append(spill)
    source = jnp.concatenate(parts, 0)
    across = dot_three(halves(source), (basis_high[...], basis_low[...]))
    driven = dot_three((drive_high[...], drive_low[...]), halves(across))
    factor = scale[...]
    responses = [driven[k * WIN : (k + 1) * WIN] * factor for k in range(3)]
    response = jnp.concatenate(responses, 0)
    back = (back_high[side], back_low[side])
    reach = dot_three(halves(response), back)
    spread[...] = reach[:WIN]
    edge = (edge_high[...], edge_low[...])
    high, low = halves(reach)
    rims = [
        dot_three(edge, (high[k * WIN : (k + 1) * WIN], low[k * WIN : (k + 1) * WIN])) for k in range(3)
    ]
    near[:8, :] = jnp.where(mine > 0, rims[1][8:], 0.0)
    near[8:, :] = jnp.where(mine < rows - 1, rims[2][:8], 0.0)
    base = 8 * blocks
    tail = sent.shape[1] - base - 8
    total = jnp.sum(source[:SUBN], 0, keepdims=True)
    place = iota((tail, LANES), 0)
    sums = jnp.zeros((tail, LANES), F32)
    for block in range(blocks):
        cut = slice(block * SUBN, (block + 1) * SUBN)
        sums = jnp.where(place == block, total[:, cut], sums)
        sums = jnp.where(place == blocks + block, spill[:1, cut], sums)
    for target in range(rows):
        sent[target, : base + 8, :] = jnp.zeros((base + 8, LANES), F32)
        sent[target, base + 8 :, :] = sums

    def put(target, rim, raw):
        sent[target, base : base + 8, :] = rim
        if raw is not None:
            for block in range(blocks):
                sent[target, 8 * block : 8 * block + 8, :] = raw[:, block * SUBN : (block + 1) * SUBN]

    @pl.when(mine >= 1)
    def _():
        put(mine - 1, rims[0][:8], source[:8])

    @pl.when(mine >= 2)
    def _():
        put(mine - 2, rims[1][:8], None)

    @pl.when(mine + 1 < rows)
    def _():
        put(mine + 1, rims[0][8:], source[SUBN - 8 : SUBN])

    @pl.when(mine + 2 < rows)
    def _():
        put(mine + 2, rims[2][8:], None)


def phase_kernel(
    sizes, received, spread, near, basis_high, basis_low, back_high, back_low, halo_high, halo_low,
    out_high, out_low, scale, coarse, phase,
):
    blocks, rows = sizes
    mine = lax.axis_index("row")
    side = lax.axis_index("col")
    base = 8 * blocks
    tail = received.shape[1] - base - 8
    above = jnp.maximum(mine - 1, 0)
    below = jnp.minimum(mine + 1, rows - 1)
    has_above = mine > 0
    has_below = mine < rows - 1
    first = iota((8, LANES), 0) == 0
    top, bottom, spilt = [], [], []
    for block in range(blocks):
        top.append(jnp.where(has_above, received[above, 8 * block : 8 * block + 8, :], 0.0))
        bottom.append(jnp.where(has_below, received[below, 8 * block : 8 * block + 8, :], 0.0))
        line = received[above, pl.ds(base + 8 + blocks + block, 1), :]
        spilt.append(jnp.where(jnp.logical_and(first, has_above), line, 0.0))
    halo = jnp.concatenate(
        [jnp.concatenate(top, 1), jnp.concatenate(spilt, 1), jnp.concatenate(bottom, 1)], 0
    )
    across = dot_three(halves(halo), (basis_high[...], basis_low[...]))
    driven = dot_three((halo_high[...], halo_low[...]), halves(across))
    reach = dot_three(halves(driven * scale[...]), (back_high[side], back_low[side]))
    solved = dot_three((out_high[...], out_low[...]), halves(spread[...] + reach))
    weighted = jnp.zeros((tail, LANES), F32)
    for origin in range(rows):
        count = jnp.sum(received[origin, base + 8 :, :], 1, keepdims=True)
        weighted = weighted + count * coarse[origin]
    own = iota((tail, LANES), 1) == mine * blocks + side
    level = jnp.sum(jnp.where(own, weighted, 0.0), keepdims=True)
    solved = solved + level
    head = near[:8, :] + jnp.where(has_above, received[above, base : base + 8, :], 0.0)
    head = head + jnp.where(mine > 1, received[jnp.maximum(mine - 2, 0), base : base + 8, :], 0.0)
    foot = near[8:, :] + jnp.where(has_below, received[below, base : base + 8, :], 0.0)
    foot = foot + jnp.where(
        mine < rows - 2, received[jnp.minimum(mine + 2, rows - 1), base : base + 8, :], 0.0
    )
    phase[0, :8, :] = solved[:8] + head
    phase[0, 8 : SUBN - 8, :] = solved[8 : SUBN - 8]
    phase[0, SUBN - 8 :, :] = solved[SUBN - 8 :] + foot


def coarse_table(blocks_down, blocks_across, tail):
    inverse = coarse_inverse(blocks_down, blocks_across)
    number = blocks_down * blocks_across
    lanes = -(-number // LANES) * LANES
    table = np.zeros((blocks_down, tail, lanes), np.float32)
    for row in range(blocks_down):
        for block in range(blocks_across):
            table[row, block, :number] = inverse[row * blocks_across + block]
            if row + 1 < blocks_down:
                table[row, blocks_across + block, :number] = inverse[(row + 1) * blocks_across + block]
    return table


def in_vmem(count):
    return [pl.BlockSpec(memory_space=pltpu.VMEM)] * count


PARAMS = pltpu.CompilerParams(vmem_limit_bytes=48 * 1024 * 1024)


def body(pixels):
    frames, pixel_rows, pixel_cols = pixels.shape
    stripe = pixel_rows // PIX
    width = pixel_cols // PIX
    rows = lax.axis_size("row")
    blocks = lax.axis_size("col")
    cores = lax.axis_size("sub")
    pieces = blocks * cores
    assert frames == cores and width == blocks * SUBN and stripe * pieces == SUBN

    field = pl.pallas_call(
        functools.partial(moments_kernel, (frames, stripe, blocks, cores, rows * pieces)),
        out_shape=jax.ShapeDtypeStruct((pieces, 2 * stripe + 8, width), F32),
        in_specs=[pl.BlockSpec(memory_space=pltpu.HBM)],
        out_specs=pl.BlockSpec(memory_space=pltpu.VMEM),
        scratch_shapes=[
            pltpu.VMEM((frames, pixel_rows, pixel_cols), BF16),
            pltpu.SemaphoreType.DMA((frames, blocks)),
        ],
        compiler_params=PARAMS,
        name="moments",
    )(pltpu.with_memory_space_constraint(pixels, pltpu.HBM))

    field = lax.all_to_all(field, ("col", "sub"), split_axis=0, concat_axis=0, tiled=True)

    vectors, scale = sine_basis()
    basis = column_basis(blocks)
    basis_pair = [jnp.asarray(part) for part in split_const(basis)]
    back = basis.T.reshape(blocks * WIN, blocks, SUBN).transpose(1, 0, 2)
    back_pair = [jnp.asarray(part) for part in split_const(back)]
    scale_wide = jnp.asarray(np.tile(scale, (1, blocks)).astype(np.float32))
    reached = SUBN + 8
    drive = np.zeros((3, WIN, reached))
    drive[0] = vectors[:, MARGIN:]
    drive[1, :, :8] = vectors[:, WIN - 8 :]
    drive[2, :, SUBN - 8 : SUBN + 1] = vectors[:, :9]
    drive_pair = [jnp.asarray(part) for part in split_const(drive.reshape(3 * WIN, reached))]
    edge = np.concatenate([vectors[:8], vectors[WIN - 8 :]], 0)
    edge_pair = [jnp.asarray(part) for part in split_const(edge)]
    tail = -(-2 * blocks // 8) * 8
    height = 8 * blocks + 8 + tail

    sent, spread, near = pl.pallas_call(
        functools.partial(rims_kernel, (stripe, pieces, blocks, rows)),
        out_shape=(
            jax.ShapeDtypeStruct((rows, height, LANES), F32),
            jax.ShapeDtypeStruct((WIN, SUBN), F32),
            jax.ShapeDtypeStruct((16, SUBN), F32),
        ),
        in_specs=in_vmem(10),
        out_specs=tuple(in_vmem(3)),
        compiler_params=PARAMS,
        name="rims",
    )(field, *basis_pair, *back_pair, *drive_pair, *edge_pair, scale_wide)

    received = lax.all_to_all(sent, "row", split_axis=0, concat_axis=0, tiled=True)

    halo = np.zeros((WIN, 24))
    halo[:, :9] = vectors[:, :9]
    halo[:, 16:] = vectors[:, WIN - 8 :]
    halo_pair = [jnp.asarray(part) for part in split_const(halo)]
    out_pair = [jnp.asarray(part) for part in split_const(vectors[MARGIN : MARGIN + SUBN])]
    phase = pl.pallas_call(
        functools.partial(phase_kernel, (blocks, rows)),
        out_shape=jax.ShapeDtypeStruct((1, SUBN, SUBN), F32),
        in_specs=in_vmem(13),
        out_specs=pl.BlockSpec(memory_space=pltpu.VMEM),
        compiler_params=PARAMS,
        name="phase",
    )(
        received, spread, near, *basis_pair, *back_pair, *halo_pair, *out_pair, scale_wide,
        jnp.asarray(coarse_table(rows, blocks, tail)),
    )
    mean_flux = field[:, stripe + 8 :, :SUBN].reshape(1, SUBN, SUBN)
    spot_size = field[:, stripe + 8 :, SUBN : 2 * SUBN].reshape(1, SUBN, SUBN)
    return phase, mean_flux, spot_size


def solution(mesh):
    placed = P(("groups", "sub"), "row", "col")
    return jax.shard_map(
        body,
        mesh=mesh,
        in_specs=(P("groups", ("row", "col", "sub"), None),),
        out_specs=(placed, placed, placed),
        check_vma=False,
    )
```

```python
import functools
import math

import jax
import jax.numpy as jnp
import numpy as np
from jax import lax
from jax.experimental import pallas as pl
from jax.experimental.pallas import tpu as pltpu
from jax.sharding import PartitionSpec as P

PIX = 8
SUBN = 128
MARGIN = 8
WIN = SUBN + 2 * MARGIN
CHUNK = 256
LANES = 128
GROUP = CHUNK // PIX
DAMPING = 2e-05
F32 = jnp.float32
BF16 = jnp.bfloat16


def constant_pair(values):
    high = np.asarray(values).astype(jnp.bfloat16)
    low = (values - high.astype(np.float64)).astype(jnp.bfloat16)
    return jnp.asarray(high), jnp.asarray(low)


def sine_basis():
    order = np.arange(1, WIN + 1, dtype=np.float64)
    vectors = np.sqrt(2.0 / (WIN + 1)) * np.sin(math.pi * order[:, None] * order[None, :] / (WIN + 1))
    spectrum = 2.0 - 2.0 * np.cos(math.pi * order / (WIN + 1))
    return vectors, 1.0 / (spectrum[:, None] + spectrum[None, :] + DAMPING)


def padded(blocks):
    return -(-blocks * WIN // LANES) * LANES


def column_basis(blocks):
    vectors, _ = sine_basis()
    table = np.zeros((blocks * SUBN, padded(blocks)))
    for block in range(blocks):
        low = max(block * SUBN - MARGIN, 0)
        high = min((block + 1) * SUBN + MARGIN, blocks * SUBN)
        start = low - (block * SUBN - MARGIN)
        table[low:high, block * WIN : (block + 1) * WIN] = vectors[start : start + high - low]
    return table


def widened(table, blocks):
    wide = np.zeros(table.shape[:-1] + (padded(blocks),), np.float32)
    wide[..., : blocks * WIN] = np.tile(table, (1,) * (table.ndim - 1) + (blocks,))
    return wide


def edge_tables():
    vectors, scale = sine_basis()
    ends = np.concatenate([vectors[:8], vectors[WIN - 8 :]], 0)
    def driven_by(rows):
        return np.einsum("oa,ai,ab->iob", ends, vectors[:, rows], scale)
    return driven_by(slice(WIN - 8, WIN)), driven_by(slice(0, 9))


def coarse_inverse(blocks_down, blocks_across):
    number = blocks_down * blocks_across
    row, col = np.divmod(np.arange(number), blocks_across)
    apart = np.abs(row[:, None] - row[None, :]) + np.abs(col[:, None] - col[None, :])
    touching = (apart == 1).astype(np.float64)
    laplace = np.diag(touching.sum(1)) - touching
    return np.linalg.inv(SUBN * laplace + DAMPING * SUBN * SUBN * np.eye(number))


def halves(values):
    high = values.astype(BF16)
    return high, (values - high.astype(F32)).astype(BF16)


def dot(left, right):
    return jnp.dot(left, right, preferred_element_type=F32)


def dot_three(left, right):
    return dot(left[0], right[0]) + (dot(left[0], right[1]) + dot(left[1], right[0]))


def iota(shape, axis):
    return lax.broadcasted_iota(jnp.int32, shape, axis)


def power(offset, kind):
    return jnp.where(kind == 0, 1.0, jnp.where(kind == 1, offset, offset * offset))


def offset_of(place):
    return (place % PIX).astype(F32) - (PIX - 1) / 2.0


def row_moments(stripe):
    shape = (3 * stripe, stripe * PIX)
    row, place = iota(shape, 0), iota(shape, 1)
    hit = place // PIX == row % stripe
    return jnp.where(hit, power(offset_of(place), row // stripe), 0.0).astype(BF16)


def column_moments(chunk):
    places = LANES // GROUP
    shape = (CHUNK, LANES)
    place, lane = iota(shape, 0), iota(shape, 1)
    kind = (lane // GROUP + (places - chunk)) % places
    hit = jnp.logical_and(place // PIX == lane % GROUP, kind < 3)
    return jnp.where(hit, power(offset_of(place), kind), 0.0).astype(BF16)


def moments_kernel(sizes, pixels, field, held, arrived):
    frames, stripe, blocks, cores, stripes = sizes
    width = blocks * SUBN
    places = LANES // GROUP
    span = LANES * PIX

    def copy(frame, part):
        where = (frame, slice(None), pl.ds(part * span, span))
        return pltpu.make_async_copy(pixels.at[where], held.at[where], arrived.at[frame, part])

    for frame in range(frames):
        for part in range(blocks):
            copy(frame, part).start()
    row_table = row_moments(stripe)
    col_tables = [column_moments(chunk) for chunk in range(places)]
    position = (lax.axis_index("row") * blocks + lax.axis_index("col")) * cores + lax.axis_index("sub")
    group = iota((stripe, LANES), 1) // GROUP

    def gather(pieces, kind):
        total = pieces[-1]
        for chunk in range(places - 1):
            total = jnp.where(group == (kind + chunk) % places, pieces[chunk], total)
        return pltpu.roll(total, LANES - GROUP * kind, 1) if kind else total

    row = iota((stripe, width), 0)
    column = iota((stripe, width), 1)

    def columns_of(lines):
        high, low = halves(lines)
        pieces = []
        for chunk in range(places):
            cut = slice(chunk * CHUNK, (chunk + 1) * CHUNK)
            weights = col_tables[chunk]
            pieces.append(dot(high[:, cut], weights) + dot(low[:, cut], weights))
        plain = [piece[:stripe] for piece in pieces]
        tilted = [piece[stripe : 2 * stripe] for piece in pieces]
        bent = [piece[2 * stripe :] for piece in pieces]
        return gather(plain, 0), gather(plain, 1), gather(tilted, 0), gather(plain, 2) + gather(bent, 0)

    def finish(frame, parts):
        intensity, moment_x, moment_y, moment_two = [jnp.concatenate(kind, 1) for kind in zip(*parts)]
        inverse = 1.0 / intensity
        slope_x = moment_x * inverse
        slope_y = moment_y * inverse
        spot_size = moment_two * inverse - slope_x * slope_x - slope_y * slope_y
        mean_flux = intensity * (1.0 / (PIX * PIX))
        flow_x = jnp.where(column < width - 1, slope_x, 0.0)
        flow_y = jnp.where(position * stripe + row < stripes * stripe - 1, slope_y, 0.0)
        left = jnp.where(column > 0, pltpu.roll(flow_x, 1, 1), 0.0)
        above = pltpu.roll(flow_y, 1, 0)
        source = left - flow_x + jnp.where(row > 0, above, 0.0) - flow_y
        spill = jnp.where(row[:8] == 0, above[:8], 0.0)
        for block in range(blocks):
            target = block * cores + frame
            own = slice(block * SUBN, (block + 1) * SUBN)
            field[target, :stripe, :] = source
            field[target, stripe : stripe + 8, :] = spill
            field[target, stripe + 8 :, :SUBN] = mean_flux[:, own]
            field[target, stripe + 8 :, SUBN : 2 * SUBN] = spot_size[:, own]

    waiting, parts = None, []

    def advance():
        frame, lines = waiting
        parts.append(columns_of(lines))
        if len(parts) == blocks:
            finish(frame, parts)
            parts.clear()

    for frame in range(frames):
        for part in range(blocks):
            copy(frame, part).wait()
            lines = dot(row_table, held[frame, :, pl.ds(part * span, span)])
            if waiting is not None:
                advance()
            waiting = (frame, lines)
    advance()


def rims_kernel(
    sizes, field, basis_high, basis_low, back_high, back_low, drive_high, drive_low, edge_high, edge_low, scale,
    above_table, below_table, sent, spectrum, near,
):
    stripe, pieces, blocks, rows = sizes
    tiles = padded(blocks) // LANES
    mine = lax.axis_index("row")
    side = lax.axis_index("col")
    parts = []
    for piece in range(pieces):
        block = field[piece, :stripe, :]
        if piece:
            head = block[:8] + field[piece - 1, stripe : stripe + 8, :]
            block = head if stripe == 8 else jnp.concatenate([head, block[8:]], 0)
        parts.append(block)
    spill = field[pieces - 1, stripe : stripe + 8, :]
    parts.append(spill)
    source = jnp.concatenate(parts, 0)
    across = dot_three(halves(source), (basis_high[...], basis_low[...]))
    driven = dot_three((drive_high[...], drive_low[...]), halves(across))
    response = driven * scale[...]
    spectrum[...] = response
    edges = [dot_three((edge_high[...], edge_low[...]), halves(response))]
    for table, start, count in ((above_table, 0, 8), (below_table, SUBN - 8, 9)):
        total = across[start : start + 1] * table[0]
        for step in range(1, count):
            total = total + across[start + step : start + step + 1] * table[step]
        edges.append(total)
    rims = dot_three(halves(jnp.concatenate(edges, 0)), (back_high[side], back_low[side]))
    near[:8, :] = jnp.where(mine > 0, rims[24:32], 0.0)
    near[8:, :] = jnp.where(mine < rows - 1, rims[32:40], 0.0)
    base = 8 * tiles
    tail = sent.shape[1] - base - 8
    total = jnp.sum(source[:SUBN], 0, keepdims=True)
    place = iota((tail, LANES), 0)
    sums = jnp.zeros((tail, LANES), F32)
    for block in range(blocks):
        cut = slice(block * SUBN, (block + 1) * SUBN)
        sums = jnp.where(place == block, total[:, cut], sums)
        sums = jnp.where(place == blocks + block, spill[:1, cut], sums)
    for tile in range(tiles):
        cut = slice(tile * LANES, (tile + 1) * LANES)
        sums = jnp.where(place == 2 * blocks + tile, across[SUBN : SUBN + 1, cut], sums)
    for target in range(rows):
        sent[target, : base + 8, :] = jnp.zeros((base + 8, LANES), F32)
        sent[target, base + 8 :, :] = sums

    def put(target, rim, lines):
        sent[target, base : base + 8, :] = rim
        if lines is not None:
            for tile in range(tiles):
                sent[target, 8 * tile : 8 * tile + 8, :] = lines[:, tile * LANES : (tile + 1) * LANES]

    @pl.when(mine >= 1)
    def _():
        put(mine - 1, rims[:8], across[:8])

    @pl.when(mine >= 2)
    def _():
        put(mine - 2, rims[16:24], None)

    @pl.when(mine + 1 < rows)
    def _():
        put(mine + 1, rims[8:16], across[SUBN - 8 : SUBN])

    @pl.when(mine + 2 < rows)
    def _():
        put(mine + 2, rims[40:], None)


def phase_kernel(
    sizes, received, spectrum, near, back_high, back_low, halo_high, halo_low, out_high, out_low, scale, coarse,
    phase,
):
    blocks, rows = sizes
    tiles = padded(blocks) // LANES
    mine = lax.axis_index("row")
    side = lax.axis_index("col")
    base = 8 * tiles
    tail = received.shape[1] - base - 8
    above = jnp.maximum(mine - 1, 0)
    below = jnp.minimum(mine + 1, rows - 1)
    has_above = mine > 0
    has_below = mine < rows - 1
    first = iota((8, LANES), 0) == 0
    top, bottom, spilt = [], [], []
    for tile in range(tiles):
        top.append(jnp.where(has_above, received[above, 8 * tile : 8 * tile + 8, :], 0.0))
        bottom.append(jnp.where(has_below, received[below, 8 * tile : 8 * tile + 8, :], 0.0))
        line = received[above, pl.ds(base + 8 + 2 * blocks + tile, 1), :]
        spilt.append(jnp.where(jnp.logical_and(first, has_above), line, 0.0))
    across = jnp.concatenate(
        [jnp.concatenate(top, 1), jnp.concatenate(spilt, 1), jnp.concatenate(bottom, 1)], 0
    )
    driven = dot_three((halo_high[...], halo_low[...]), halves(across))
    response = spectrum[...] + driven * scale[...]
    reach = dot_three(halves(response), (back_high[side], back_low[side]))
    solved = dot_three((out_high[...], out_low[...]), halves(reach))
    weighted = jnp.zeros((tail, coarse.shape[2]), F32)
    for origin in range(rows):
        count = jnp.sum(received[origin, base + 8 :, :], 1, keepdims=True)
        weighted = weighted + count * coarse[origin]
    own = iota(weighted.shape, 1) == mine * blocks + side
    level = jnp.sum(jnp.where(own, weighted, 0.0), keepdims=True)
    solved = solved + level
    head = near[:8, :] + jnp.where(has_above, received[above, base : base + 8, :], 0.0)
    head = head + jnp.where(mine > 1, received[jnp.maximum(mine - 2, 0), base : base + 8, :], 0.0)
    foot = near[8:, :] + jnp.where(has_below, received[below, base : base + 8, :], 0.0)
    foot = foot + jnp.where(
        mine < rows - 2, received[jnp.minimum(mine + 2, rows - 1), base : base + 8, :], 0.0
    )
    phase[0, :8, :] = solved[:8] + head
    phase[0, 8 : SUBN - 8, :] = solved[8 : SUBN - 8]
    phase[0, SUBN - 8 :, :] = solved[SUBN - 8 :] + foot


def coarse_table(blocks_down, blocks_across, tail):
    inverse = coarse_inverse(blocks_down, blocks_across)
    number = blocks_down * blocks_across
    lanes = -(-number // LANES) * LANES
    table = np.zeros((blocks_down, tail, lanes), np.float32)
    for row in range(blocks_down):
        for block in range(blocks_across):
            table[row, block, :number] = inverse[row * blocks_across + block]
            if row + 1 < blocks_down:
                table[row, blocks_across + block, :number] = inverse[(row + 1) * blocks_across + block]
    return table


def in_vmem(count):
    return [pl.BlockSpec(memory_space=pltpu.VMEM)] * count


PARAMS = pltpu.CompilerParams(vmem_limit_bytes=48 * 1024 * 1024)


def body(pixels):
    frames, pixel_rows, pixel_cols = pixels.shape
    stripe = pixel_rows // PIX
    width = pixel_cols // PIX
    rows = lax.axis_size("row")
    blocks = lax.axis_size("col")
    cores = lax.axis_size("sub")
    pieces = blocks * cores
    assert frames == cores and width == blocks * SUBN and stripe * pieces == SUBN

    field = pl.pallas_call(
        functools.partial(moments_kernel, (frames, stripe, blocks, cores, rows * pieces)),
        out_shape=jax.ShapeDtypeStruct((pieces, 2 * stripe + 8, width), F32),
        in_specs=[pl.BlockSpec(memory_space=pltpu.HBM)],
        out_specs=pl.BlockSpec(memory_space=pltpu.VMEM),
        scratch_shapes=[
            pltpu.VMEM((frames, pixel_rows, pixel_cols), BF16),
            pltpu.SemaphoreType.DMA((frames, blocks)),
        ],
        compiler_params=PARAMS,
        name="moments",
    )(pltpu.with_memory_space_constraint(pixels, pltpu.HBM))

    field = lax.all_to_all(field, ("col", "sub"), split_axis=0, concat_axis=0, tiled=True)

    vectors, scale = sine_basis()
    basis = column_basis(blocks)
    full = padded(blocks)
    tiles = full // LANES
    basis_pair = constant_pair(basis)
    back_pair = constant_pair(basis.T.reshape(full, blocks, SUBN).transpose(1, 0, 2))
    scale_wide = jnp.asarray(widened(scale, blocks))
    drive_pair = constant_pair(vectors[:, MARGIN:])
    edge_pair = constant_pair(np.concatenate([vectors[:8], vectors[WIN - 8 :]], 0))
    side_tables = [jnp.asarray(widened(table, blocks)) for table in edge_tables()]
    tail = -(-(2 * blocks + tiles) // 8) * 8
    height = 8 * tiles + 8 + tail

    sent, spectrum, near = pl.pallas_call(
        functools.partial(rims_kernel, (stripe, pieces, blocks, rows)),
        out_shape=(
            jax.ShapeDtypeStruct((rows, height, LANES), F32),
            jax.ShapeDtypeStruct((WIN, full), F32),
            jax.ShapeDtypeStruct((16, SUBN), F32),
        ),
        in_specs=in_vmem(12),
        out_specs=tuple(in_vmem(3)),
        compiler_params=PARAMS,
        name="rims",
    )(field, *basis_pair, *back_pair, *drive_pair, *edge_pair, scale_wide, *side_tables)

    received = lax.all_to_all(sent, "row", split_axis=0, concat_axis=0, tiled=True)

    halo = np.zeros((WIN, 24))
    halo[:, :9] = vectors[:, :9]
    halo[:, 16:] = vectors[:, WIN - 8 :]
    halo_pair = constant_pair(halo)
    out_pair = constant_pair(vectors[MARGIN : MARGIN + SUBN])
    phase = pl.pallas_call(
        functools.partial(phase_kernel, (blocks, rows)),
        out_shape=jax.ShapeDtypeStruct((1, SUBN, SUBN), F32),
        in_specs=in_vmem(11),
        out_specs=pl.BlockSpec(memory_space=pltpu.VMEM),
        compiler_params=PARAMS,
        name="phase",
    )(
        received, spectrum, near, *back_pair, *halo_pair, *out_pair, scale_wide,
        jnp.asarray(coarse_table(rows, blocks, tail)),
    )
    mean_flux = field[:, stripe + 8 :, :SUBN].reshape(1, SUBN, SUBN)
    spot_size = field[:, stripe + 8 :, SUBN : 2 * SUBN].reshape(1, SUBN, SUBN)
    return phase, mean_flux, spot_size


def solution(mesh):
    placed = P(("groups", "sub"), "row", "col")
    return jax.shard_map(
        body,
        mesh=mesh,
        in_specs=(P("groups", ("row", "col", "sub"), None),),
        out_specs=(placed, placed, placed),
        check_vma=False,
    )
```

```python
import functools
import math

import jax
import jax.numpy as jnp
import numpy as np
from jax import lax
from jax.experimental import pallas as pl
from jax.experimental.pallas import tpu as pltpu
from jax.sharding import PartitionSpec as P

PIX = 8
SUBN = 128
MARGIN = 8
WIN = SUBN + 2 * MARGIN
CHUNK = 256
LANES = 128
GROUP = CHUNK // PIX
DAMPING = 2e-05
F32 = jnp.float32
BF16 = jnp.bfloat16


def constant_pair(values):
    high = np.asarray(values).astype(jnp.bfloat16)
    low = (values - high.astype(np.float64)).astype(jnp.bfloat16)
    return jnp.asarray(high), jnp.asarray(low)


def sine_basis():
    order = np.arange(1, WIN + 1, dtype=np.float64)
    vectors = np.sqrt(2.0 / (WIN + 1)) * np.sin(math.pi * order[:, None] * order[None, :] / (WIN + 1))
    spectrum = 2.0 - 2.0 * np.cos(math.pi * order / (WIN + 1))
    return vectors, 1.0 / (spectrum[:, None] + spectrum[None, :] + DAMPING)


def padded(blocks):
    return -(-blocks * WIN // LANES) * LANES


def column_basis(blocks):
    vectors, _ = sine_basis()
    table = np.zeros((blocks * SUBN, padded(blocks)))
    for block in range(blocks):
        low = max(block * SUBN - MARGIN, 0)
        high = min((block + 1) * SUBN + MARGIN, blocks * SUBN)
        start = low - (block * SUBN - MARGIN)
        table[low:high, block * WIN : (block + 1) * WIN] = vectors[start : start + high - low]
    return table


def widened(table, blocks):
    wide = np.zeros(table.shape[:-1] + (padded(blocks),), np.float32)
    wide[..., : blocks * WIN] = np.tile(table, (1,) * (table.ndim - 1) + (blocks,))
    return wide


def edge_tables():
    vectors, scale = sine_basis()
    ends = np.concatenate([vectors[:8], vectors[WIN - 8 :]], 0)
    def driven_by(rows):
        return np.einsum("oa,ai,ab->iob", ends, vectors[:, rows], scale)
    return driven_by(slice(WIN - 8, WIN)), driven_by(slice(0, 9))


def coarse_inverse(blocks_down, blocks_across):
    number = blocks_down * blocks_across
    row, col = np.divmod(np.arange(number), blocks_across)
    apart = np.abs(row[:, None] - row[None, :]) + np.abs(col[:, None] - col[None, :])
    touching = (apart == 1).astype(np.float64)
    laplace = np.diag(touching.sum(1)) - touching
    return np.linalg.inv(SUBN * laplace + DAMPING * SUBN * SUBN * np.eye(number))


def halves(values):
    high = values.astype(BF16)
    return high, (values - high.astype(F32)).astype(BF16)


def dot(left, right):
    return jnp.dot(left, right, preferred_element_type=F32)


def dot_three(left, right):
    return dot(left[0], right[0]) + (dot(left[0], right[1]) + dot(left[1], right[0]))


def iota(shape, axis):
    return lax.broadcasted_iota(jnp.int32, shape, axis)


def power(offset, kind):
    return jnp.where(kind == 0, 1.0, jnp.where(kind == 1, offset, offset * offset))


def offset_of(place):
    return (place % PIX).astype(F32) - (PIX - 1) / 2.0


def row_moments(stripe):
    shape = (3 * stripe, stripe * PIX)
    row, place = iota(shape, 0), iota(shape, 1)
    hit = place // PIX == row % stripe
    return jnp.where(hit, power(offset_of(place), row // stripe), 0.0).astype(BF16)


def column_moments(chunk):
    places = LANES // GROUP
    shape = (CHUNK, LANES)
    place, lane = iota(shape, 0), iota(shape, 1)
    kind = (lane // GROUP + (places - chunk)) % places
    hit = jnp.logical_and(place // PIX == lane % GROUP, kind < 3)
    return jnp.where(hit, power(offset_of(place), kind), 0.0).astype(BF16)


def moments_kernel(sizes, pixels, field, held, arrived):
    frames, stripe, blocks, cores, stripes = sizes
    width = blocks * SUBN
    places = LANES // GROUP
    span = LANES * PIX

    def copy(frame, part):
        where = (frame, slice(None), pl.ds(part * span, span))
        return pltpu.make_async_copy(pixels.at[where], held.at[where], arrived.at[frame, part])

    for frame in range(frames):
        for part in range(blocks):
            copy(frame, part).start()
    row_table = row_moments(stripe)
    col_tables = [column_moments(chunk) for chunk in range(places)]
    position = (lax.axis_index("row") * blocks + lax.axis_index("col")) * cores + lax.axis_index("sub")
    group = iota((stripe, LANES), 1) // GROUP

    def gather(pieces, kind):
        total = pieces[-1]
        for chunk in range(places - 1):
            total = jnp.where(group == (kind + chunk) % places, pieces[chunk], total)
        return pltpu.roll(total, LANES - GROUP * kind, 1) if kind else total

    row = iota((stripe, width), 0)
    column = iota((stripe, width), 1)

    def columns_of(lines):
        high, low = halves(lines)
        pieces = []
        for chunk in range(places):
            cut = slice(chunk * CHUNK, (chunk + 1) * CHUNK)
            weights = col_tables[chunk]
            pieces.append(dot(high[:, cut], weights) + dot(low[:, cut], weights))
        plain = [piece[:stripe] for piece in pieces]
        tilted = [piece[stripe : 2 * stripe] for piece in pieces]
        bent = [piece[2 * stripe :] for piece in pieces]
        return gather(plain, 0), gather(plain, 1), gather(tilted, 0), gather(plain, 2) + gather(bent, 0)

    def finish(frame, parts):
        intensity, moment_x, moment_y, moment_two = [jnp.concatenate(kind, 1) for kind in zip(*parts)]
        inverse = 1.0 / intensity
        slope_x = moment_x * inverse
        slope_y = moment_y * inverse
        spot_size = moment_two * inverse - slope_x * slope_x - slope_y * slope_y
        mean_flux = intensity * (1.0 / (PIX * PIX))
        flow_x = jnp.where(column < width - 1, slope_x, 0.0)
        flow_y = jnp.where(position * stripe + row < stripes * stripe - 1, slope_y, 0.0)
        left = jnp.where(column > 0, pltpu.roll(flow_x, 1, 1), 0.0)
        above = pltpu.roll(flow_y, 1, 0)
        source = left - flow_x + jnp.where(row > 0, above, 0.0) - flow_y
        spill = jnp.where(row[:8] == 0, above[:8], 0.0)
        for block in range(blocks):
            target = block * cores + frame
            own = slice(block * SUBN, (block + 1) * SUBN)
            field[target, :stripe, :] = source
            field[target, stripe : stripe + 8, :] = spill
            field[target, stripe + 8 :, :SUBN] = mean_flux[:, own]
            field[target, stripe + 8 :, SUBN : 2 * SUBN] = spot_size[:, own]

    def lines_of(frame):
        for part in range(blocks):
            copy(frame, part).wait()
        return [dot(row_table, held[frame, :, pl.ds(part * span, span)]) for part in range(blocks)]

    lines = [lines_of(frame) for frame in range(frames)]
    for frame in range(frames):
        finish(frame, [columns_of(part) for part in lines[frame]])


def rims_kernel(
    sizes, field, basis_high, basis_low, back_high, back_low, drive_high, drive_low, edge_high, edge_low, scale,
    above_table, below_table, sent, spectrum, near,
):
    stripe, pieces, blocks, rows = sizes
    tiles = padded(blocks) // LANES
    mine = lax.axis_index("row")
    side = lax.axis_index("col")
    parts = []
    for piece in range(pieces):
        block = field[piece, :stripe, :]
        if piece:
            head = block[:8] + field[piece - 1, stripe : stripe + 8, :]
            block = head if stripe == 8 else jnp.concatenate([head, block[8:]], 0)
        parts.append(block)
    spill = field[pieces - 1, stripe : stripe + 8, :]
    parts.append(spill)
    source = jnp.concatenate(parts, 0)
    across = dot_three(halves(source), (basis_high[...], basis_low[...]))
    driven = dot_three((drive_high[...], drive_low[...]), halves(across))
    response = driven * scale[...]
    spectrum[...] = response
    edges = [dot_three((edge_high[...], edge_low[...]), halves(response))]
    for table, start, count in ((above_table, 0, 8), (below_table, SUBN - 8, 9)):
        total = across[start : start + 1] * table[0]
        for step in range(1, count):
            total = total + across[start + step : start + step + 1] * table[step]
        edges.append(total)
    rims = dot_three(halves(jnp.concatenate(edges, 0)), (back_high[side], back_low[side]))
    near[:8, :] = jnp.where(mine > 0, rims[24:32], 0.0)
    near[8:, :] = jnp.where(mine < rows - 1, rims[32:40], 0.0)
    base = 8 * tiles
    tail = sent.shape[1] - base - 8
    total = jnp.sum(source[:SUBN], 0, keepdims=True)
    place = iota((tail, LANES), 0)
    sums = jnp.zeros((tail, LANES), F32)
    for block in range(blocks):
        cut = slice(block * SUBN, (block + 1) * SUBN)
        sums = jnp.where(place == block, total[:, cut], sums)
        sums = jnp.where(place == blocks + block, spill[:1, cut], sums)
    for tile in range(tiles):
        cut = slice(tile * LANES, (tile + 1) * LANES)
        sums = jnp.where(place == 2 * blocks + tile, across[SUBN : SUBN + 1, cut], sums)
    for target in range(rows):
        sent[target, : base + 8, :] = jnp.zeros((base + 8, LANES), F32)
        sent[target, base + 8 :, :] = sums

    def put(target, rim, lines):
        sent[target, base : base + 8, :] = rim
        if lines is not None:
            for tile in range(tiles):
                sent[target, 8 * tile : 8 * tile + 8, :] = lines[:, tile * LANES : (tile + 1) * LANES]

    @pl.when(mine >= 1)
    def _():
        put(mine - 1, rims[:8], across[:8])

    @pl.when(mine >= 2)
    def _():
        put(mine - 2, rims[16:24], None)

    @pl.when(mine + 1 < rows)
    def _():
        put(mine + 1, rims[8:16], across[SUBN - 8 : SUBN])

    @pl.when(mine + 2 < rows)
    def _():
        put(mine + 2, rims[40:], None)


def phase_kernel(
    sizes, received, field, spectrum, near, back_high, back_low, halo_high, halo_low, out_high, out_low, scale,
    coarse, phase, mean_flux, spot_size,
):
    stripe, pieces, blocks, rows = sizes
    for piece in range(pieces):
        where = slice(piece * stripe, (piece + 1) * stripe)
        mean_flux[0, where, :] = field[piece, stripe + 8 :, :SUBN]
        spot_size[0, where, :] = field[piece, stripe + 8 :, SUBN : 2 * SUBN]
    tiles = padded(blocks) // LANES
    mine = lax.axis_index("row")
    side = lax.axis_index("col")
    base = 8 * tiles
    tail = received.shape[1] - base - 8
    above = jnp.maximum(mine - 1, 0)
    below = jnp.minimum(mine + 1, rows - 1)
    has_above = mine > 0
    has_below = mine < rows - 1
    first = iota((8, LANES), 0) == 0
    top, bottom, spilt = [], [], []
    for tile in range(tiles):
        top.append(jnp.where(has_above, received[above, 8 * tile : 8 * tile + 8, :], 0.0))
        bottom.append(jnp.where(has_below, received[below, 8 * tile : 8 * tile + 8, :], 0.0))
        line = received[above, pl.ds(base + 8 + 2 * blocks + tile, 1), :]
        spilt.append(jnp.where(jnp.logical_and(first, has_above), line, 0.0))
    across = jnp.concatenate(
        [jnp.concatenate(top, 1), jnp.concatenate(spilt, 1), jnp.concatenate(bottom, 1)], 0
    )
    driven = dot_three((halo_high[...], halo_low[...]), halves(across))
    response = spectrum[...] + driven * scale[...]
    reach = dot_three(halves(response), (back_high[side], back_low[side]))
    solved = dot_three((out_high[...], out_low[...]), halves(reach))
    weighted = jnp.zeros((tail, coarse.shape[2]), F32)
    for origin in range(rows):
        count = jnp.sum(received[origin, base + 8 :, :], 1, keepdims=True)
        weighted = weighted + count * coarse[origin]
    own = iota(weighted.shape, 1) == mine * blocks + side
    level = jnp.sum(jnp.where(own, weighted, 0.0), keepdims=True)
    solved = solved + level
    head = near[:8, :] + jnp.where(has_above, received[above, base : base + 8, :], 0.0)
    head = head + jnp.where(mine > 1, received[jnp.maximum(mine - 2, 0), base : base + 8, :], 0.0)
    foot = near[8:, :] + jnp.where(has_below, received[below, base : base + 8, :], 0.0)
    foot = foot + jnp.where(
        mine < rows - 2, received[jnp.minimum(mine + 2, rows - 1), base : base + 8, :], 0.0
    )
    phase[0, :8, :] = solved[:8] + head
    phase[0, 8 : SUBN - 8, :] = solved[8 : SUBN - 8]
    phase[0, SUBN - 8 :, :] = solved[SUBN - 8 :] + foot


def coarse_table(blocks_down, blocks_across, tail):
    inverse = coarse_inverse(blocks_down, blocks_across)
    number = blocks_down * blocks_across
    lanes = -(-number // LANES) * LANES
    table = np.zeros((blocks_down, tail, lanes), np.float32)
    for row in range(blocks_down):
        for block in range(blocks_across):
            table[row, block, :number] = inverse[row * blocks_across + block]
            if row + 1 < blocks_down:
                table[row, blocks_across + block, :number] = inverse[(row + 1) * blocks_across + block]
    return table


def in_vmem(count):
    return [pl.BlockSpec(memory_space=pltpu.VMEM)] * count


PARAMS = pltpu.CompilerParams(vmem_limit_bytes=48 * 1024 * 1024)


def body(pixels):
    frames, pixel_rows, pixel_cols = pixels.shape
    stripe = pixel_rows // PIX
    width = pixel_cols // PIX
    rows = lax.axis_size("row")
    blocks = lax.axis_size("col")
    cores = lax.axis_size("sub")
    pieces = blocks * cores
    assert frames == cores and width == blocks * SUBN and stripe * pieces == SUBN

    field = pl.pallas_call(
        functools.partial(moments_kernel, (frames, stripe, blocks, cores, rows * pieces)),
        out_shape=jax.ShapeDtypeStruct((pieces, 2 * stripe + 8, width), F32),
        in_specs=[pl.BlockSpec(memory_space=pltpu.HBM)],
        out_specs=pl.BlockSpec(memory_space=pltpu.VMEM),
        scratch_shapes=[
            pltpu.VMEM((frames, pixel_rows, pixel_cols), BF16),
            pltpu.SemaphoreType.DMA((frames, blocks)),
        ],
        compiler_params=PARAMS,
        name="moments",
    )(pltpu.with_memory_space_constraint(pixels, pltpu.HBM))

    field = lax.all_to_all(field, ("col", "sub"), split_axis=0, concat_axis=0, tiled=True)

    vectors, scale = sine_basis()
    basis = column_basis(blocks)
    full = padded(blocks)
    tiles = full // LANES
    basis_pair = constant_pair(basis)
    back_pair = constant_pair(basis.T.reshape(full, blocks, SUBN).transpose(1, 0, 2))
    scale_wide = jnp.asarray(widened(scale, blocks))
    drive_pair = constant_pair(vectors[:, MARGIN:])
    edge_pair = constant_pair(np.concatenate([vectors[:8], vectors[WIN - 8 :]], 0))
    side_tables = [jnp.asarray(widened(table, blocks)) for table in edge_tables()]
    tail = -(-(2 * blocks + tiles) // 8) * 8
    height = 8 * tiles + 8 + tail

    sent, spectrum, near = pl.pallas_call(
        functools.partial(rims_kernel, (stripe, pieces, blocks, rows)),
        out_shape=(
            jax.ShapeDtypeStruct((rows, height, LANES), F32),
            jax.ShapeDtypeStruct((WIN, full), F32),
            jax.ShapeDtypeStruct((16, SUBN), F32),
        ),
        in_specs=in_vmem(12),
        out_specs=tuple(in_vmem(3)),
        compiler_params=PARAMS,
        name="rims",
    )(field, *basis_pair, *back_pair, *drive_pair, *edge_pair, scale_wide, *side_tables)

    received = lax.all_to_all(sent, "row", split_axis=0, concat_axis=0, tiled=True)

    halo = np.zeros((WIN, 24))
    halo[:, :9] = vectors[:, :9]
    halo[:, 16:] = vectors[:, WIN - 8 :]
    halo_pair = constant_pair(halo)
    out_pair = constant_pair(vectors[MARGIN : MARGIN + SUBN])
    return pl.pallas_call(
        functools.partial(phase_kernel, (stripe, pieces, blocks, rows)),
        out_shape=(jax.ShapeDtypeStruct((1, SUBN, SUBN), F32),) * 3,
        in_specs=in_vmem(12),
        out_specs=tuple(in_vmem(3)),
        compiler_params=PARAMS,
        name="phase",
    )(
        received, field, spectrum, near, *back_pair, *halo_pair, *out_pair, scale_wide,
        jnp.asarray(coarse_table(rows, blocks, tail)),
    )

def solution(mesh):
    placed = P(("groups", "sub"), "row", "col")
    return jax.shard_map(
        body,
        mesh=mesh,
        in_specs=(P("groups", ("row", "col", "sub"), None),),
        out_specs=(placed, placed, placed),
        check_vma=False,
    )
```

```python
import functools
import math

import jax
import jax.numpy as jnp
import numpy as np
from jax import lax
from jax.experimental import pallas as pl
from jax.experimental.pallas import tpu as pltpu
from jax.sharding import PartitionSpec as P

PIX = 8
SUBN = 128
MARGIN = 8
WIN = SUBN + 2 * MARGIN
CHUNK = 256
LANES = 128
GROUP = CHUNK // PIX
DAMPING = 2e-05
F32 = jnp.float32
BF16 = jnp.bfloat16


def constant_pair(values):
    high = np.asarray(values).astype(jnp.bfloat16)
    low = (values - high.astype(np.float64)).astype(jnp.bfloat16)
    return jnp.asarray(high), jnp.asarray(low)


def sine_basis():
    order = np.arange(1, WIN + 1, dtype=np.float64)
    vectors = np.sqrt(2.0 / (WIN + 1)) * np.sin(math.pi * order[:, None] * order[None, :] / (WIN + 1))
    spectrum = 2.0 - 2.0 * np.cos(math.pi * order / (WIN + 1))
    return vectors, 1.0 / (spectrum[:, None] + spectrum[None, :] + DAMPING)


def padded(blocks):
    return -(-blocks * WIN // LANES) * LANES


def column_basis(blocks):
    vectors, _ = sine_basis()
    table = np.zeros((blocks * SUBN, padded(blocks)))
    for block in range(blocks):
        low = max(block * SUBN - MARGIN, 0)
        high = min((block + 1) * SUBN + MARGIN, blocks * SUBN)
        start = low - (block * SUBN - MARGIN)
        table[low:high, block * WIN : (block + 1) * WIN] = vectors[start : start + high - low]
    return table


def widened(table, blocks):
    wide = np.zeros(table.shape[:-1] + (padded(blocks),), np.float32)
    wide[..., : blocks * WIN] = np.tile(table, (1,) * (table.ndim - 1) + (blocks,))
    return wide


def edge_tables():
    vectors, scale = sine_basis()
    ends = np.concatenate([vectors[:8], vectors[WIN - 8 :]], 0)
    def driven_by(rows):
        return np.einsum("oa,ai,ab->iob", ends, vectors[:, rows], scale)
    return driven_by(slice(WIN - 8, WIN)), driven_by(slice(0, 9))


def coarse_inverse(blocks_down, blocks_across):
    number = blocks_down * blocks_across
    row, col = np.divmod(np.arange(number), blocks_across)
    apart = np.abs(row[:, None] - row[None, :]) + np.abs(col[:, None] - col[None, :])
    touching = (apart == 1).astype(np.float64)
    laplace = np.diag(touching.sum(1)) - touching
    return np.linalg.inv(SUBN * laplace + DAMPING * SUBN * SUBN * np.eye(number))


def halves(values):
    high = values.astype(BF16)
    return high, (values - high.astype(F32)).astype(BF16)


def dot(left, right):
    return jnp.dot(left, right, preferred_element_type=F32)


def dot_three(left, right):
    return dot(left[0], right[0]) + (dot(left[0], right[1]) + dot(left[1], right[0]))


def iota(shape, axis):
    return lax.broadcasted_iota(jnp.int32, shape, axis)


def power(offset, kind):
    return jnp.where(kind == 0, 1.0, jnp.where(kind == 1, offset, offset * offset))


def offset_of(place):
    return (place % PIX).astype(F32) - (PIX - 1) / 2.0


def row_moments(stripe):
    shape = (3 * stripe, stripe * PIX)
    row, place = iota(shape, 0), iota(shape, 1)
    hit = place // PIX == row % stripe
    return jnp.where(hit, power(offset_of(place), row // stripe), 0.0).astype(BF16)


def column_moments(chunk):
    places = LANES // GROUP
    shape = (CHUNK, LANES)
    place, lane = iota(shape, 0), iota(shape, 1)
    kind = (lane // GROUP + (places - chunk)) % places
    hit = jnp.logical_and(place // PIX == lane % GROUP, kind < 3)
    return jnp.where(hit, power(offset_of(place), kind), 0.0).astype(BF16)


def swapped(count):
    return count <= 4 and count & (count - 1) == 0


def exchange(pieces, axes, count):
    if not swapped(count):
        return [lax.all_to_all(pieces[0], axes, split_axis=0, concat_axis=0, tiled=True)]
    return [pieces[0]] + [
        lax.ppermute(pieces[k], axes, [(i, i ^ k) for i in range(count)]) for k in range(1, count)
    ]


def piece_shapes(count, shape):
    if swapped(count):
        return [jax.ShapeDtypeStruct(shape, F32)] * count
    return [jax.ShapeDtypeStruct((count,) + shape, F32)]


def pick(index, values):
    total = values[-1]
    for step in range(len(values) - 1):
        total = jnp.where(index == step, values[step], total)
    return total


def moments_kernel(sizes, pixels, *refs):
    frames, stripe, blocks, cores, stripes = sizes
    pieces = blocks * cores
    slots = pieces if swapped(pieces) else 1
    fields, extras = refs[:slots], refs[slots : 2 * slots]
    held, arrived = refs[2 * slots :]
    width = blocks * SUBN
    places = LANES // GROUP
    span = LANES * PIX

    def copy(frame, part):
        where = (frame, slice(None), pl.ds(part * span, span))
        return pltpu.make_async_copy(pixels.at[where], held.at[where], arrived.at[frame, part])

    for frame in range(frames):
        for part in range(blocks):
            copy(frame, part).start()
    row_table = row_moments(stripe)
    col_tables = [column_moments(chunk) for chunk in range(places)]
    slot = lax.axis_index("col") * cores + lax.axis_index("sub")
    position = lax.axis_index("row") * pieces + slot
    group = iota((stripe, LANES), 1) // GROUP

    def gather(pieces, kind):
        total = pieces[-1]
        for chunk in range(places - 1):
            total = jnp.where(group == (kind + chunk) % places, pieces[chunk], total)
        return pltpu.roll(total, LANES - GROUP * kind, 1) if kind else total

    row = iota((stripe, width), 0)
    column = iota((stripe, width), 1)

    def columns_of(lines):
        high, low = halves(lines)
        pieces = []
        for chunk in range(places):
            cut = slice(chunk * CHUNK, (chunk + 1) * CHUNK)
            weights = col_tables[chunk]
            pieces.append(dot(high[:, cut], weights) + dot(low[:, cut], weights))
        plain = [piece[:stripe] for piece in pieces]
        tilted = [piece[stripe : 2 * stripe] for piece in pieces]
        bent = [piece[2 * stripe :] for piece in pieces]
        return gather(plain, 0), gather(plain, 1), gather(tilted, 0), gather(plain, 2) + gather(bent, 0)

    def finish(frame, parts):
        intensity, moment_x, moment_y, moment_two = [jnp.concatenate(kind, 1) for kind in zip(*parts)]
        inverse = 1.0 / intensity
        slope_x = moment_x * inverse
        slope_y = moment_y * inverse
        spot_size = moment_two * inverse - slope_x * slope_x - slope_y * slope_y
        mean_flux = intensity * (1.0 / (PIX * PIX))
        flow_x = jnp.where(column < width - 1, slope_x, 0.0)
        flow_y = jnp.where(position * stripe + row < stripes * stripe - 1, slope_y, 0.0)
        left = jnp.where(column > 0, pltpu.roll(flow_x, 1, 1), 0.0)
        above = pltpu.roll(flow_y, 1, 0)
        source = left - flow_x + jnp.where(row > 0, above, 0.0) - flow_y
        spill = jnp.where(row[:8] == 0, above[:8], 0.0)
        fluxes = [mean_flux[:, block * SUBN : (block + 1) * SUBN] for block in range(blocks)]
        spots = [spot_size[:, block * SUBN : (block + 1) * SUBN] for block in range(blocks)]
        return source, spill, fluxes, spots

    def lines_of(frame):
        for part in range(blocks):
            copy(frame, part).wait()
        return [dot(row_table, held[frame, :, pl.ds(part * span, span)]) for part in range(blocks)]

    lines = [lines_of(frame) for frame in range(frames)]
    found = [finish(frame, [columns_of(part) for part in lines[frame]]) for frame in range(frames)]
    for piece in range(pieces):
        if slots > 1:
            target = slot ^ piece
            frame, block = target % cores, target // cores
            source, spill = [pick(frame, [one[kind] for one in found]) for kind in range(2)]
            flux, spot = [pick(frame, [pick(block, one[kind]) for one in found]) for kind in range(2, 4)]
            field, extra = fields[piece], extras[piece]
        else:
            frame, block = piece % cores, piece // cores
            source, spill, flux, spot = found[frame]
            flux, spot = flux[block], spot[block]
            field, extra = fields[0].at[piece], extras[0].at[piece]
        field[:stripe, :] = source
        field[stripe:, :] = spill
        extra[:stripe, :] = flux
        extra[stripe:, :] = spot


def pieces_of(refs, slots, count, mine):
    if slots > 1:
        return [(mine ^ step, refs[step]) for step in range(count)]
    return [(step, refs[0].at[step]) for step in range(count)]


def rims_kernel(sizes, *refs):
    stripe, pieces, blocks, cores, rows = sizes
    slots = pieces if swapped(pieces) else 1
    outs = rows if swapped(rows) else 1
    fields, refs = refs[:slots], refs[slots:]
    basis_high, basis_low, back_high, back_low, drive_high, drive_low, edge_high, edge_low = refs[:8]
    scale, above_table, below_table = refs[8:11]
    sent, near, lined = refs[11 : 11 + outs], refs[11 + outs + 1], refs[11 + outs + 2]
    spectrum = refs[11 + outs]
    tiles = padded(blocks) // LANES
    mine = lax.axis_index("row")
    side = lax.axis_index("col")
    arranged = pieces_of(fields, slots, pieces, side * cores + lax.axis_index("sub"))
    lined[SUBN:, :] = jnp.zeros((8, lined.shape[1]), F32)
    for place, field in arranged:
        lined[pl.ds(pl.multiple_of(place * stripe, 8), stripe), :] = field[:stripe, :]
    for place, field in arranged:
        head = pl.ds(pl.multiple_of((place + 1) * stripe, 8), 8)
        lined[head, :] = lined[head, :] + field[stripe:, :]
    source = lined[...]
    across = dot_three(halves(source), (basis_high[...], basis_low[...]))
    driven = dot_three((drive_high[...], drive_low[...]), halves(across))
    response = driven * scale[...]
    spectrum[...] = response
    edges = [dot_three((edge_high[...], edge_low[...]), halves(response))]
    for table, start, count in ((above_table, 0, 8), (below_table, SUBN - 8, 9)):
        total = across[start : start + 1] * table[0]
        for step in range(1, count):
            total = total + across[start + step : start + step + 1] * table[step]
        edges.append(total)
    rims = dot_three(halves(jnp.concatenate(edges, 0)), (back_high[side], back_low[side]))
    near[:8, :] = jnp.where(mine > 0, rims[24:32], 0.0)
    near[8:, :] = jnp.where(mine < rows - 1, rims[32:40], 0.0)
    base = 8 * tiles
    tail = sent[0].shape[-2] - base - 8
    total = jnp.sum(source[:SUBN], 0, keepdims=True)
    place = iota((tail, LANES), 0)
    sums = jnp.zeros((tail, LANES), F32)
    for block in range(blocks):
        cut = slice(block * SUBN, (block + 1) * SUBN)
        sums = jnp.where(place == block, total[:, cut], sums)
        sums = jnp.where(place == blocks + block, source[SUBN : SUBN + 1, cut], sums)
    for tile in range(tiles):
        cut = slice(tile * LANES, (tile + 1) * LANES)
        sums = jnp.where(place == 2 * blocks + tile, across[SUBN : SUBN + 1, cut], sums)
    for target, piece in pieces_of(sent, outs, rows, mine):
        ahead = target - mine
        rim = jnp.where(ahead == -1, rims[:8], 0.0)
        rim = jnp.where(ahead == 1, rims[8:16], rim)
        rim = jnp.where(ahead == -2, rims[16:24], rim)
        rim = jnp.where(ahead == 2, rims[40:], rim)
        for tile in range(tiles):
            cut = slice(tile * LANES, (tile + 1) * LANES)
            line = jnp.where(ahead == -1, across[:8, cut], across[SUBN - 8 : SUBN, cut])
            piece[8 * tile : 8 * tile + 8, :] = line
        piece[base : base + 8, :] = rim
        piece[base + 8 :, :] = sums


def phase_kernel(sizes, *refs):
    stripe, pieces, blocks, cores, rows = sizes
    slots = pieces if swapped(pieces) else 1
    ins = rows if swapped(rows) else 1
    received, extras, refs = refs[:ins], refs[ins : ins + slots], refs[ins + slots :]
    spectrum, near, back_high, back_low, halo_high, halo_low, out_high, out_low, scale, coarse = refs[:10]
    phase, mean_flux, spot_size = refs[10:]
    tiles = padded(blocks) // LANES
    mine = lax.axis_index("row")
    side = lax.axis_index("col")
    for place, extra in pieces_of(extras, slots, pieces, side * cores + lax.axis_index("sub")):
        where = pl.ds(pl.multiple_of(place * stripe, 8), stripe)
        mean_flux[0, where, :] = extra[:stripe, :]
        spot_size[0, where, :] = extra[stripe:, :]
    base = 8 * tiles
    tail = received[0].shape[-2] - base - 8
    arranged = pieces_of(received, ins, rows, mine)

    def of_row(row, where):
        if ins == 1:
            inside = jnp.logical_and(row >= 0, row < rows)
            return jnp.where(inside, received[0][jnp.clip(row, 0, rows - 1), where, :], 0.0)
        total = jnp.zeros((where.stop - where.start, LANES), F32)
        for origin, piece in arranged[1:]:
            total = jnp.where(origin == row, piece[where, :], total)
        return total

    above = of_row(mine - 1, slice(0, received[0].shape[-2]))
    below = of_row(mine + 1, slice(0, base + 8))
    first = iota((8, LANES), 0) == 0
    top, bottom, spilt = [], [], []
    for tile in range(tiles):
        top.append(above[8 * tile : 8 * tile + 8])
        bottom.append(below[8 * tile : 8 * tile + 8])
        start = base + 8 + 2 * blocks + tile
        spilt.append(jnp.where(first, above[start : start + 1], 0.0))
    across = jnp.concatenate(
        [jnp.concatenate(top, 1), jnp.concatenate(spilt, 1), jnp.concatenate(bottom, 1)], 0
    )
    driven = dot_three((halo_high[...], halo_low[...]), halves(across))
    response = spectrum[...] + driven * scale[...]
    reach = dot_three(halves(response), (back_high[side], back_low[side]))
    solved = dot_three((out_high[...], out_low[...]), halves(reach))
    weighted = jnp.zeros((tail, coarse.shape[2]), F32)
    for origin, piece in arranged:
        count = jnp.sum(piece[base + 8 :, :], 1, keepdims=True)
        weighted = weighted + count * coarse[origin]
    own = iota(weighted.shape, 1) == mine * blocks + side
    level = jnp.sum(jnp.where(own, weighted, 0.0), keepdims=True)
    solved = solved + level
    rim = slice(base, base + 8)
    head = near[:8, :] + above[rim] + of_row(mine - 2, rim)
    foot = near[8:, :] + below[rim] + of_row(mine + 2, rim)
    phase[0, :8, :] = solved[:8] + head
    phase[0, 8 : SUBN - 8, :] = solved[8 : SUBN - 8]
    phase[0, SUBN - 8 :, :] = solved[SUBN - 8 :] + foot


def coarse_table(blocks_down, blocks_across, tail):
    inverse = coarse_inverse(blocks_down, blocks_across)
    number = blocks_down * blocks_across
    lanes = -(-number // LANES) * LANES
    table = np.zeros((blocks_down, tail, lanes), np.float32)
    for row in range(blocks_down):
        for block in range(blocks_across):
            table[row, block, :number] = inverse[row * blocks_across + block]
            if row + 1 < blocks_down:
                table[row, blocks_across + block, :number] = inverse[(row + 1) * blocks_across + block]
    return table


def in_vmem(count):
    return [pl.BlockSpec(memory_space=pltpu.VMEM)] * count


PARAMS = pltpu.CompilerParams(vmem_limit_bytes=48 * 1024 * 1024)


def body(pixels):
    frames, pixel_rows, pixel_cols = pixels.shape
    stripe = pixel_rows // PIX
    width = pixel_cols // PIX
    rows = lax.axis_size("row")
    blocks = lax.axis_size("col")
    cores = lax.axis_size("sub")
    pieces = blocks * cores
    assert frames == cores and width == blocks * SUBN and stripe * pieces == SUBN

    field_shapes = piece_shapes(pieces, (stripe + 8, width))
    extra_shapes = piece_shapes(pieces, (2 * stripe, SUBN))
    made = pl.pallas_call(
        functools.partial(moments_kernel, (frames, stripe, blocks, cores, rows * pieces)),
        out_shape=field_shapes + extra_shapes,
        in_specs=[pl.BlockSpec(memory_space=pltpu.HBM)],
        out_specs=in_vmem(len(field_shapes + extra_shapes)),
        scratch_shapes=[
            pltpu.VMEM((frames, pixel_rows, pixel_cols), BF16),
            pltpu.SemaphoreType.DMA((frames, blocks)),
        ],
        compiler_params=PARAMS,
        name="moments",
    )(pltpu.with_memory_space_constraint(pixels, pltpu.HBM))
    fields = exchange(made[: len(field_shapes)], ("col", "sub"), pieces)
    extras = exchange(made[len(field_shapes) :], ("col", "sub"), pieces)

    vectors, scale = sine_basis()
    basis = column_basis(blocks)
    full = padded(blocks)
    tiles = full // LANES
    basis_pair = constant_pair(basis)
    back_pair = constant_pair(basis.T.reshape(full, blocks, SUBN).transpose(1, 0, 2))
    scale_wide = jnp.asarray(widened(scale, blocks))
    drive_pair = constant_pair(vectors[:, MARGIN:])
    edge_pair = constant_pair(np.concatenate([vectors[:8], vectors[WIN - 8 :]], 0))
    side_tables = [jnp.asarray(widened(table, blocks)) for table in edge_tables()]
    tail = -(-(2 * blocks + tiles) // 8) * 8
    height = 8 * tiles + 8 + tail

    row_shapes = piece_shapes(rows, (height, LANES))
    sizes = (stripe, pieces, blocks, cores, rows)
    *sent, spectrum, near = pl.pallas_call(
        functools.partial(rims_kernel, sizes),
        out_shape=row_shapes
        + [jax.ShapeDtypeStruct((WIN, full), F32), jax.ShapeDtypeStruct((16, SUBN), F32)],
        in_specs=in_vmem(len(fields) + 11),
        out_specs=in_vmem(len(row_shapes) + 2),
        scratch_shapes=[pltpu.VMEM((SUBN + 8, width), F32)],
        compiler_params=PARAMS,
        name="rims",
    )(*fields, *basis_pair, *back_pair, *drive_pair, *edge_pair, scale_wide, *side_tables)
    received = exchange(sent, ("row",), rows)

    halo = np.zeros((WIN, 24))
    halo[:, :9] = vectors[:, :9]
    halo[:, 16:] = vectors[:, WIN - 8 :]
    halo_pair = constant_pair(halo)
    out_pair = constant_pair(vectors[MARGIN : MARGIN + SUBN])
    return pl.pallas_call(
        functools.partial(phase_kernel, sizes),
        out_shape=[jax.ShapeDtypeStruct((1, SUBN, SUBN), F32)] * 3,
        in_specs=in_vmem(len(received) + len(extras) + 10),
        out_specs=in_vmem(3),
        compiler_params=PARAMS,
        name="phase",
    )(
        *received, *extras, spectrum, near, *back_pair, *halo_pair, *out_pair, scale_wide,
        jnp.asarray(coarse_table(rows, blocks, tail)),
    )


def solution(mesh):
    placed = P(("groups", "sub"), "row", "col")
    return jax.shard_map(
        body,
        mesh=mesh,
        in_specs=(P("groups", ("row", "col", "sub"), None),),
        out_specs=(placed, placed, placed),
        check_vma=False,
    )
```

```python
import functools
import math

import jax
import jax.numpy as jnp
import numpy as np
from jax import lax
from jax.experimental import pallas as pl
from jax.experimental.pallas import tpu as pltpu
from jax.sharding import PartitionSpec as P

PIX = 8
SUBN = 128
MARGIN = 8
WIN = SUBN + 2 * MARGIN
CHUNK = 256
LANES = 128
GROUP = CHUNK // PIX
DAMPING = 2e-05
F32 = jnp.float32
BF16 = jnp.bfloat16


def constant_pair(values):
    high = np.asarray(values).astype(jnp.bfloat16)
    low = (values - high.astype(np.float64)).astype(jnp.bfloat16)
    return jnp.asarray(high), jnp.asarray(low)


def sine_basis():
    order = np.arange(1, WIN + 1, dtype=np.float64)
    vectors = np.sqrt(2.0 / (WIN + 1)) * np.sin(math.pi * order[:, None] * order[None, :] / (WIN + 1))
    spectrum = 2.0 - 2.0 * np.cos(math.pi * order / (WIN + 1))
    return vectors, 1.0 / (spectrum[:, None] + spectrum[None, :] + DAMPING)


def padded(blocks):
    return -(-blocks * WIN // LANES) * LANES


def column_basis(blocks):
    vectors, _ = sine_basis()
    table = np.zeros((blocks * SUBN, padded(blocks)))
    for block in range(blocks):
        low = max(block * SUBN - MARGIN, 0)
        high = min((block + 1) * SUBN + MARGIN, blocks * SUBN)
        start = low - (block * SUBN - MARGIN)
        table[low:high, block * WIN : (block + 1) * WIN] = vectors[start : start + high - low]
    return table


def widened(table, blocks):
    wide = np.zeros(table.shape[:-1] + (padded(blocks),), np.float32)
    wide[..., : blocks * WIN] = np.tile(table, (1,) * (table.ndim - 1) + (blocks,))
    return wide


def edge_tables():
    vectors, scale = sine_basis()
    ends = np.concatenate([vectors[:8], vectors[WIN - 8 :]], 0)
    def driven_by(rows):
        return np.einsum("oa,ai,ab->iob", ends, vectors[:, rows], scale)
    return driven_by(slice(WIN - 8, WIN)), driven_by(slice(0, 9))


def coarse_inverse(blocks_down, blocks_across):
    number = blocks_down * blocks_across
    row, col = np.divmod(np.arange(number), blocks_across)
    apart = np.abs(row[:, None] - row[None, :]) + np.abs(col[:, None] - col[None, :])
    touching = (apart == 1).astype(np.float64)
    laplace = np.diag(touching.sum(1)) - touching
    return np.linalg.inv(SUBN * laplace + DAMPING * SUBN * SUBN * np.eye(number))


def halves(values):
    high = values.astype(BF16)
    return high, (values - high.astype(F32)).astype(BF16)


def dot(left, right):
    return jnp.dot(left, right, preferred_element_type=F32)


def dot_three(left, right):
    return dot(left[0], right[0]) + (dot(left[0], right[1]) + dot(left[1], right[0]))


def iota(shape, axis):
    return lax.broadcasted_iota(jnp.int32, shape, axis)


def power(offset, kind):
    return jnp.where(kind == 0, 1.0, jnp.where(kind == 1, offset, offset * offset))


def offset_of(place):
    return (place % PIX).astype(F32) - (PIX - 1) / 2.0


def row_moments(stripe):
    shape = (3 * stripe, stripe * PIX)
    row, place = iota(shape, 0), iota(shape, 1)
    hit = place // PIX == row % stripe
    return jnp.where(hit, power(offset_of(place), row // stripe), 0.0).astype(BF16)


def column_moments(chunk):
    places = LANES // GROUP
    shape = (CHUNK, LANES)
    place, lane = iota(shape, 0), iota(shape, 1)
    kind = (lane // GROUP + (places - chunk)) % places
    hit = jnp.logical_and(place // PIX == lane % GROUP, kind < 3)
    return jnp.where(hit, power(offset_of(place), kind), 0.0).astype(BF16)


ORDER = {1: (), 2: (1,), 4: (2, 3, 1)}


def swapped(count):
    return count in ORDER


def exchange(pieces, axes, count):
    if not swapped(count):
        return [lax.all_to_all(pieces[0], axes, split_axis=0, concat_axis=0, tiled=True)]
    return [pieces[0]] + [
        lax.ppermute(pieces[k], axes, [(i, i ^ k) for i in range(count)]) for k in ORDER[count]
    ]


def piece_shapes(count, shape):
    if swapped(count):
        return [jax.ShapeDtypeStruct(shape, F32)] * count
    return [jax.ShapeDtypeStruct((count,) + shape, F32)]


def pick(index, values):
    total = values[-1]
    for step in range(len(values) - 1):
        total = jnp.where(index == step, values[step], total)
    return total


def moments_kernel(sizes, pixels, *refs):
    frames, stripe, blocks, cores, stripes = sizes
    pieces = blocks * cores
    slots = pieces if swapped(pieces) else 1
    fields, extras = refs[:slots], refs[slots : 2 * slots]
    held, arrived = refs[2 * slots :]
    width = blocks * SUBN
    places = LANES // GROUP
    span = LANES * PIX

    def copy(frame, part):
        where = (frame, slice(None), pl.ds(part * span, span))
        return pltpu.make_async_copy(pixels.at[where], held.at[where], arrived.at[frame, part])

    for frame in range(frames):
        for part in range(blocks):
            copy(frame, part).start()
    row_table = row_moments(stripe)
    col_tables = [column_moments(chunk) for chunk in range(places)]
    slot = lax.axis_index("col") * cores + lax.axis_index("sub")
    position = lax.axis_index("row") * pieces + slot
    group = iota((stripe, LANES), 1) // GROUP

    def gather(pieces, kind):
        total = pieces[-1]
        for chunk in range(places - 1):
            total = jnp.where(group == (kind + chunk) % places, pieces[chunk], total)
        return pltpu.roll(total, LANES - GROUP * kind, 1) if kind else total

    row = iota((stripe, width), 0)
    column = iota((stripe, width), 1)

    def columns_of(lines):
        high, low = halves(lines)
        pieces = []
        for chunk in range(places):
            cut = slice(chunk * CHUNK, (chunk + 1) * CHUNK)
            weights = col_tables[chunk]
            pieces.append(dot(high[:, cut], weights) + dot(low[:, cut], weights))
        plain = [piece[:stripe] for piece in pieces]
        tilted = [piece[stripe : 2 * stripe] for piece in pieces]
        bent = [piece[2 * stripe :] for piece in pieces]
        return gather(plain, 0), gather(plain, 1), gather(tilted, 0), gather(plain, 2) + gather(bent, 0)

    def finish(frame, parts):
        intensity, moment_x, moment_y, moment_two = [jnp.concatenate(kind, 1) for kind in zip(*parts)]
        inverse = 1.0 / intensity
        slope_x = moment_x * inverse
        slope_y = moment_y * inverse
        spot_size = moment_two * inverse - slope_x * slope_x - slope_y * slope_y
        mean_flux = intensity * (1.0 / (PIX * PIX))
        flow_x = jnp.where(column < width - 1, slope_x, 0.0)
        flow_y = jnp.where(position * stripe + row < stripes * stripe - 1, slope_y, 0.0)
        left = jnp.where(column > 0, pltpu.roll(flow_x, 1, 1), 0.0)
        above = pltpu.roll(flow_y, 1, 0)
        source = left - flow_x + jnp.where(row > 0, above, 0.0) - flow_y
        spill = jnp.where(row[:8] == 0, above[:8], 0.0)
        fluxes = [mean_flux[:, block * SUBN : (block + 1) * SUBN] for block in range(blocks)]
        spots = [spot_size[:, block * SUBN : (block + 1) * SUBN] for block in range(blocks)]
        return source, spill, fluxes, spots

    def lines_of(frame):
        for part in range(blocks):
            copy(frame, part).wait()
        return [dot(row_table, held[frame, :, pl.ds(part * span, span)]) for part in range(blocks)]

    lines = [lines_of(frame) for frame in range(frames)]
    found = [finish(frame, [columns_of(part) for part in lines[frame]]) for frame in range(frames)]
    for piece in range(pieces):
        if slots > 1:
            target = slot ^ piece
            frame, block = target % cores, target // cores
            source, spill = [pick(frame, [one[kind] for one in found]) for kind in range(2)]
            flux, spot = [pick(frame, [pick(block, one[kind]) for one in found]) for kind in range(2, 4)]
            field, extra = fields[piece], extras[piece]
        else:
            frame, block = piece % cores, piece // cores
            source, spill, flux, spot = found[frame]
            flux, spot = flux[block], spot[block]
            field, extra = fields[0].at[piece], extras[0].at[piece]
        field[:stripe, :] = source
        field[stripe:, :] = spill
        extra[:stripe, :] = flux
        extra[stripe:, :] = spot


def pieces_of(refs, slots, count, mine, order):
    if slots > 1:
        return [(mine ^ step, ref) for step, ref in zip((0,) + tuple(order), refs)]
    return [(step, refs[0].at[step]) for step in range(count)]


def rims_kernel(sizes, *refs):
    stripe, pieces, blocks, cores, rows = sizes
    slots = pieces if swapped(pieces) else 1
    outs = rows if swapped(rows) else 1
    fields, refs = refs[:slots], refs[slots:]
    basis_high, basis_low, back_high, back_low, drive_high, drive_low, edge_high, edge_low = refs[:8]
    scale, above_table, below_table = refs[8:11]
    sent, near, lined = refs[11 : 11 + outs], refs[11 + outs + 1], refs[11 + outs + 2]
    spectrum = refs[11 + outs]
    tiles = padded(blocks) // LANES
    mine = lax.axis_index("row")
    side = lax.axis_index("col")
    slot = side * cores + lax.axis_index("sub")
    arranged = pieces_of(fields, slots, pieces, slot, ORDER.get(pieces))
    lined[SUBN:, :] = jnp.zeros((8, lined.shape[1]), F32)
    for place, field in arranged:
        lined[pl.ds(pl.multiple_of(place * stripe, 8), stripe), :] = field[:stripe, :]
    for place, field in arranged:
        head = pl.ds(pl.multiple_of((place + 1) * stripe, 8), 8)
        lined[head, :] = lined[head, :] + field[stripe:, :]
    source = lined[...]
    across = dot_three(halves(source), (basis_high[...], basis_low[...]))
    driven = dot_three((drive_high[...], drive_low[...]), halves(across))
    response = driven * scale[...]
    spectrum[...] = response
    edges = [dot_three((edge_high[...], edge_low[...]), halves(response))]
    for table, start, count in ((above_table, 0, 8), (below_table, SUBN - 8, 9)):
        total = across[start : start + 1] * table[0]
        for step in range(1, count):
            total = total + across[start + step : start + step + 1] * table[step]
        edges.append(total)
    rims = dot_three(halves(jnp.concatenate(edges, 0)), (back_high[side], back_low[side]))
    near[:8, :] = jnp.where(mine > 0, rims[24:32], 0.0)
    near[8:, :] = jnp.where(mine < rows - 1, rims[32:40], 0.0)
    base = 8 * tiles
    tail = sent[0].shape[-2] - base - 8
    total = jnp.sum(source[:SUBN], 0, keepdims=True)
    place = iota((tail, LANES), 0)
    sums = jnp.zeros((tail, LANES), F32)
    for block in range(blocks):
        cut = slice(block * SUBN, (block + 1) * SUBN)
        sums = jnp.where(place == block, total[:, cut], sums)
        sums = jnp.where(place == blocks + block, source[SUBN : SUBN + 1, cut], sums)
    for tile in range(tiles):
        cut = slice(tile * LANES, (tile + 1) * LANES)
        sums = jnp.where(place == 2 * blocks + tile, across[SUBN : SUBN + 1, cut], sums)
    for target, piece in pieces_of(sent, outs, rows, mine, range(1, rows)):
        ahead = target - mine
        rim = jnp.where(ahead == -1, rims[:8], 0.0)
        rim = jnp.where(ahead == 1, rims[8:16], rim)
        rim = jnp.where(ahead == -2, rims[16:24], rim)
        rim = jnp.where(ahead == 2, rims[40:], rim)
        for tile in range(tiles):
            cut = slice(tile * LANES, (tile + 1) * LANES)
            line = jnp.where(ahead == -1, across[:8, cut], across[SUBN - 8 : SUBN, cut])
            piece[8 * tile : 8 * tile + 8, :] = line
        piece[base : base + 8, :] = rim
        piece[base + 8 :, :] = sums


def phase_kernel(sizes, *refs):
    stripe, pieces, blocks, cores, rows = sizes
    slots = pieces if swapped(pieces) else 1
    ins = rows if swapped(rows) else 1
    received, extras, refs = refs[:ins], refs[ins : ins + slots], refs[ins + slots :]
    spectrum, near, back_high, back_low, halo_high, halo_low, out_high, out_low, scale, coarse = refs[:10]
    phase, mean_flux, spot_size = refs[10:]
    tiles = padded(blocks) // LANES
    mine = lax.axis_index("row")
    side = lax.axis_index("col")
    slot = side * cores + lax.axis_index("sub")
    for place, extra in pieces_of(extras, slots, pieces, slot, ORDER.get(pieces)):
        where = pl.ds(pl.multiple_of(place * stripe, 8), stripe)
        mean_flux[0, where, :] = extra[:stripe, :]
        spot_size[0, where, :] = extra[stripe:, :]
    base = 8 * tiles
    tail = received[0].shape[-2] - base - 8
    arranged = pieces_of(received, ins, rows, mine, ORDER.get(rows))

    def of_row(row, where):
        if ins == 1:
            inside = jnp.logical_and(row >= 0, row < rows)
            return jnp.where(inside, received[0][jnp.clip(row, 0, rows - 1), where, :], 0.0)
        total = jnp.zeros((where.stop - where.start, LANES), F32)
        for origin, piece in arranged[1:]:
            total = jnp.where(origin == row, piece[where, :], total)
        return total

    above = of_row(mine - 1, slice(0, received[0].shape[-2]))
    below = of_row(mine + 1, slice(0, base + 8))
    first = iota((8, LANES), 0) == 0
    top, bottom, spilt = [], [], []
    for tile in range(tiles):
        top.append(above[8 * tile : 8 * tile + 8])
        bottom.append(below[8 * tile : 8 * tile + 8])
        start = base + 8 + 2 * blocks + tile
        spilt.append(jnp.where(first, above[start : start + 1], 0.0))
    across = jnp.concatenate(
        [jnp.concatenate(top, 1), jnp.concatenate(spilt, 1), jnp.concatenate(bottom, 1)], 0
    )
    driven = dot_three((halo_high[...], halo_low[...]), halves(across))
    response = spectrum[...] + driven * scale[...]
    reach = dot_three(halves(response), (back_high[side], back_low[side]))
    solved = dot_three((out_high[...], out_low[...]), halves(reach))
    weighted = jnp.zeros((tail, coarse.shape[2]), F32)
    for origin, piece in arranged:
        count = jnp.sum(piece[base + 8 :, :], 1, keepdims=True)
        weighted = weighted + count * coarse[origin]
    own = iota(weighted.shape, 1) == mine * blocks + side
    level = jnp.sum(jnp.where(own, weighted, 0.0), keepdims=True)
    solved = solved + level
    rim = slice(base, base + 8)
    head = near[:8, :] + above[rim] + of_row(mine - 2, rim)
    foot = near[8:, :] + below[rim] + of_row(mine + 2, rim)
    phase[0, :8, :] = solved[:8] + head
    phase[0, 8 : SUBN - 8, :] = solved[8 : SUBN - 8]
    phase[0, SUBN - 8 :, :] = solved[SUBN - 8 :] + foot


def coarse_table(blocks_down, blocks_across, tail):
    inverse = coarse_inverse(blocks_down, blocks_across)
    number = blocks_down * blocks_across
    lanes = -(-number // LANES) * LANES
    table = np.zeros((blocks_down, tail, lanes), np.float32)
    for row in range(blocks_down):
        for block in range(blocks_across):
            table[row, block, :number] = inverse[row * blocks_across + block]
            if row + 1 < blocks_down:
                table[row, blocks_across + block, :number] = inverse[(row + 1) * blocks_across + block]
    return table


def in_vmem(count):
    return [pl.BlockSpec(memory_space=pltpu.VMEM)] * count


PARAMS = pltpu.CompilerParams(vmem_limit_bytes=48 * 1024 * 1024)


def body(pixels):
    frames, pixel_rows, pixel_cols = pixels.shape
    stripe = pixel_rows // PIX
    width = pixel_cols // PIX
    rows = lax.axis_size("row")
    blocks = lax.axis_size("col")
    cores = lax.axis_size("sub")
    pieces = blocks * cores
    assert frames == cores and width == blocks * SUBN and stripe * pieces == SUBN

    field_shapes = piece_shapes(pieces, (stripe + 8, width))
    extra_shapes = piece_shapes(pieces, (2 * stripe, SUBN))
    made = pl.pallas_call(
        functools.partial(moments_kernel, (frames, stripe, blocks, cores, rows * pieces)),
        out_shape=field_shapes + extra_shapes,
        in_specs=[pl.BlockSpec(memory_space=pltpu.HBM)],
        out_specs=in_vmem(len(field_shapes + extra_shapes)),
        scratch_shapes=[
            pltpu.VMEM((frames, pixel_rows, pixel_cols), BF16),
            pltpu.SemaphoreType.DMA((frames, blocks)),
        ],
        compiler_params=PARAMS,
        name="moments",
    )(pltpu.with_memory_space_constraint(pixels, pltpu.HBM))
    fields = exchange(made[: len(field_shapes)], ("col", "sub"), pieces)
    extras = exchange(made[len(field_shapes) :], ("col", "sub"), pieces)

    vectors, scale = sine_basis()
    basis = column_basis(blocks)
    full = padded(blocks)
    tiles = full // LANES
    basis_pair = constant_pair(basis)
    back_pair = constant_pair(basis.T.reshape(full, blocks, SUBN).transpose(1, 0, 2))
    scale_wide = jnp.asarray(widened(scale, blocks))
    drive_pair = constant_pair(vectors[:, MARGIN:])
    edge_pair = constant_pair(np.concatenate([vectors[:8], vectors[WIN - 8 :]], 0))
    side_tables = [jnp.asarray(widened(table, blocks)) for table in edge_tables()]
    tail = -(-(2 * blocks + tiles) // 8) * 8
    height = 8 * tiles + 8 + tail

    row_shapes = piece_shapes(rows, (height, LANES))
    sizes = (stripe, pieces, blocks, cores, rows)
    *sent, spectrum, near = pl.pallas_call(
        functools.partial(rims_kernel, sizes),
        out_shape=row_shapes
        + [jax.ShapeDtypeStruct((WIN, full), F32), jax.ShapeDtypeStruct((16, SUBN), F32)],
        in_specs=in_vmem(len(fields) + 11),
        out_specs=in_vmem(len(row_shapes) + 2),
        scratch_shapes=[pltpu.VMEM((SUBN + 8, width), F32)],
        compiler_params=PARAMS,
        name="rims",
    )(*fields, *basis_pair, *back_pair, *drive_pair, *edge_pair, scale_wide, *side_tables)
    received = exchange(sent, ("row",), rows)

    halo = np.zeros((WIN, 24))
    halo[:, :9] = vectors[:, :9]
    halo[:, 16:] = vectors[:, WIN - 8 :]
    halo_pair = constant_pair(halo)
    out_pair = constant_pair(vectors[MARGIN : MARGIN + SUBN])
    return pl.pallas_call(
        functools.partial(phase_kernel, sizes),
        out_shape=[jax.ShapeDtypeStruct((1, SUBN, SUBN), F32)] * 3,
        in_specs=in_vmem(len(received) + len(extras) + 10),
        out_specs=in_vmem(3),
        compiler_params=PARAMS,
        name="phase",
    )(
        *received, *extras, spectrum, near, *back_pair, *halo_pair, *out_pair, scale_wide,
        jnp.asarray(coarse_table(rows, blocks, tail)),
    )


def solution(mesh):
    placed = P(("groups", "sub"), "row", "col")
    return jax.shard_map(
        body,
        mesh=mesh,
        in_specs=(P("groups", ("row", "col", "sub"), None),),
        out_specs=(placed, placed, placed),
        check_vma=False,
    )
```

```python
import functools
import math

import jax
import jax.numpy as jnp
import numpy as np
from jax import lax
from jax.experimental import pallas as pl
from jax.experimental.pallas import tpu as pltpu
from jax.sharding import PartitionSpec as P

PIX = 8
SUBN = 128
MARGIN = 8
WIN = SUBN + 2 * MARGIN
CHUNK = 256
LANES = 128
GROUP = CHUNK // PIX
DAMPING = 2e-05
F32 = jnp.float32
BF16 = jnp.bfloat16


def constant_pair(values):
    high = np.asarray(values).astype(jnp.bfloat16)
    low = (values - high.astype(np.float64)).astype(jnp.bfloat16)
    return jnp.asarray(high), jnp.asarray(low)


def sine_basis():
    order = np.arange(1, WIN + 1, dtype=np.float64)
    vectors = np.sqrt(2.0 / (WIN + 1)) * np.sin(math.pi * order[:, None] * order[None, :] / (WIN + 1))
    spectrum = 2.0 - 2.0 * np.cos(math.pi * order / (WIN + 1))
    return vectors, 1.0 / (spectrum[:, None] + spectrum[None, :] + DAMPING)


def padded(blocks):
    return -(-blocks * WIN // LANES) * LANES


def column_basis(blocks):
    vectors, _ = sine_basis()
    table = np.zeros((blocks * SUBN, padded(blocks)))
    for block in range(blocks):
        low = max(block * SUBN - MARGIN, 0)
        high = min((block + 1) * SUBN + MARGIN, blocks * SUBN)
        start = low - (block * SUBN - MARGIN)
        table[low:high, block * WIN : (block + 1) * WIN] = vectors[start : start + high - low]
    return table


def widened(table, blocks):
    wide = np.zeros(table.shape[:-1] + (padded(blocks),), np.float32)
    wide[..., : blocks * WIN] = np.tile(table, (1,) * (table.ndim - 1) + (blocks,))
    return wide


def edge_tables():
    vectors, scale = sine_basis()
    ends = np.concatenate([vectors[:8], vectors[WIN - 8 :]], 0)
    def driven_by(rows):
        return np.einsum("oa,ai,ab->iob", ends, vectors[:, rows], scale)
    return driven_by(slice(WIN - 8, WIN)), driven_by(slice(0, 9))


def coarse_inverse(blocks_down, blocks_across):
    number = blocks_down * blocks_across
    row, col = np.divmod(np.arange(number), blocks_across)
    apart = np.abs(row[:, None] - row[None, :]) + np.abs(col[:, None] - col[None, :])
    touching = (apart == 1).astype(np.float64)
    laplace = np.diag(touching.sum(1)) - touching
    return np.linalg.inv(SUBN * laplace + DAMPING * SUBN * SUBN * np.eye(number))


def halves(values):
    high = values.astype(BF16)
    return high, (values - high.astype(F32)).astype(BF16)


def dot(left, right):
    return jnp.dot(left, right, preferred_element_type=F32)


def dot_three(left, right):
    return dot(left[0], right[0]) + (dot(left[0], right[1]) + dot(left[1], right[0]))


def stacked_left(values, depth):
    wide = np.zeros((values.shape[0], depth))
    wide[:, : values.shape[1]] = values
    high = wide.astype(jnp.bfloat16)
    low = (wide - high.astype(np.float64)).astype(jnp.bfloat16)
    return jnp.asarray(np.concatenate([high, high, low], 1))


def dot_stacked(left, right):
    high, low = halves(right)
    return dot(left, jnp.concatenate([high, low, high], 0))


def iota(shape, axis):
    return lax.broadcasted_iota(jnp.int32, shape, axis)


def power(offset, kind):
    return jnp.where(kind == 0, 1.0, jnp.where(kind == 1, offset, offset * offset))


def offset_of(place):
    return (place % PIX).astype(F32) - (PIX - 1) / 2.0


def row_moments(stripe):
    shape = (3 * stripe, stripe * PIX)
    row, place = iota(shape, 0), iota(shape, 1)
    hit = place // PIX == row % stripe
    return jnp.where(hit, power(offset_of(place), row // stripe), 0.0).astype(BF16)


def column_moments(chunk):
    places = LANES // GROUP
    shape = (CHUNK, LANES)
    place, lane = iota(shape, 0), iota(shape, 1)
    kind = (lane // GROUP + (places - chunk)) % places
    hit = jnp.logical_and(place // PIX == lane % GROUP, kind < 3)
    return jnp.where(hit, power(offset_of(place), kind), 0.0).astype(BF16)


ORDER = {1: (), 2: (1,), 4: (2, 3, 1)}


def swapped(count):
    return count in ORDER


def exchange(pieces, axes, count):
    if not swapped(count):
        return [lax.all_to_all(pieces[0], axes, split_axis=0, concat_axis=0, tiled=True)]
    return [pieces[0]] + [
        lax.ppermute(pieces[k], axes, [(i, i ^ k) for i in range(count)]) for k in ORDER[count]
    ]


def piece_shapes(count, shape):
    if swapped(count):
        return [jax.ShapeDtypeStruct(shape, F32)] * count
    return [jax.ShapeDtypeStruct((count,) + shape, F32)]


def pick(index, values):
    total = values[-1]
    for step in range(len(values) - 1):
        total = jnp.where(index == step, values[step], total)
    return total


def moments_kernel(sizes, pixels, *refs):
    frames, stripe, blocks, cores, stripes = sizes
    pieces = blocks * cores
    slots = pieces if swapped(pieces) else 1
    fields, extras = refs[:slots], refs[slots : 2 * slots]
    held, arrived = refs[2 * slots :]
    width = blocks * SUBN
    places = LANES // GROUP
    span = LANES * PIX

    def copy(frame, part):
        where = (frame, slice(None), pl.ds(part * span, span))
        return pltpu.make_async_copy(pixels.at[where], held.at[where], arrived.at[frame, part])

    for frame in range(frames):
        for part in range(blocks):
            copy(frame, part).start()
    row_table = row_moments(stripe)
    col_tables = [column_moments(chunk) for chunk in range(places)]
    slot = lax.axis_index("col") * cores + lax.axis_index("sub")
    position = lax.axis_index("row") * pieces + slot
    group = iota((stripe, LANES), 1) // GROUP

    def gather(pieces, kind):
        total = pieces[-1]
        for chunk in range(places - 1):
            total = jnp.where(group == (kind + chunk) % places, pieces[chunk], total)
        return pltpu.roll(total, LANES - GROUP * kind, 1) if kind else total

    row = iota((stripe, width), 0)
    column = iota((stripe, width), 1)

    def columns_of(lines):
        high, low = halves(lines)
        pieces = []
        for chunk in range(places):
            cut = slice(chunk * CHUNK, (chunk + 1) * CHUNK)
            weights = col_tables[chunk]
            pieces.append(dot(high[:, cut], weights) + dot(low[:, cut], weights))
        plain = [piece[:stripe] for piece in pieces]
        tilted = [piece[stripe : 2 * stripe] for piece in pieces]
        bent = [piece[2 * stripe :] for piece in pieces]
        return gather(plain, 0), gather(plain, 1), gather(tilted, 0), gather(plain, 2) + gather(bent, 0)

    def finish(frame, parts):
        intensity, moment_x, moment_y, moment_two = [jnp.concatenate(kind, 1) for kind in zip(*parts)]
        inverse = 1.0 / intensity
        slope_x = moment_x * inverse
        slope_y = moment_y * inverse
        spot_size = moment_two * inverse - slope_x * slope_x - slope_y * slope_y
        mean_flux = intensity * (1.0 / (PIX * PIX))
        flow_x = jnp.where(column < width - 1, slope_x, 0.0)
        flow_y = jnp.where(position * stripe + row < stripes * stripe - 1, slope_y, 0.0)
        left = jnp.where(column > 0, pltpu.roll(flow_x, 1, 1), 0.0)
        above = pltpu.roll(flow_y, 1, 0)
        source = left - flow_x + jnp.where(row > 0, above, 0.0) - flow_y
        spill = jnp.where(row[:8] == 0, above[:8], 0.0)
        fluxes = [mean_flux[:, block * SUBN : (block + 1) * SUBN] for block in range(blocks)]
        spots = [spot_size[:, block * SUBN : (block + 1) * SUBN] for block in range(blocks)]
        return source, spill, fluxes, spots

    def lines_of(frame):
        for part in range(blocks):
            copy(frame, part).wait()
        return [dot(row_table, held[frame, :, pl.ds(part * span, span)]) for part in range(blocks)]

    lines = [lines_of(frame) for frame in range(frames)]
    found = [finish(frame, [columns_of(part) for part in lines[frame]]) for frame in range(frames)]
    for piece in range(pieces):
        if slots > 1:
            target = slot ^ piece
            frame, block = target % cores, target // cores
            source, spill = [pick(frame, [one[kind] for one in found]) for kind in range(2)]
            flux, spot = [pick(frame, [pick(block, one[kind]) for one in found]) for kind in range(2, 4)]
            field, extra = fields[piece], extras[piece]
        else:
            frame, block = piece % cores, piece // cores
            source, spill, flux, spot = found[frame]
            flux, spot = flux[block], spot[block]
            field, extra = fields[0].at[piece], extras[0].at[piece]
        field[:stripe, :] = source
        field[stripe:, :] = spill
        extra[:stripe, :] = flux
        extra[stripe:, :] = spot


def pieces_of(refs, slots, count, mine, order):
    if slots > 1:
        return [(mine ^ step, ref) for step, ref in zip((0,) + tuple(order), refs)]
    return [(step, refs[0].at[step]) for step in range(count)]


def rims_kernel(sizes, *refs):
    stripe, pieces, blocks, cores, rows = sizes
    slots = pieces if swapped(pieces) else 1
    outs = rows if swapped(rows) else 1
    fields, refs = refs[:slots], refs[slots:]
    basis_high, basis_low, back_high, back_low, drive, edge = refs[:6]
    scale, above_table, below_table = refs[6:9]
    sent, near, lined = refs[9 : 9 + outs], refs[9 + outs + 1], refs[9 + outs + 2]
    spectrum = refs[9 + outs]
    tiles = padded(blocks) // LANES
    mine = lax.axis_index("row")
    side = lax.axis_index("col")
    slot = side * cores + lax.axis_index("sub")
    arranged = pieces_of(fields, slots, pieces, slot, ORDER.get(pieces))
    lined[SUBN:, :] = jnp.zeros((16, lined.shape[1]), F32)
    for place, field in arranged:
        lined[pl.ds(pl.multiple_of(place * stripe, 8), stripe), :] = field[:stripe, :]
    for place, field in arranged:
        head = pl.ds(pl.multiple_of((place + 1) * stripe, 8), 8)
        lined[head, :] = lined[head, :] + field[stripe:, :]
    source = lined[...]
    across = dot_three(halves(source), (basis_high[...], basis_low[...]))
    driven = dot_stacked(drive[...], across)
    response = driven * scale[...]
    spectrum[...] = response
    edges = [dot_stacked(edge[...], response)]
    for table, start, count in ((above_table, 0, 8), (below_table, SUBN - 8, 9)):
        total = across[start : start + 1] * table[0]
        for step in range(1, count):
            total = total + across[start + step : start + step + 1] * table[step]
        edges.append(total)
    rims = dot_three(halves(jnp.concatenate(edges, 0)), (back_high[side], back_low[side]))
    near[:8, :] = jnp.where(mine > 0, rims[24:32], 0.0)
    near[8:, :] = jnp.where(mine < rows - 1, rims[32:40], 0.0)
    base = 8 * tiles
    tail = sent[0].shape[-2] - base - 8
    total = jnp.sum(source[:SUBN], 0, keepdims=True)
    place = iota((tail, LANES), 0)
    sums = jnp.zeros((tail, LANES), F32)
    for block in range(blocks):
        cut = slice(block * SUBN, (block + 1) * SUBN)
        sums = jnp.where(place == block, total[:, cut], sums)
        sums = jnp.where(place == blocks + block, source[SUBN : SUBN + 1, cut], sums)
    for tile in range(tiles):
        cut = slice(tile * LANES, (tile + 1) * LANES)
        sums = jnp.where(place == 2 * blocks + tile, across[SUBN : SUBN + 1, cut], sums)
    for target, piece in pieces_of(sent, outs, rows, mine, range(1, rows)):
        ahead = target - mine
        rim = jnp.where(ahead == -1, rims[:8], 0.0)
        rim = jnp.where(ahead == 1, rims[8:16], rim)
        rim = jnp.where(ahead == -2, rims[16:24], rim)
        rim = jnp.where(ahead == 2, rims[40:], rim)
        for tile in range(tiles):
            cut = slice(tile * LANES, (tile + 1) * LANES)
            line = jnp.where(ahead == -1, across[:8, cut], across[SUBN - 8 : SUBN, cut])
            piece[8 * tile : 8 * tile + 8, :] = line
        piece[base : base + 8, :] = rim
        piece[base + 8 :, :] = sums


def phase_kernel(sizes, *refs):
    stripe, pieces, blocks, cores, rows = sizes
    slots = pieces if swapped(pieces) else 1
    ins = rows if swapped(rows) else 1
    received, extras, refs = refs[:ins], refs[ins : ins + slots], refs[ins + slots :]
    spectrum, near, back_high, back_low, halo, out, scale, coarse = refs[:8]
    phase, mean_flux, spot_size = refs[8:]
    tiles = padded(blocks) // LANES
    mine = lax.axis_index("row")
    side = lax.axis_index("col")
    slot = side * cores + lax.axis_index("sub")
    for place, extra in pieces_of(extras, slots, pieces, slot, ORDER.get(pieces)):
        where = pl.ds(pl.multiple_of(place * stripe, 8), stripe)
        mean_flux[0, where, :] = extra[:stripe, :]
        spot_size[0, where, :] = extra[stripe:, :]
    base = 8 * tiles
    tail = received[0].shape[-2] - base - 8
    arranged = pieces_of(received, ins, rows, mine, ORDER.get(rows))

    def of_row(row, where):
        if ins == 1:
            inside = jnp.logical_and(row >= 0, row < rows)
            return jnp.where(inside, received[0][jnp.clip(row, 0, rows - 1), where, :], 0.0)
        total = jnp.zeros((where.stop - where.start, LANES), F32)
        for origin, piece in arranged[1:]:
            total = jnp.where(origin == row, piece[where, :], total)
        return total

    above = of_row(mine - 1, slice(0, received[0].shape[-2]))
    below = of_row(mine + 1, slice(0, base + 8))
    first = iota((8, LANES), 0) == 0
    top, bottom, spilt = [], [], []
    empty = [jnp.zeros((8, LANES), F32)] * tiles
    for tile in range(tiles):
        top.append(above[8 * tile : 8 * tile + 8])
        bottom.append(below[8 * tile : 8 * tile + 8])
        start = base + 8 + 2 * blocks + tile
        spilt.append(jnp.where(first, above[start : start + 1], 0.0))
    across = jnp.concatenate(
        [jnp.concatenate(part, 1) for part in (top, spilt, bottom, empty)], 0
    )
    driven = dot_stacked(halo[...], across)
    response = spectrum[...] + driven * scale[...]
    reach = dot_three(halves(response), (back_high[side], back_low[side]))
    solved = dot_stacked(out[...], reach)
    weighted = jnp.zeros((tail, coarse.shape[2]), F32)
    for origin, piece in arranged:
        count = jnp.sum(piece[base + 8 :, :], 1, keepdims=True)
        weighted = weighted + count * coarse[origin]
    own = iota(weighted.shape, 1) == mine * blocks + side
    level = jnp.sum(jnp.where(own, weighted, 0.0), keepdims=True)
    solved = solved + level
    rim = slice(base, base + 8)
    head = near[:8, :] + above[rim] + of_row(mine - 2, rim)
    foot = near[8:, :] + below[rim] + of_row(mine + 2, rim)
    phase[0, :8, :] = solved[:8] + head
    phase[0, 8 : SUBN - 8, :] = solved[8 : SUBN - 8]
    phase[0, SUBN - 8 :, :] = solved[SUBN - 8 :] + foot


def coarse_table(blocks_down, blocks_across, tail):
    inverse = coarse_inverse(blocks_down, blocks_across)
    number = blocks_down * blocks_across
    lanes = -(-number // LANES) * LANES
    table = np.zeros((blocks_down, tail, lanes), np.float32)
    for row in range(blocks_down):
        for block in range(blocks_across):
            table[row, block, :number] = inverse[row * blocks_across + block]
            if row + 1 < blocks_down:
                table[row, blocks_across + block, :number] = inverse[(row + 1) * blocks_across + block]
    return table


def in_vmem(count):
    return [pl.BlockSpec(memory_space=pltpu.VMEM)] * count


PARAMS = pltpu.CompilerParams(vmem_limit_bytes=48 * 1024 * 1024)


def body(pixels):
    frames, pixel_rows, pixel_cols = pixels.shape
    stripe = pixel_rows // PIX
    width = pixel_cols // PIX
    rows = lax.axis_size("row")
    blocks = lax.axis_size("col")
    cores = lax.axis_size("sub")
    pieces = blocks * cores
    assert frames == cores and width == blocks * SUBN and stripe * pieces == SUBN

    field_shapes = piece_shapes(pieces, (stripe + 8, width))
    extra_shapes = piece_shapes(pieces, (2 * stripe, SUBN))
    made = pl.pallas_call(
        functools.partial(moments_kernel, (frames, stripe, blocks, cores, rows * pieces)),
        out_shape=field_shapes + extra_shapes,
        in_specs=[pl.BlockSpec(memory_space=pltpu.HBM)],
        out_specs=in_vmem(len(field_shapes + extra_shapes)),
        scratch_shapes=[
            pltpu.VMEM((frames, pixel_rows, pixel_cols), BF16),
            pltpu.SemaphoreType.DMA((frames, blocks)),
        ],
        compiler_params=PARAMS,
        name="moments",
    )(pltpu.with_memory_space_constraint(pixels, pltpu.HBM))
    fields = exchange(made[: len(field_shapes)], ("col", "sub"), pieces)
    extras = exchange(made[len(field_shapes) :], ("col", "sub"), pieces)

    vectors, scale = sine_basis()
    basis = column_basis(blocks)
    full = padded(blocks)
    tiles = full // LANES
    basis_pair = constant_pair(basis)
    back_pair = constant_pair(basis.T.reshape(full, blocks, SUBN).transpose(1, 0, 2))
    scale_wide = jnp.asarray(widened(scale, blocks))
    drive = stacked_left(vectors[:, MARGIN:], WIN)
    edge = stacked_left(np.concatenate([vectors[:8], vectors[WIN - 8 :]], 0), WIN)
    side_tables = [jnp.asarray(widened(table, blocks)) for table in edge_tables()]
    tail = -(-(2 * blocks + tiles) // 8) * 8
    height = 8 * tiles + 8 + tail

    row_shapes = piece_shapes(rows, (height, LANES))
    sizes = (stripe, pieces, blocks, cores, rows)
    *sent, spectrum, near = pl.pallas_call(
        functools.partial(rims_kernel, sizes),
        out_shape=row_shapes
        + [jax.ShapeDtypeStruct((WIN, full), F32), jax.ShapeDtypeStruct((16, SUBN), F32)],
        in_specs=in_vmem(len(fields) + 9),
        out_specs=in_vmem(len(row_shapes) + 2),
        scratch_shapes=[pltpu.VMEM((SUBN + 16, width), F32)],
        compiler_params=PARAMS,
        name="rims",
    )(*fields, *basis_pair, *back_pair, drive, edge, scale_wide, *side_tables)
    received = exchange(sent, ("row",), rows)

    halo = np.zeros((WIN, 24))
    halo[:, :9] = vectors[:, :9]
    halo[:, 16:] = vectors[:, WIN - 8 :]
    halo = stacked_left(halo, 32)
    out = stacked_left(vectors[MARGIN : MARGIN + SUBN], WIN)
    return pl.pallas_call(
        functools.partial(phase_kernel, sizes),
        out_shape=[jax.ShapeDtypeStruct((1, SUBN, SUBN), F32)] * 3,
        in_specs=in_vmem(len(received) + len(extras) + 8),
        out_specs=in_vmem(3),
        compiler_params=PARAMS,
        name="phase",
    )(
        *received, *extras, spectrum, near, *back_pair, halo, out, scale_wide,
        jnp.asarray(coarse_table(rows, blocks, tail)),
    )


def solution(mesh):
    placed = P(("groups", "sub"), "row", "col")
    return jax.shard_map(
        body,
        mesh=mesh,
        in_specs=(P("groups", ("row", "col", "sub"), None),),
        out_specs=(placed, placed, placed),
        check_vma=False,
    )
```

```python
import functools
import math

import jax
import jax.numpy as jnp
import numpy as np
from jax import lax
from jax.experimental import pallas as pl
from jax.experimental.pallas import tpu as pltpu
from jax.sharding import PartitionSpec as P

PIX = 8
SUBN = 128
MARGIN = 8
WIN = SUBN + 2 * MARGIN
CHUNK = 256
LANES = 128
GROUP = CHUNK // PIX
DAMPING = 2e-05
F32 = jnp.float32
BF16 = jnp.bfloat16


def constant_pair(values):
    high = np.asarray(values).astype(jnp.bfloat16)
    low = (values - high.astype(np.float64)).astype(jnp.bfloat16)
    return high, low


def sine_basis():
    order = np.arange(1, WIN + 1, dtype=np.float64)
    vectors = np.sqrt(2.0 / (WIN + 1)) * np.sin(math.pi * order[:, None] * order[None, :] / (WIN + 1))
    spectrum = 2.0 - 2.0 * np.cos(math.pi * order / (WIN + 1))
    return vectors, 1.0 / (spectrum[:, None] + spectrum[None, :] + DAMPING)


def padded(blocks):
    return -(-blocks * WIN // LANES) * LANES


def column_basis(blocks):
    vectors, _ = sine_basis()
    table = np.zeros((blocks * SUBN, padded(blocks)))
    for block in range(blocks):
        low = max(block * SUBN - MARGIN, 0)
        high = min((block + 1) * SUBN + MARGIN, blocks * SUBN)
        start = low - (block * SUBN - MARGIN)
        table[low:high, block * WIN : (block + 1) * WIN] = vectors[start : start + high - low]
    return table


def widened(table, blocks):
    wide = np.zeros(table.shape[:-1] + (padded(blocks),), np.float32)
    wide[..., : blocks * WIN] = np.tile(table, (1,) * (table.ndim - 1) + (blocks,))
    return wide


def edge_tables():
    vectors, scale = sine_basis()
    ends = np.concatenate([vectors[:8], vectors[WIN - 8 :]], 0)
    def driven_by(rows):
        return np.einsum("oa,ai,ab->iob", ends, vectors[:, rows], scale)
    return driven_by(slice(WIN - 8, WIN)), driven_by(slice(0, 9))


def coarse_inverse(blocks_down, blocks_across):
    number = blocks_down * blocks_across
    row, col = np.divmod(np.arange(number), blocks_across)
    apart = np.abs(row[:, None] - row[None, :]) + np.abs(col[:, None] - col[None, :])
    touching = (apart == 1).astype(np.float64)
    laplace = np.diag(touching.sum(1)) - touching
    return np.linalg.inv(SUBN * laplace + DAMPING * SUBN * SUBN * np.eye(number))


def halves(values):
    high = values.astype(BF16)
    return high, (values - high.astype(F32)).astype(BF16)


def dot(left, right):
    return jnp.dot(left, right, preferred_element_type=F32)


def dot_three(left, right):
    return dot(left[0], right[0]) + (dot(left[0], right[1]) + dot(left[1], right[0]))


def stacked_left(values, depth):
    wide = np.zeros((values.shape[0], depth))
    wide[:, : values.shape[1]] = values
    high = wide.astype(jnp.bfloat16)
    low = (wide - high.astype(np.float64)).astype(jnp.bfloat16)
    return np.concatenate([high, high, low], 1)


def dot_stacked(left, right):
    high, low = halves(right)
    return dot(left, jnp.concatenate([high, low, high], 0))


def iota(shape, axis):
    return lax.broadcasted_iota(jnp.int32, shape, axis)


def power(offset, kind):
    return jnp.where(kind == 0, 1.0, jnp.where(kind == 1, offset, offset * offset))


def offset_of(place):
    return (place % PIX).astype(F32) - (PIX - 1) / 2.0


def row_moments(stripe):
    shape = (3 * stripe, stripe * PIX)
    row, place = iota(shape, 0), iota(shape, 1)
    hit = place // PIX == row % stripe
    return jnp.where(hit, power(offset_of(place), row // stripe), 0.0).astype(BF16)


def column_moments(chunk):
    places = LANES // GROUP
    shape = (CHUNK, LANES)
    place, lane = iota(shape, 0), iota(shape, 1)
    kind = (lane // GROUP + (places - chunk)) % places
    hit = jnp.logical_and(place // PIX == lane % GROUP, kind < 3)
    return jnp.where(hit, power(offset_of(place), kind), 0.0).astype(BF16)


ORDER = {1: (), 2: (1,), 4: (2, 3, 1)}


def swapped(count):
    return count in ORDER


def exchange(pieces, axes, count):
    if not swapped(count):
        return [lax.all_to_all(pieces[0], axes, split_axis=0, concat_axis=0, tiled=True)]
    return [pieces[0]] + [
        lax.ppermute(pieces[k], axes, [(i, i ^ k) for i in range(count)]) for k in ORDER[count]
    ]


def piece_shapes(count, shape):
    if swapped(count):
        return [jax.ShapeDtypeStruct(shape, F32)] * count
    return [jax.ShapeDtypeStruct((count,) + shape, F32)]


def pick(index, values):
    total = values[-1]
    for step in range(len(values) - 1):
        total = jnp.where(index == step, values[step], total)
    return total


def spill_rows(blocks):
    return -(-blocks // 8) * 8


def moments_kernel(sizes, pixels, *refs):
    frames, stripe, blocks, cores, stripes = sizes
    pieces = blocks * cores
    slots = pieces if swapped(pieces) else 1
    fields, extras = refs[:slots], refs[slots : 2 * slots]
    held, arrived = refs[2 * slots :]
    width = blocks * SUBN
    places = LANES // GROUP
    span = LANES * PIX

    def copy(frame, part):
        where = (frame, slice(None), pl.ds(part * span, span))
        return pltpu.make_async_copy(pixels.at[where], held.at[where], arrived.at[frame, part])

    for frame in range(frames):
        for part in range(blocks):
            copy(frame, part).start()
    row_table = row_moments(stripe)
    col_tables = [column_moments(chunk) for chunk in range(places)]
    slot = lax.axis_index("col") * cores + lax.axis_index("sub")
    position = lax.axis_index("row") * pieces + slot
    group = iota((stripe, LANES), 1) // GROUP

    def gather(pieces, kind):
        total = pieces[-1]
        for chunk in range(places - 1):
            total = jnp.where(group == (kind + chunk) % places, pieces[chunk], total)
        return pltpu.roll(total, LANES - GROUP * kind, 1) if kind else total

    row = iota((stripe, width), 0)
    column = iota((stripe, width), 1)

    def columns_of(lines):
        high, low = halves(lines)
        pieces = []
        for chunk in range(places):
            cut = slice(chunk * CHUNK, (chunk + 1) * CHUNK)
            weights = col_tables[chunk]
            pieces.append(dot(high[:, cut], weights) + dot(low[:, cut], weights))
        plain = [piece[:stripe] for piece in pieces]
        tilted = [piece[stripe : 2 * stripe] for piece in pieces]
        bent = [piece[2 * stripe :] for piece in pieces]
        return gather(plain, 0), gather(plain, 1), gather(tilted, 0), gather(plain, 2) + gather(bent, 0)

    def finish(frame, parts):
        intensity, moment_x, moment_y, moment_two = [jnp.concatenate(kind, 1) for kind in zip(*parts)]
        inverse = 1.0 / intensity
        slope_x = moment_x * inverse
        slope_y = moment_y * inverse
        spot_size = moment_two * inverse - slope_x * slope_x - slope_y * slope_y
        mean_flux = intensity * (1.0 / (PIX * PIX))
        flow_x = jnp.where(column < width - 1, slope_x, 0.0)
        flow_y = jnp.where(position * stripe + row < stripes * stripe - 1, slope_y, 0.0)
        left = jnp.where(column > 0, pltpu.roll(flow_x, 1, 1), 0.0)
        above = pltpu.roll(flow_y, 1, 0)
        source = left - flow_x + jnp.where(row > 0, above, 0.0) - flow_y
        spill = jnp.zeros((spill_rows(blocks), LANES), F32)
        spot_row = iota(spill.shape, 0)
        for block in range(blocks):
            last = flow_y[stripe - 1 :, block * SUBN : (block + 1) * SUBN]
            spill = jnp.where(spot_row == block, last, spill)
        fluxes = [mean_flux[:, block * SUBN : (block + 1) * SUBN] for block in range(blocks)]
        spots = [spot_size[:, block * SUBN : (block + 1) * SUBN] for block in range(blocks)]
        return source, spill, fluxes, spots

    def lines_of(frame):
        for part in range(blocks):
            copy(frame, part).wait()
        return [dot(row_table, held[frame, :, pl.ds(part * span, span)]) for part in range(blocks)]

    lines = [lines_of(frame) for frame in range(frames)]
    found = [finish(frame, [columns_of(part) for part in lines[frame]]) for frame in range(frames)]
    for piece in range(pieces):
        if slots > 1:
            target = slot ^ piece
            frame, block = target % cores, target // cores
            source, spill = [pick(frame, [one[kind] for one in found]) for kind in range(2)]
            flux, spot = [pick(frame, [pick(block, one[kind]) for one in found]) for kind in range(2, 4)]
            field, extra = fields[piece], extras[piece]
        else:
            frame, block = piece % cores, piece // cores
            source, spill, flux, spot = found[frame]
            flux, spot = flux[block], spot[block]
            field, extra = fields[0].at[piece], extras[0].at[piece]
        for block in range(blocks):
            field[block * stripe : (block + 1) * stripe, :] = source[:, block * SUBN : (block + 1) * SUBN]
        field[blocks * stripe :, :] = spill
        extra[:stripe, :] = flux
        extra[stripe:, :] = spot


def pieces_of(refs, slots, count, mine, order):
    if slots > 1:
        return [(mine ^ step, ref) for step, ref in zip((0,) + tuple(order), refs)]
    return [(step, refs[0].at[step]) for step in range(count)]


def back_of(back, side, tiles):
    depth = tiles * LANES
    start = pl.multiple_of(side * (2 * depth), LANES)
    return back[pl.ds(start, depth), :], back[pl.ds(start + depth, depth), :]


def rims_kernel(sizes, *refs):
    stripe, pieces, blocks, cores, rows = sizes
    width = blocks * SUBN
    slots = pieces if swapped(pieces) else 1
    outs = rows if swapped(rows) else 1
    fields, refs = refs[:slots], refs[slots:]
    basis, back, left, real = refs[:4]
    sent, near, lined = refs[4 : 4 + outs], refs[4 + outs + 1], refs[4 + outs + 2]
    spectrum = refs[4 + outs]
    tiles = padded(blocks) // LANES
    mine = lax.axis_index("row")
    side = lax.axis_index("col")
    slot = side * cores + lax.axis_index("sub")
    arranged = pieces_of(fields, slots, pieces, slot, ORDER.get(pieces))
    lined[SUBN:, :] = jnp.zeros((16, lined.shape[1]), F32)
    for place, field in arranged:
        for block in range(blocks):
            where = pl.ds(pl.multiple_of(place * stripe, 8), stripe)
            lined[where, block * SUBN : (block + 1) * SUBN] = field[block * stripe : (block + 1) * stripe, :]
    first = iota((8, LANES), 0) == 0
    for place, field in arranged:
        head = pl.ds(pl.multiple_of((place + 1) * stripe, 8), 8)
        for block in range(blocks):
            cut = slice(block * SUBN, (block + 1) * SUBN)
            last = field[blocks * stripe + block : blocks * stripe + block + 1, :]
            lined[head, cut] = lined[head, cut] + jnp.where(first, last, 0.0)
    source = lined[...]
    across = dot_three(halves(source), (basis[:width, :], basis[width:, :]))
    driven = dot_stacked(left[:WIN, :], across)
    response = driven * real[:WIN, :]
    spectrum[...] = response
    edges = [dot_stacked(left[WIN : WIN + 16, :], response)]
    for place, start, count in ((WIN, 0, 8), (WIN + 8 * 16, SUBN - 8, 9)):
        total = across[start : start + 1] * real[place : place + 16, :]
        for step in range(1, count):
            table = real[place + 16 * step : place + 16 * step + 16, :]
            total = total + across[start + step : start + step + 1] * table
        edges.append(total)
    rims = dot_three(halves(jnp.concatenate(edges, 0)), back_of(back, side, tiles))
    near[:8, :] = jnp.where(mine > 0, rims[24:32], 0.0)
    near[8:, :] = jnp.where(mine < rows - 1, rims[32:40], 0.0)
    base = 8 * tiles
    tail = sent[0].shape[-2] - base - 8
    total = jnp.sum(source[:SUBN], 0, keepdims=True)
    place = iota((tail, LANES), 0)
    sums = jnp.zeros((tail, LANES), F32)
    for block in range(blocks):
        cut = slice(block * SUBN, (block + 1) * SUBN)
        sums = jnp.where(place == block, total[:, cut], sums)
        sums = jnp.where(place == blocks + block, source[SUBN : SUBN + 1, cut], sums)
    for tile in range(tiles):
        cut = slice(tile * LANES, (tile + 1) * LANES)
        sums = jnp.where(place == 2 * blocks + tile, across[SUBN : SUBN + 1, cut], sums)
    for target, piece in pieces_of(sent, outs, rows, mine, range(1, rows)):
        ahead = target - mine
        rim = jnp.where(ahead == -1, rims[:8], 0.0)
        rim = jnp.where(ahead == 1, rims[8:16], rim)
        rim = jnp.where(ahead == -2, rims[16:24], rim)
        rim = jnp.where(ahead == 2, rims[40:], rim)
        for tile in range(tiles):
            cut = slice(tile * LANES, (tile + 1) * LANES)
            line = jnp.where(ahead == -1, across[:8, cut], across[SUBN - 8 : SUBN, cut])
            piece[8 * tile : 8 * tile + 8, :] = line
        piece[base : base + 8, :] = rim
        piece[base + 8 :, :] = sums


def phase_kernel(sizes, *refs):
    stripe, pieces, blocks, cores, rows = sizes
    slots = pieces if swapped(pieces) else 1
    ins = rows if swapped(rows) else 1
    received, extras, refs = refs[:ins], refs[ins : ins + slots], refs[ins + slots :]
    spectrum, near, back, left, real = refs[:5]
    phase, mean_flux, spot_size = refs[5:]
    tiles = padded(blocks) // LANES
    mine = lax.axis_index("row")
    side = lax.axis_index("col")
    slot = side * cores + lax.axis_index("sub")
    for place, extra in pieces_of(extras, slots, pieces, slot, ORDER.get(pieces)):
        where = pl.ds(pl.multiple_of(place * stripe, 8), stripe)
        mean_flux[0, where, :] = extra[:stripe, :]
        spot_size[0, where, :] = extra[stripe:, :]
    base = 8 * tiles
    tail = received[0].shape[-2] - base - 8
    arranged = pieces_of(received, ins, rows, mine, ORDER.get(rows))

    def of_row(row, where):
        if ins == 1:
            inside = jnp.logical_and(row >= 0, row < rows)
            return jnp.where(inside, received[0][jnp.clip(row, 0, rows - 1), where, :], 0.0)
        total = jnp.zeros((where.stop - where.start, LANES), F32)
        for origin, piece in arranged[1:]:
            total = jnp.where(origin == row, piece[where, :], total)
        return total

    above = of_row(mine - 1, slice(0, received[0].shape[-2]))
    below = of_row(mine + 1, slice(0, base + 8))
    first = iota((8, LANES), 0) == 0
    top, bottom, spilt = [], [], []
    empty = [jnp.zeros((8, LANES), F32)] * tiles
    for tile in range(tiles):
        top.append(above[8 * tile : 8 * tile + 8])
        bottom.append(below[8 * tile : 8 * tile + 8])
        start = base + 8 + 2 * blocks + tile
        spilt.append(jnp.where(first, above[start : start + 1], 0.0))
    across = jnp.concatenate(
        [jnp.concatenate(part, 1) for part in (top, spilt, bottom, empty)], 0
    )
    halo = left[WIN + 16 + SUBN :, : 3 * across.shape[0]]
    driven = dot_stacked(halo, across)
    response = spectrum[...] + driven * real[:WIN, :]
    reach = dot_three(halves(response), back_of(back, side, tiles))
    solved = dot_stacked(left[WIN + 16 : WIN + 16 + SUBN, :], reach)
    coarse = WIN + 17 * 16
    weighted = jnp.zeros((tail, real.shape[1]), F32)
    for origin, piece in arranged:
        count = jnp.sum(piece[base + 8 :, :], 1, keepdims=True)
        weighted = weighted + count * real[pl.ds(pl.multiple_of(coarse + origin * tail, 8), tail), :]
    own = iota(weighted.shape, 1) == mine * blocks + side
    level = jnp.sum(jnp.where(own, weighted, 0.0), keepdims=True)
    solved = solved + level
    rim = slice(base, base + 8)
    head = near[:8, :] + above[rim] + of_row(mine - 2, rim)
    foot = near[8:, :] + below[rim] + of_row(mine + 2, rim)
    phase[0, :8, :] = solved[:8] + head
    phase[0, 8 : SUBN - 8, :] = solved[8 : SUBN - 8]
    phase[0, SUBN - 8 :, :] = solved[SUBN - 8 :] + foot


def coarse_table(blocks_down, blocks_across, tail):
    inverse = coarse_inverse(blocks_down, blocks_across)
    number = blocks_down * blocks_across
    lanes = -(-number // LANES) * LANES
    table = np.zeros((blocks_down, tail, lanes), np.float32)
    for row in range(blocks_down):
        for block in range(blocks_across):
            table[row, block, :number] = inverse[row * blocks_across + block]
            if row + 1 < blocks_down:
                table[row, blocks_across + block, :number] = inverse[(row + 1) * blocks_across + block]
    return table


def in_vmem(count):
    return [pl.BlockSpec(memory_space=pltpu.VMEM)] * count


PARAMS = pltpu.CompilerParams(vmem_limit_bytes=48 * 1024 * 1024)


def body(pixels):
    frames, pixel_rows, pixel_cols = pixels.shape
    stripe = pixel_rows // PIX
    width = pixel_cols // PIX
    rows = lax.axis_size("row")
    blocks = lax.axis_size("col")
    cores = lax.axis_size("sub")
    pieces = blocks * cores
    assert frames == cores and width == blocks * SUBN and stripe * pieces == SUBN

    field_shapes = piece_shapes(pieces, (blocks * stripe + spill_rows(blocks), LANES))
    extra_shapes = piece_shapes(pieces, (2 * stripe, SUBN))
    made = pl.pallas_call(
        functools.partial(moments_kernel, (frames, stripe, blocks, cores, rows * pieces)),
        out_shape=field_shapes + extra_shapes,
        in_specs=[pl.BlockSpec(memory_space=pltpu.HBM)],
        out_specs=in_vmem(len(field_shapes + extra_shapes)),
        scratch_shapes=[
            pltpu.VMEM((frames, pixel_rows, pixel_cols), BF16),
            pltpu.SemaphoreType.DMA((frames, blocks)),
        ],
        compiler_params=PARAMS,
        name="moments",
    )(pltpu.with_memory_space_constraint(pixels, pltpu.HBM))
    fields = exchange(made[: len(field_shapes)], ("col", "sub"), pieces)
    extras = exchange(made[len(field_shapes) :], ("col", "sub"), pieces)

    vectors, scale = sine_basis()
    basis = column_basis(blocks)
    full = padded(blocks)
    tiles = full // LANES
    tail = -(-(2 * blocks + tiles) // 8) * 8
    height = 8 * tiles + 8 + tail
    halo = np.zeros((WIN, 24))
    halo[:, :9] = vectors[:, :9]
    halo[:, 16:] = vectors[:, WIN - 8 :]
    lefts = [
        stacked_left(vectors[:, MARGIN:], WIN),
        stacked_left(np.concatenate([vectors[:8], vectors[WIN - 8 :]], 0), WIN),
        stacked_left(vectors[MARGIN : MARGIN + SUBN], WIN),
        np.pad(stacked_left(halo, 32), ((0, 0), (0, 3 * WIN - 96))),
    ]
    back = constant_pair(basis.T.reshape(full, blocks, SUBN).transpose(1, 0, 2))
    tables = [widened(table, blocks).reshape(-1, full) for table in (scale,) + edge_tables()]
    coarse = coarse_table(rows, blocks, tail)
    tables.append(np.pad(coarse, ((0, 0), (0, 0), (0, full - coarse.shape[2]))).reshape(-1, full))
    wide = jnp.asarray(np.concatenate(constant_pair(basis), 0))
    back = jnp.asarray(np.concatenate(back, 1).reshape(-1, SUBN))
    left = jnp.asarray(np.concatenate(lefts, 0))
    real = jnp.asarray(np.concatenate(tables, 0).astype(np.float32))

    row_shapes = piece_shapes(rows, (height, LANES))
    sizes = (stripe, pieces, blocks, cores, rows)
    *sent, spectrum, near = pl.pallas_call(
        functools.partial(rims_kernel, sizes),
        out_shape=row_shapes
        + [jax.ShapeDtypeStruct((WIN, full), F32), jax.ShapeDtypeStruct((16, SUBN), F32)],
        in_specs=in_vmem(len(fields) + 4),
        out_specs=in_vmem(len(row_shapes) + 2),
        scratch_shapes=[pltpu.VMEM((SUBN + 16, width), F32)],
        compiler_params=PARAMS,
        name="rims",
    )(*fields, wide, back, left, real)
    received = exchange(sent, ("row",), rows)

    return pl.pallas_call(
        functools.partial(phase_kernel, sizes),
        out_shape=[jax.ShapeDtypeStruct((1, SUBN, SUBN), F32)] * 3,
        in_specs=in_vmem(len(received) + len(extras) + 5),
        out_specs=in_vmem(3),
        compiler_params=PARAMS,
        name="phase",
    )(*received, *extras, spectrum, near, back, left, real)


def solution(mesh):
    placed = P(("groups", "sub"), "row", "col")
    return jax.shard_map(
        body,
        mesh=mesh,
        in_specs=(P("groups", ("row", "col", "sub"), None),),
        out_specs=(placed, placed, placed),
        check_vma=False,
    )
```

```python
import functools
import math

import jax
import jax.numpy as jnp
import numpy as np
from jax import lax
from jax.experimental import pallas as pl
from jax.experimental.pallas import tpu as pltpu
from jax.sharding import PartitionSpec as P

PIX = 8
SUBN = 128
MARGIN = 8
WIN = SUBN + 2 * MARGIN
CHUNK = 256
LANES = 128
GROUP = CHUNK // PIX
DAMPING = 2e-05
F32 = jnp.float32
BF16 = jnp.bfloat16


def constant_pair(values):
    high = np.asarray(values).astype(jnp.bfloat16)
    low = (values - high.astype(np.float64)).astype(jnp.bfloat16)
    return high, low


def sine_basis():
    order = np.arange(1, WIN + 1, dtype=np.float64)
    vectors = np.sqrt(2.0 / (WIN + 1)) * np.sin(math.pi * order[:, None] * order[None, :] / (WIN + 1))
    spectrum = 2.0 - 2.0 * np.cos(math.pi * order / (WIN + 1))
    return vectors, 1.0 / (spectrum[:, None] + spectrum[None, :] + DAMPING)


def padded(blocks):
    return -(-blocks * WIN // LANES) * LANES


def column_basis(blocks):
    vectors, _ = sine_basis()
    table = np.zeros((blocks * SUBN, padded(blocks)))
    for block in range(blocks):
        low = max(block * SUBN - MARGIN, 0)
        high = min((block + 1) * SUBN + MARGIN, blocks * SUBN)
        start = low - (block * SUBN - MARGIN)
        table[low:high, block * WIN : (block + 1) * WIN] = vectors[start : start + high - low]
    return table


def widened(table, blocks):
    wide = np.zeros(table.shape[:-1] + (padded(blocks),), np.float32)
    wide[..., : blocks * WIN] = np.tile(table, (1,) * (table.ndim - 1) + (blocks,))
    return wide


def edge_tables():
    vectors, scale = sine_basis()
    ends = np.concatenate([vectors[:8], vectors[WIN - 8 :]], 0)
    def driven_by(rows):
        return np.einsum("oa,ai,ab->iob", ends, vectors[:, rows], scale)
    return driven_by(slice(WIN - 8, WIN)), driven_by(slice(0, 9))


def coarse_inverse(blocks_down, blocks_across):
    number = blocks_down * blocks_across
    row, col = np.divmod(np.arange(number), blocks_across)
    apart = np.abs(row[:, None] - row[None, :]) + np.abs(col[:, None] - col[None, :])
    touching = (apart == 1).astype(np.float64)
    laplace = np.diag(touching.sum(1)) - touching
    return np.linalg.inv(SUBN * laplace + DAMPING * SUBN * SUBN * np.eye(number))


def halves(values):
    high = values.astype(BF16)
    return high, (values - high.astype(F32)).astype(BF16)


def dot(left, right):
    return jnp.dot(left, right, preferred_element_type=F32)


def dot_three(left, right):
    return dot(left[0], right[0]) + (dot(left[0], right[1]) + dot(left[1], right[0]))


def stacked_left(values, depth):
    wide = np.zeros((values.shape[0], depth))
    wide[:, : values.shape[1]] = values
    high = wide.astype(jnp.bfloat16)
    low = (wide - high.astype(np.float64)).astype(jnp.bfloat16)
    return np.concatenate([high, high, low], 1)


def dot_stacked(left, right):
    high, low = halves(right)
    return dot(left, jnp.concatenate([high, low, high], 0))


def iota(shape, axis):
    return lax.broadcasted_iota(jnp.int32, shape, axis)


def power(offset, kind):
    return jnp.where(kind == 0, 1.0, jnp.where(kind == 1, offset, offset * offset))


def offset_of(place):
    return (place % PIX).astype(F32) - (PIX - 1) / 2.0


def row_moments(stripe):
    shape = (3 * stripe, stripe * PIX)
    row, place = iota(shape, 0), iota(shape, 1)
    hit = place // PIX == row % stripe
    return jnp.where(hit, power(offset_of(place), row // stripe), 0.0).astype(BF16)


def column_moments(chunk):
    places = LANES // GROUP
    shape = (CHUNK, LANES)
    place, lane = iota(shape, 0), iota(shape, 1)
    kind = (lane // GROUP + (places - chunk)) % places
    hit = jnp.logical_and(place // PIX == lane % GROUP, kind < 3)
    return jnp.where(hit, power(offset_of(place), kind), 0.0).astype(BF16)


ORDER = {1: (), 2: (1,), 4: (2, 3, 1)}


def swapped(count):
    return count in ORDER


def exchange(pieces, axes, count):
    if not swapped(count):
        return [lax.all_to_all(pieces[0], axes, split_axis=0, concat_axis=0, tiled=True)]
    return [pieces[0]] + [
        lax.ppermute(pieces[k], axes, [(i, i ^ k) for i in range(count)]) for k in ORDER[count]
    ]


def piece_shapes(count, shape):
    if swapped(count):
        return [jax.ShapeDtypeStruct(shape, F32)] * count
    return [jax.ShapeDtypeStruct((count,) + shape, F32)]


def pick(index, values):
    total = values[-1]
    for step in range(len(values) - 1):
        total = jnp.where(index == step, values[step], total)
    return total


def spill_rows(blocks):
    return -(-blocks // 8) * 8


def moments_kernel(sizes, pixels, *refs):
    frames, stripe, blocks, cores, stripes = sizes
    pieces = blocks * cores
    slots = pieces if swapped(pieces) else 1
    fields, extras = refs[:slots], refs[slots : 2 * slots]
    held, arrived = refs[2 * slots :]
    width = blocks * SUBN
    places = LANES // GROUP
    span = LANES * PIX

    def copy(frame, part):
        where = (frame, slice(None), pl.ds(part * span, span))
        return pltpu.make_async_copy(pixels.at[where], held.at[where], arrived.at[frame, part])

    for frame in range(frames):
        for part in range(blocks):
            copy(frame, part).start()
    row_table = row_moments(stripe)
    col_tables = [column_moments(chunk) for chunk in range(places)]
    slot = lax.axis_index("col") * cores + lax.axis_index("sub")
    position = lax.axis_index("row") * pieces + slot
    group = iota((stripe, LANES), 1) // GROUP

    def gather(pieces, kind):
        total = pieces[-1]
        for chunk in range(places - 1):
            total = jnp.where(group == (kind + chunk) % places, pieces[chunk], total)
        return pltpu.roll(total, LANES - GROUP * kind, 1) if kind else total

    row = iota((stripe, width), 0)
    column = iota((stripe, width), 1)

    def columns_of(lines):
        high, low = halves(lines)
        pieces = []
        for chunk in range(places):
            cut = slice(chunk * CHUNK, (chunk + 1) * CHUNK)
            weights = col_tables[chunk]
            pieces.append(dot(high[:, cut], weights) + dot(low[:, cut], weights))
        plain = [piece[:stripe] for piece in pieces]
        tilted = [piece[stripe : 2 * stripe] for piece in pieces]
        bent = [piece[2 * stripe :] for piece in pieces]
        return gather(plain, 0), gather(plain, 1), gather(tilted, 0), gather(plain, 2) + gather(bent, 0)

    def finish(frame, parts):
        intensity, moment_x, moment_y, moment_two = [jnp.concatenate(kind, 1) for kind in zip(*parts)]
        inverse = 1.0 / intensity
        slope_x = moment_x * inverse
        slope_y = moment_y * inverse
        spot_size = moment_two * inverse - slope_x * slope_x - slope_y * slope_y
        mean_flux = intensity * (1.0 / (PIX * PIX))
        flow_x = jnp.where(column < width - 1, slope_x, 0.0)
        flow_y = jnp.where(position * stripe + row < stripes * stripe - 1, slope_y, 0.0)
        left = jnp.where(column > 0, pltpu.roll(flow_x, 1, 1), 0.0)
        above = pltpu.roll(flow_y, 1, 0)
        source = left - flow_x + jnp.where(row > 0, above, 0.0) - flow_y
        spill = jnp.zeros((spill_rows(blocks), LANES), F32)
        spot_row = iota(spill.shape, 0)
        for block in range(blocks):
            last = flow_y[stripe - 1 :, block * SUBN : (block + 1) * SUBN]
            spill = jnp.where(spot_row == block, last, spill)
        fluxes = [mean_flux[:, block * SUBN : (block + 1) * SUBN] for block in range(blocks)]
        spots = [spot_size[:, block * SUBN : (block + 1) * SUBN] for block in range(blocks)]
        return source, spill, fluxes, spots

    def lines_of(frame):
        for part in range(blocks):
            copy(frame, part).wait()
        return [dot(row_table, held[frame, :, pl.ds(part * span, span)]) for part in range(blocks)]

    lines = [lines_of(frame) for frame in range(frames)]
    found = [finish(frame, [columns_of(part) for part in lines[frame]]) for frame in range(frames)]
    for piece in range(pieces):
        if slots > 1:
            target = slot ^ piece
            frame, block = target % cores, target // cores
            source, spill = [pick(frame, [one[kind] for one in found]) for kind in range(2)]
            flux, spot = [pick(frame, [pick(block, one[kind]) for one in found]) for kind in range(2, 4)]
            field, extra = fields[piece], extras[piece]
        else:
            frame, block = piece % cores, piece // cores
            source, spill, flux, spot = found[frame]
            flux, spot = flux[block], spot[block]
            field, extra = fields[0].at[piece], extras[0].at[piece]
        for block in range(blocks):
            field[block * stripe : (block + 1) * stripe, :] = source[:, block * SUBN : (block + 1) * SUBN]
        field[blocks * stripe :, :] = spill
        extra[:stripe, :] = flux
        extra[stripe:, :] = spot


def pieces_of(refs, slots, count, mine, order):
    if slots > 1:
        return [(mine ^ step, ref) for step, ref in zip((0,) + tuple(order), refs)]
    return [(step, refs[0].at[step]) for step in range(count)]


def back_of(back, side, tiles):
    depth = tiles * LANES
    start = pl.multiple_of(side * (2 * depth), LANES)
    return back[pl.ds(start, depth), :], back[pl.ds(start + depth, depth), :]


def rims_kernel(sizes, *refs):
    stripe, pieces, blocks, cores, rows = sizes
    width = blocks * SUBN
    slots = pieces if swapped(pieces) else 1
    outs = rows if swapped(rows) else 1
    fields, refs = refs[:slots], refs[slots:]
    basis, back, left, real = refs[:4]
    sent, near, lined = refs[4 : 4 + outs], refs[4 + outs + 1], refs[4 + outs + 2]
    spectrum = refs[4 + outs]
    tiles = padded(blocks) // LANES
    mine = lax.axis_index("row")
    side = lax.axis_index("col")
    slot = side * cores + lax.axis_index("sub")
    arranged = pieces_of(fields, slots, pieces, slot, ORDER.get(pieces))
    lined[SUBN:, :] = jnp.zeros((16, lined.shape[1]), F32)
    for place, field in arranged:
        for block in range(blocks):
            where = pl.ds(pl.multiple_of(place * stripe, 8), stripe)
            lined[where, block * SUBN : (block + 1) * SUBN] = field[block * stripe : (block + 1) * stripe, :]
    first = iota((8, LANES), 0) == 0
    for place, field in arranged:
        head = pl.ds(pl.multiple_of((place + 1) * stripe, 8), 8)
        for block in range(blocks):
            cut = slice(block * SUBN, (block + 1) * SUBN)
            last = field[blocks * stripe + block : blocks * stripe + block + 1, :]
            lined[head, cut] = lined[head, cut] + jnp.where(first, last, 0.0)
    source = lined[...]
    across = dot_three(halves(source), (basis[:width, :], basis[width:, :]))
    driven = dot_stacked(left[:WIN, :], across)
    response = driven * real[:WIN, :]
    spectrum[...] = response
    edges = [dot_stacked(left[WIN : WIN + 16, :], response)]
    for place, start, count in ((WIN, 0, 8), (WIN + 8 * 16, SUBN - 8, 9)):
        total = across[start : start + 1] * real[place : place + 16, :]
        for step in range(1, count):
            table = real[place + 16 * step : place + 16 * step + 16, :]
            total = total + across[start + step : start + step + 1] * table
        edges.append(total)
    rims = dot_three(halves(jnp.concatenate(edges, 0)), back_of(back, side, tiles))
    near[:8, :] = jnp.where(mine > 0, rims[24:32], 0.0)
    near[8:, :] = jnp.where(mine < rows - 1, rims[32:40], 0.0)
    base = 8 * tiles
    tail = sent[0].shape[-2] - base - 8
    total = jnp.sum(source[:SUBN], 0, keepdims=True)
    place = iota((tail, LANES), 0)
    sums = jnp.zeros((tail, LANES), F32)
    for block in range(blocks):
        cut = slice(block * SUBN, (block + 1) * SUBN)
        sums = jnp.where(place == block, total[:, cut], sums)
        sums = jnp.where(place == blocks + block, source[SUBN : SUBN + 1, cut], sums)
    for tile in range(tiles):
        cut = slice(tile * LANES, (tile + 1) * LANES)
        sums = jnp.where(place == 2 * blocks + tile, across[SUBN : SUBN + 1, cut], sums)
    for target, piece in pieces_of(sent, outs, rows, mine, range(1, rows)):
        ahead = target - mine
        rim = jnp.where(ahead == -1, rims[:8], 0.0)
        rim = jnp.where(ahead == 1, rims[8:16], rim)
        rim = jnp.where(ahead == -2, rims[16:24], rim)
        rim = jnp.where(ahead == 2, rims[40:], rim)
        for tile in range(tiles):
            cut = slice(tile * LANES, (tile + 1) * LANES)
            line = jnp.where(ahead == -1, across[:8, cut], across[SUBN - 8 : SUBN, cut])
            piece[8 * tile : 8 * tile + 8, :] = line
        piece[base : base + 8, :] = rim
        piece[base + 8 :, :] = sums


def outputs_kernel(sizes, *refs):
    stripe, pieces, blocks, cores, rows = sizes
    slots = pieces if swapped(pieces) else 1
    extras, (mean_flux, spot_size) = refs[:slots], refs[slots:]
    slot = lax.axis_index("col") * cores + lax.axis_index("sub")
    for place, extra in pieces_of(extras, slots, pieces, slot, ORDER.get(pieces)):
        where = pl.ds(pl.multiple_of(place * stripe, 8), stripe)
        mean_flux[0, where, :] = extra[:stripe, :]
        spot_size[0, where, :] = extra[stripe:, :]


def phase_kernel(sizes, *refs):
    stripe, pieces, blocks, cores, rows = sizes
    slots = pieces if swapped(pieces) else 1
    ins = rows if swapped(rows) else 1
    received, refs = refs[:ins], refs[ins:]
    spectrum, near, back, left, real = refs[:5]
    phase = refs[5]
    tiles = padded(blocks) // LANES
    mine = lax.axis_index("row")
    side = lax.axis_index("col")
    base = 8 * tiles
    tail = received[0].shape[-2] - base - 8
    arranged = pieces_of(received, ins, rows, mine, ORDER.get(rows))

    def of_row(row, where):
        if ins == 1:
            inside = jnp.logical_and(row >= 0, row < rows)
            return jnp.where(inside, received[0][jnp.clip(row, 0, rows - 1), where, :], 0.0)
        total = jnp.zeros((where.stop - where.start, LANES), F32)
        for origin, piece in arranged[1:]:
            total = jnp.where(origin == row, piece[where, :], total)
        return total

    above = of_row(mine - 1, slice(0, received[0].shape[-2]))
    below = of_row(mine + 1, slice(0, base + 8))
    first = iota((8, LANES), 0) == 0
    top, bottom, spilt = [], [], []
    empty = [jnp.zeros((8, LANES), F32)] * tiles
    for tile in range(tiles):
        top.append(above[8 * tile : 8 * tile + 8])
        bottom.append(below[8 * tile : 8 * tile + 8])
        start = base + 8 + 2 * blocks + tile
        spilt.append(jnp.where(first, above[start : start + 1], 0.0))
    across = jnp.concatenate(
        [jnp.concatenate(part, 1) for part in (top, spilt, bottom, empty)], 0
    )
    halo = left[WIN + 16 + SUBN :, : 3 * across.shape[0]]
    driven = dot_stacked(halo, across)
    response = spectrum[...] + driven * real[:WIN, :]
    reach = dot_three(halves(response), back_of(back, side, tiles))
    solved = dot_stacked(left[WIN + 16 : WIN + 16 + SUBN, :], reach)
    coarse = WIN + 17 * 16
    weighted = jnp.zeros((tail, real.shape[1]), F32)
    for origin, piece in arranged:
        count = jnp.sum(piece[base + 8 :, :], 1, keepdims=True)
        weighted = weighted + count * real[pl.ds(pl.multiple_of(coarse + origin * tail, 8), tail), :]
    own = iota(weighted.shape, 1) == mine * blocks + side
    level = jnp.sum(jnp.where(own, weighted, 0.0), keepdims=True)
    solved = solved + level
    rim = slice(base, base + 8)
    head = near[:8, :] + above[rim] + of_row(mine - 2, rim)
    foot = near[8:, :] + below[rim] + of_row(mine + 2, rim)
    phase[0, :8, :] = solved[:8] + head
    phase[0, 8 : SUBN - 8, :] = solved[8 : SUBN - 8]
    phase[0, SUBN - 8 :, :] = solved[SUBN - 8 :] + foot


def coarse_table(blocks_down, blocks_across, tail):
    inverse = coarse_inverse(blocks_down, blocks_across)
    number = blocks_down * blocks_across
    lanes = -(-number // LANES) * LANES
    table = np.zeros((blocks_down, tail, lanes), np.float32)
    for row in range(blocks_down):
        for block in range(blocks_across):
            table[row, block, :number] = inverse[row * blocks_across + block]
            if row + 1 < blocks_down:
                table[row, blocks_across + block, :number] = inverse[(row + 1) * blocks_across + block]
    return table


def in_vmem(count):
    return [pl.BlockSpec(memory_space=pltpu.VMEM)] * count


PARAMS = pltpu.CompilerParams(vmem_limit_bytes=48 * 1024 * 1024)


def body(pixels):
    frames, pixel_rows, pixel_cols = pixels.shape
    stripe = pixel_rows // PIX
    width = pixel_cols // PIX
    rows = lax.axis_size("row")
    blocks = lax.axis_size("col")
    cores = lax.axis_size("sub")
    pieces = blocks * cores
    assert frames == cores and width == blocks * SUBN and stripe * pieces == SUBN

    field_shapes = piece_shapes(pieces, (blocks * stripe + spill_rows(blocks), LANES))
    extra_shapes = piece_shapes(pieces, (2 * stripe, SUBN))
    made = pl.pallas_call(
        functools.partial(moments_kernel, (frames, stripe, blocks, cores, rows * pieces)),
        out_shape=field_shapes + extra_shapes,
        in_specs=[pl.BlockSpec(memory_space=pltpu.HBM)],
        out_specs=in_vmem(len(field_shapes + extra_shapes)),
        scratch_shapes=[
            pltpu.VMEM((frames, pixel_rows, pixel_cols), BF16),
            pltpu.SemaphoreType.DMA((frames, blocks)),
        ],
        compiler_params=PARAMS,
        name="moments",
    )(pltpu.with_memory_space_constraint(pixels, pltpu.HBM))
    fields = exchange(made[: len(field_shapes)], ("col", "sub"), pieces)
    extras = exchange(made[len(field_shapes) :], ("col", "sub"), pieces)

    vectors, scale = sine_basis()
    basis = column_basis(blocks)
    full = padded(blocks)
    tiles = full // LANES
    tail = -(-(2 * blocks + tiles) // 8) * 8
    height = 8 * tiles + 8 + tail
    halo = np.zeros((WIN, 24))
    halo[:, :9] = vectors[:, :9]
    halo[:, 16:] = vectors[:, WIN - 8 :]
    lefts = [
        stacked_left(vectors[:, MARGIN:], WIN),
        stacked_left(np.concatenate([vectors[:8], vectors[WIN - 8 :]], 0), WIN),
        stacked_left(vectors[MARGIN : MARGIN + SUBN], WIN),
        np.pad(stacked_left(halo, 32), ((0, 0), (0, 3 * WIN - 96))),
    ]
    back = constant_pair(basis.T.reshape(full, blocks, SUBN).transpose(1, 0, 2))
    tables = [widened(table, blocks).reshape(-1, full) for table in (scale,) + edge_tables()]
    coarse = coarse_table(rows, blocks, tail)
    tables.append(np.pad(coarse, ((0, 0), (0, 0), (0, full - coarse.shape[2]))).reshape(-1, full))
    wide = jnp.asarray(np.concatenate(constant_pair(basis), 0))
    back = jnp.asarray(np.concatenate(back, 1).reshape(-1, SUBN))
    left = jnp.asarray(np.concatenate(lefts, 0))
    real = jnp.asarray(np.concatenate(tables, 0).astype(np.float32))

    row_shapes = piece_shapes(rows, (height, LANES))
    sizes = (stripe, pieces, blocks, cores, rows)
    *sent, spectrum, near = pl.pallas_call(
        functools.partial(rims_kernel, sizes),
        out_shape=row_shapes
        + [jax.ShapeDtypeStruct((WIN, full), F32), jax.ShapeDtypeStruct((16, SUBN), F32)],
        in_specs=in_vmem(len(fields) + 4),
        out_specs=in_vmem(len(row_shapes) + 2),
        scratch_shapes=[pltpu.VMEM((SUBN + 16, width), F32)],
        compiler_params=PARAMS,
        name="rims",
    )(*fields, wide, back, left, real)
    received = exchange(sent, ("row",), rows)

    mean_flux, spot_size = pl.pallas_call(
        functools.partial(outputs_kernel, sizes),
        out_shape=[jax.ShapeDtypeStruct((1, SUBN, SUBN), F32)] * 2,
        in_specs=in_vmem(len(extras)),
        out_specs=in_vmem(2),
        compiler_params=PARAMS,
        name="outputs",
    )(*extras)
    phase = pl.pallas_call(
        functools.partial(phase_kernel, sizes),
        out_shape=jax.ShapeDtypeStruct((1, SUBN, SUBN), F32),
        in_specs=in_vmem(len(received) + 5),
        out_specs=pl.BlockSpec(memory_space=pltpu.VMEM),
        compiler_params=PARAMS,
        name="phase",
    )(*received, spectrum, near, back, left, real)
    return phase, mean_flux, spot_size


def solution(mesh):
    placed = P(("groups", "sub"), "row", "col")
    return jax.shard_map(
        body,
        mesh=mesh,
        in_specs=(P("groups", ("row", "col", "sub"), None),),
        out_specs=(placed, placed, placed),
        check_vma=False,
    )
```

```python
import functools
import math

import jax
import jax.numpy as jnp
import numpy as np
from jax import lax
from jax.experimental import pallas as pl
from jax.experimental.pallas import tpu as pltpu
from jax.sharding import PartitionSpec as P

PIX = 8
SUBN = 128
MARGIN = 8
WIN = SUBN + 2 * MARGIN
CHUNK = 256
LANES = 128
GROUP = CHUNK // PIX
DAMPING = 2e-05
F32 = jnp.float32
BF16 = jnp.bfloat16


def constant_pair(values):
    high = np.asarray(values).astype(jnp.bfloat16)
    low = (values - high.astype(np.float64)).astype(jnp.bfloat16)
    return high, low


def sine_basis():
    order = np.arange(1, WIN + 1, dtype=np.float64)
    vectors = np.sqrt(2.0 / (WIN + 1)) * np.sin(math.pi * order[:, None] * order[None, :] / (WIN + 1))
    spectrum = 2.0 - 2.0 * np.cos(math.pi * order / (WIN + 1))
    return vectors, 1.0 / (spectrum[:, None] + spectrum[None, :] + DAMPING)


def padded(blocks):
    return -(-blocks * WIN // LANES) * LANES


def column_basis(blocks):
    vectors, _ = sine_basis()
    table = np.zeros((blocks * SUBN, padded(blocks)))
    for block in range(blocks):
        low = max(block * SUBN - MARGIN, 0)
        high = min((block + 1) * SUBN + MARGIN, blocks * SUBN)
        start = low - (block * SUBN - MARGIN)
        table[low:high, block * WIN : (block + 1) * WIN] = vectors[start : start + high - low]
    return table


def widened(table, blocks):
    wide = np.zeros(table.shape[:-1] + (padded(blocks),), np.float32)
    wide[..., : blocks * WIN] = np.tile(table, (1,) * (table.ndim - 1) + (blocks,))
    return wide


def edge_tables():
    vectors, scale = sine_basis()
    ends = np.concatenate([vectors[:8], vectors[WIN - 8 :]], 0)
    def driven_by(rows):
        return np.einsum("oa,ai,ab->iob", ends, vectors[:, rows], scale)
    return driven_by(slice(WIN - 8, WIN)), driven_by(slice(0, 9))


def coarse_inverse(blocks_down, blocks_across):
    number = blocks_down * blocks_across
    row, col = np.divmod(np.arange(number), blocks_across)
    apart = np.abs(row[:, None] - row[None, :]) + np.abs(col[:, None] - col[None, :])
    touching = (apart == 1).astype(np.float64)
    laplace = np.diag(touching.sum(1)) - touching
    return np.linalg.inv(SUBN * laplace + DAMPING * SUBN * SUBN * np.eye(number))


def halves(values):
    high = values.astype(BF16)
    return high, (values - high.astype(F32)).astype(BF16)


def dot(left, right):
    return jnp.dot(left, right, preferred_element_type=F32)


def dot_three(left, right):
    return dot(left[0], right[0]) + (dot(left[0], right[1]) + dot(left[1], right[0]))


def stacked_left(values, depth):
    wide = np.zeros((values.shape[0], depth))
    wide[:, : values.shape[1]] = values
    high = wide.astype(jnp.bfloat16)
    low = (wide - high.astype(np.float64)).astype(jnp.bfloat16)
    return np.concatenate([high, high, low], 1)


def dot_stacked(left, right):
    high, low = halves(right)
    return dot(left, jnp.concatenate([high, low, high], 0))


def iota(shape, axis):
    return lax.broadcasted_iota(jnp.int32, shape, axis)


def power(offset, kind):
    return jnp.where(kind == 0, 1.0, jnp.where(kind == 1, offset, offset * offset))


def offset_of(place):
    return (place % PIX).astype(F32) - (PIX - 1) / 2.0


def row_moments(stripe):
    shape = (3 * stripe, stripe * PIX)
    row, place = iota(shape, 0), iota(shape, 1)
    hit = place // PIX == row % stripe
    return jnp.where(hit, power(offset_of(place), row // stripe), 0.0).astype(BF16)


def column_moments(chunk):
    places = LANES // GROUP
    shape = (CHUNK, LANES)
    place, lane = iota(shape, 0), iota(shape, 1)
    kind = (lane // GROUP + (places - chunk)) % places
    hit = jnp.logical_and(place // PIX == lane % GROUP, kind < 3)
    return jnp.where(hit, power(offset_of(place), kind), 0.0).astype(BF16)


ORDER = {1: (), 2: (1,), 4: (2, 3, 1)}
CELL_ORDER = {1: (), 2: (1,), 4: (2, 1, 3)}


def swapped(count):
    return count in ORDER


def exchange(pieces, axes, count, orders):
    if not swapped(count):
        return [lax.all_to_all(pieces[0], axes, split_axis=0, concat_axis=0, tiled=True)]
    return [pieces[0]] + [
        lax.ppermute(pieces[k], axes, [(i, i ^ k) for i in range(count)]) for k in orders[count]
    ]


def piece_shapes(count, shape):
    if swapped(count):
        return [jax.ShapeDtypeStruct(shape, F32)] * count
    return [jax.ShapeDtypeStruct((count,) + shape, F32)]


def pick(index, values):
    total = values[-1]
    for step in range(len(values) - 1):
        total = jnp.where(index == step, values[step], total)
    return total


def spill_rows(blocks):
    return -(-blocks // 8) * 8


def moments_kernel(sizes, pixels, *refs):
    frames, stripe, blocks, cores, stripes = sizes
    pieces = blocks * cores
    slots = pieces if swapped(pieces) else 1
    fields, extras = refs[:slots], refs[slots : 2 * slots]
    held, arrived = refs[2 * slots :]
    width = blocks * SUBN
    places = LANES // GROUP
    span = LANES * PIX

    def copy(frame, part):
        where = (frame, slice(None), pl.ds(part * span, span))
        return pltpu.make_async_copy(pixels.at[where], held.at[where], arrived.at[frame, part])

    for frame in range(frames):
        for part in range(blocks):
            copy(frame, part).start()
    row_table = row_moments(stripe)
    col_tables = [column_moments(chunk) for chunk in range(places)]
    slot = lax.axis_index("col") * cores + lax.axis_index("sub")
    position = lax.axis_index("row") * pieces + slot
    group = iota((stripe, LANES), 1) // GROUP

    def gather(pieces, kind):
        total = pieces[-1]
        for chunk in range(places - 1):
            total = jnp.where(group == (kind + chunk) % places, pieces[chunk], total)
        return pltpu.roll(total, LANES - GROUP * kind, 1) if kind else total

    row = iota((stripe, width), 0)
    column = iota((stripe, width), 1)

    def columns_of(lines):
        high, low = halves(lines)
        pieces = []
        for chunk in range(places):
            cut = slice(chunk * CHUNK, (chunk + 1) * CHUNK)
            weights = col_tables[chunk]
            pieces.append(dot(high[:, cut], weights) + dot(low[:, cut], weights))
        plain = [piece[:stripe] for piece in pieces]
        tilted = [piece[stripe : 2 * stripe] for piece in pieces]
        bent = [piece[2 * stripe :] for piece in pieces]
        return gather(plain, 0), gather(plain, 1), gather(tilted, 0), gather(plain, 2) + gather(bent, 0)

    def finish(frame, parts):
        intensity, moment_x, moment_y, moment_two = [jnp.concatenate(kind, 1) for kind in zip(*parts)]
        inverse = 1.0 / intensity
        slope_x = moment_x * inverse
        slope_y = moment_y * inverse
        spot_size = moment_two * inverse - slope_x * slope_x - slope_y * slope_y
        mean_flux = intensity * (1.0 / (PIX * PIX))
        flow_x = jnp.where(column < width - 1, slope_x, 0.0)
        flow_y = jnp.where(position * stripe + row < stripes * stripe - 1, slope_y, 0.0)
        left = jnp.where(column > 0, pltpu.roll(flow_x, 1, 1), 0.0)
        above = pltpu.roll(flow_y, 1, 0)
        source = left - flow_x + jnp.where(row > 0, above, 0.0) - flow_y
        spill = jnp.zeros((spill_rows(blocks), LANES), F32)
        spot_row = iota(spill.shape, 0)
        for block in range(blocks):
            last = flow_y[stripe - 1 :, block * SUBN : (block + 1) * SUBN]
            spill = jnp.where(spot_row == block, last, spill)
        fluxes = [mean_flux[:, block * SUBN : (block + 1) * SUBN] for block in range(blocks)]
        spots = [spot_size[:, block * SUBN : (block + 1) * SUBN] for block in range(blocks)]
        return source, spill, fluxes, spots

    def lines_of(frame):
        for part in range(blocks):
            copy(frame, part).wait()
        return [dot(row_table, held[frame, :, pl.ds(part * span, span)]) for part in range(blocks)]

    lines = [lines_of(frame) for frame in range(frames)]
    found = [finish(frame, [columns_of(part) for part in lines[frame]]) for frame in range(frames)]
    for piece in range(pieces):
        if slots > 1:
            target = slot ^ piece
            frame, block = target % cores, target // cores
            source, spill = [pick(frame, [one[kind] for one in found]) for kind in range(2)]
            flux, spot = [pick(frame, [pick(block, one[kind]) for one in found]) for kind in range(2, 4)]
            field, extra = fields[piece], extras[piece]
        else:
            frame, block = piece % cores, piece // cores
            source, spill, flux, spot = found[frame]
            flux, spot = flux[block], spot[block]
            field, extra = fields[0].at[piece], extras[0].at[piece]
        for block in range(blocks):
            field[block * stripe : (block + 1) * stripe, :] = source[:, block * SUBN : (block + 1) * SUBN]
        field[blocks * stripe :, :] = spill
        extra[:stripe, :] = flux
        extra[stripe:, :] = spot


def pieces_of(refs, slots, count, mine, order):
    if slots > 1:
        return [(mine ^ step, ref) for step, ref in zip((0,) + tuple(order), refs)]
    return [(step, refs[0].at[step]) for step in range(count)]


def back_of(back, side, tiles):
    depth = tiles * LANES
    start = pl.multiple_of(side * (2 * depth), LANES)
    return back[pl.ds(start, depth), :], back[pl.ds(start + depth, depth), :]


def rims_kernel(sizes, *refs):
    stripe, pieces, blocks, cores, rows = sizes
    width = blocks * SUBN
    slots = pieces if swapped(pieces) else 1
    outs = rows if swapped(rows) else 1
    fields, refs = refs[:slots], refs[slots:]
    basis, back, left, real = refs[:4]
    sent, near, lined = refs[4 : 4 + outs], refs[4 + outs + 1], refs[4 + outs + 2]
    spectrum = refs[4 + outs]
    tiles = padded(blocks) // LANES
    mine = lax.axis_index("row")
    side = lax.axis_index("col")
    slot = side * cores + lax.axis_index("sub")
    arranged = pieces_of(fields, slots, pieces, slot, CELL_ORDER.get(pieces))
    lined[SUBN:, :] = jnp.zeros((16, lined.shape[1]), F32)
    for place, field in arranged:
        for block in range(blocks):
            where = pl.ds(pl.multiple_of(place * stripe, 8), stripe)
            lined[where, block * SUBN : (block + 1) * SUBN] = field[block * stripe : (block + 1) * stripe, :]
    first = iota((8, LANES), 0) == 0
    for place, field in arranged:
        head = pl.ds(pl.multiple_of((place + 1) * stripe, 8), 8)
        for block in range(blocks):
            cut = slice(block * SUBN, (block + 1) * SUBN)
            last = field[blocks * stripe + block : blocks * stripe + block + 1, :]
            lined[head, cut] = lined[head, cut] + jnp.where(first, last, 0.0)
    source = lined[...]
    across = dot_three(halves(source), (basis[:width, :], basis[width:, :]))
    driven = dot_stacked(left[:WIN, :], across)
    response = driven * real[:WIN, :]
    spectrum[...] = response
    edges = [dot_stacked(left[WIN : WIN + 16, :], response)]
    for place, start, count in ((WIN, 0, 8), (WIN + 8 * 16, SUBN - 8, 9)):
        total = across[start : start + 1] * real[place : place + 16, :]
        for step in range(1, count):
            table = real[place + 16 * step : place + 16 * step + 16, :]
            total = total + across[start + step : start + step + 1] * table
        edges.append(total)
    rims = dot_three(halves(jnp.concatenate(edges, 0)), back_of(back, side, tiles))
    near[:8, :] = jnp.where(mine > 0, rims[24:32], 0.0)
    near[8:, :] = jnp.where(mine < rows - 1, rims[32:40], 0.0)
    base = 8 * tiles
    tail = sent[0].shape[-2] - base - 8
    total = jnp.sum(source[:SUBN], 0, keepdims=True)
    place = iota((tail, LANES), 0)
    sums = jnp.zeros((tail, LANES), F32)
    for block in range(blocks):
        cut = slice(block * SUBN, (block + 1) * SUBN)
        sums = jnp.where(place == block, total[:, cut], sums)
        sums = jnp.where(place == blocks + block, source[SUBN : SUBN + 1, cut], sums)
    for tile in range(tiles):
        cut = slice(tile * LANES, (tile + 1) * LANES)
        sums = jnp.where(place == 2 * blocks + tile, across[SUBN : SUBN + 1, cut], sums)
    for target, piece in pieces_of(sent, outs, rows, mine, range(1, rows)):
        ahead = target - mine
        rim = jnp.where(ahead == -1, rims[:8], 0.0)
        rim = jnp.where(ahead == 1, rims[8:16], rim)
        rim = jnp.where(ahead == -2, rims[16:24], rim)
        rim = jnp.where(ahead == 2, rims[40:], rim)
        for tile in range(tiles):
            cut = slice(tile * LANES, (tile + 1) * LANES)
            line = jnp.where(ahead == -1, across[:8, cut], across[SUBN - 8 : SUBN, cut])
            piece[8 * tile : 8 * tile + 8, :] = line
        piece[base : base + 8, :] = rim
        piece[base + 8 :, :] = sums


def outputs_kernel(sizes, *refs):
    stripe, pieces, blocks, cores, rows = sizes
    slots = pieces if swapped(pieces) else 1
    extras, (mean_flux, spot_size) = refs[:slots], refs[slots:]
    slot = lax.axis_index("col") * cores + lax.axis_index("sub")
    for place, extra in pieces_of(extras, slots, pieces, slot, CELL_ORDER.get(pieces)):
        where = pl.ds(pl.multiple_of(place * stripe, 8), stripe)
        mean_flux[0, where, :] = extra[:stripe, :]
        spot_size[0, where, :] = extra[stripe:, :]


def phase_kernel(sizes, *refs):
    stripe, pieces, blocks, cores, rows = sizes
    slots = pieces if swapped(pieces) else 1
    ins = rows if swapped(rows) else 1
    received, refs = refs[:ins], refs[ins:]
    spectrum, near, back, left, real = refs[:5]
    phase = refs[5]
    tiles = padded(blocks) // LANES
    mine = lax.axis_index("row")
    side = lax.axis_index("col")
    base = 8 * tiles
    tail = received[0].shape[-2] - base - 8
    arranged = pieces_of(received, ins, rows, mine, ORDER.get(rows))

    def of_row(row, where):
        if ins == 1:
            inside = jnp.logical_and(row >= 0, row < rows)
            return jnp.where(inside, received[0][jnp.clip(row, 0, rows - 1), where, :], 0.0)
        total = jnp.zeros((where.stop - where.start, LANES), F32)
        for origin, piece in arranged[1:]:
            total = jnp.where(origin == row, piece[where, :], total)
        return total

    above = of_row(mine - 1, slice(0, received[0].shape[-2]))
    below = of_row(mine + 1, slice(0, base + 8))
    first = iota((8, LANES), 0) == 0
    top, bottom, spilt = [], [], []
    empty = [jnp.zeros((8, LANES), F32)] * tiles
    for tile in range(tiles):
        top.append(above[8 * tile : 8 * tile + 8])
        bottom.append(below[8 * tile : 8 * tile + 8])
        start = base + 8 + 2 * blocks + tile
        spilt.append(jnp.where(first, above[start : start + 1], 0.0))
    across = jnp.concatenate(
        [jnp.concatenate(part, 1) for part in (top, spilt, bottom, empty)], 0
    )
    halo = left[WIN + 16 + SUBN :, : 3 * across.shape[0]]
    driven = dot_stacked(halo, across)
    response = spectrum[...] + driven * real[:WIN, :]
    reach = dot_three(halves(response), back_of(back, side, tiles))
    solved = dot_stacked(left[WIN + 16 : WIN + 16 + SUBN, :], reach)
    coarse = WIN + 17 * 16
    weighted = jnp.zeros((tail, real.shape[1]), F32)
    for origin, piece in arranged:
        count = jnp.sum(piece[base + 8 :, :], 1, keepdims=True)
        weighted = weighted + count * real[pl.ds(pl.multiple_of(coarse + origin * tail, 8), tail), :]
    own = iota(weighted.shape, 1) == mine * blocks + side
    level = jnp.sum(jnp.where(own, weighted, 0.0), keepdims=True)
    solved = solved + level
    rim = slice(base, base + 8)
    head = near[:8, :] + above[rim] + of_row(mine - 2, rim)
    foot = near[8:, :] + below[rim] + of_row(mine + 2, rim)
    phase[0, :8, :] = solved[:8] + head
    phase[0, 8 : SUBN - 8, :] = solved[8 : SUBN - 8]
    phase[0, SUBN - 8 :, :] = solved[SUBN - 8 :] + foot


def coarse_table(blocks_down, blocks_across, tail):
    inverse = coarse_inverse(blocks_down, blocks_across)
    number = blocks_down * blocks_across
    lanes = -(-number // LANES) * LANES
    table = np.zeros((blocks_down, tail, lanes), np.float32)
    for row in range(blocks_down):
        for block in range(blocks_across):
            table[row, block, :number] = inverse[row * blocks_across + block]
            if row + 1 < blocks_down:
                table[row, blocks_across + block, :number] = inverse[(row + 1) * blocks_across + block]
    return table


def in_vmem(count):
    return [pl.BlockSpec(memory_space=pltpu.VMEM)] * count


PARAMS = pltpu.CompilerParams(vmem_limit_bytes=48 * 1024 * 1024)


def body(pixels):
    frames, pixel_rows, pixel_cols = pixels.shape
    stripe = pixel_rows // PIX
    width = pixel_cols // PIX
    rows = lax.axis_size("row")
    blocks = lax.axis_size("col")
    cores = lax.axis_size("sub")
    pieces = blocks * cores
    assert frames == cores and width == blocks * SUBN and stripe * pieces == SUBN

    field_shapes = piece_shapes(pieces, (blocks * stripe + spill_rows(blocks), LANES))
    extra_shapes = piece_shapes(pieces, (2 * stripe, SUBN))
    made = pl.pallas_call(
        functools.partial(moments_kernel, (frames, stripe, blocks, cores, rows * pieces)),
        out_shape=field_shapes + extra_shapes,
        in_specs=[pl.BlockSpec(memory_space=pltpu.HBM)],
        out_specs=in_vmem(len(field_shapes + extra_shapes)),
        scratch_shapes=[
            pltpu.VMEM((frames, pixel_rows, pixel_cols), BF16),
            pltpu.SemaphoreType.DMA((frames, blocks)),
        ],
        compiler_params=PARAMS,
        name="moments",
    )(pltpu.with_memory_space_constraint(pixels, pltpu.HBM))
    fields = exchange(made[: len(field_shapes)], ("col", "sub"), pieces, CELL_ORDER)
    extras = exchange(made[len(field_shapes) :], ("col", "sub"), pieces, CELL_ORDER)

    vectors, scale = sine_basis()
    basis = column_basis(blocks)
    full = padded(blocks)
    tiles = full // LANES
    tail = -(-(2 * blocks + tiles) // 8) * 8
    height = 8 * tiles + 8 + tail
    halo = np.zeros((WIN, 24))
    halo[:, :9] = vectors[:, :9]
    halo[:, 16:] = vectors[:, WIN - 8 :]
    lefts = [
        stacked_left(vectors[:, MARGIN:], WIN),
        stacked_left(np.concatenate([vectors[:8], vectors[WIN - 8 :]], 0), WIN),
        stacked_left(vectors[MARGIN : MARGIN + SUBN], WIN),
        np.pad(stacked_left(halo, 32), ((0, 0), (0, 3 * WIN - 96))),
    ]
    back = constant_pair(basis.T.reshape(full, blocks, SUBN).transpose(1, 0, 2))
    tables = [widened(table, blocks).reshape(-1, full) for table in (scale,) + edge_tables()]
    coarse = coarse_table(rows, blocks, tail)
    tables.append(np.pad(coarse, ((0, 0), (0, 0), (0, full - coarse.shape[2]))).reshape(-1, full))
    wide = jnp.asarray(np.concatenate(constant_pair(basis), 0))
    back = jnp.asarray(np.concatenate(back, 1).reshape(-1, SUBN))
    left = jnp.asarray(np.concatenate(lefts, 0))
    real = jnp.asarray(np.concatenate(tables, 0).astype(np.float32))

    row_shapes = piece_shapes(rows, (height, LANES))
    sizes = (stripe, pieces, blocks, cores, rows)
    *sent, spectrum, near = pl.pallas_call(
        functools.partial(rims_kernel, sizes),
        out_shape=row_shapes
        + [jax.ShapeDtypeStruct((WIN, full), F32), jax.ShapeDtypeStruct((16, SUBN), F32)],
        in_specs=in_vmem(len(fields) + 4),
        out_specs=in_vmem(len(row_shapes) + 2),
        scratch_shapes=[pltpu.VMEM((SUBN + 16, width), F32)],
        compiler_params=PARAMS,
        name="rims",
    )(*fields, wide, back, left, real)
    received = exchange(sent, ("row",), rows, ORDER)

    mean_flux, spot_size = pl.pallas_call(
        functools.partial(outputs_kernel, sizes),
        out_shape=[jax.ShapeDtypeStruct((1, SUBN, SUBN), F32)] * 2,
        in_specs=in_vmem(len(extras)),
        out_specs=in_vmem(2),
        compiler_params=PARAMS,
        name="outputs",
    )(*extras)
    phase = pl.pallas_call(
        functools.partial(phase_kernel, sizes),
        out_shape=jax.ShapeDtypeStruct((1, SUBN, SUBN), F32),
        in_specs=in_vmem(len(received) + 5),
        out_specs=pl.BlockSpec(memory_space=pltpu.VMEM),
        compiler_params=PARAMS,
        name="phase",
    )(*received, spectrum, near, back, left, real)
    return phase, mean_flux, spot_size


def solution(mesh):
    placed = P(("groups", "sub"), "row", "col")
    return jax.shard_map(
        body,
        mesh=mesh,
        in_specs=(P("groups", ("row", "col", "sub"), None),),
        out_specs=(placed, placed, placed),
        check_vma=False,
    )
```

```python
import functools
import math

import jax
import jax.numpy as jnp
import numpy as np
from jax import lax
from jax.experimental import pallas as pl
from jax.experimental.pallas import tpu as pltpu
from jax.sharding import PartitionSpec as P

PIX = 8
SUBN = 128
MARGIN = 8
WIN = SUBN + 2 * MARGIN
CHUNK = 256
LANES = 128
GROUP = CHUNK // PIX
DAMPING = 2e-05
F32 = jnp.float32
BF16 = jnp.bfloat16


def constant_pair(values):
    high = np.asarray(values).astype(jnp.bfloat16)
    low = (values - high.astype(np.float64)).astype(jnp.bfloat16)
    return high, low


def sine_basis():
    order = np.arange(1, WIN + 1, dtype=np.float64)
    vectors = np.sqrt(2.0 / (WIN + 1)) * np.sin(math.pi * order[:, None] * order[None, :] / (WIN + 1))
    spectrum = 2.0 - 2.0 * np.cos(math.pi * order / (WIN + 1))
    return vectors, 1.0 / (spectrum[:, None] + spectrum[None, :] + DAMPING)


def padded(blocks):
    return -(-blocks * WIN // LANES) * LANES


def column_basis(blocks):
    vectors, _ = sine_basis()
    table = np.zeros((blocks * SUBN, padded(blocks)))
    for block in range(blocks):
        low = max(block * SUBN - MARGIN, 0)
        high = min((block + 1) * SUBN + MARGIN, blocks * SUBN)
        start = low - (block * SUBN - MARGIN)
        table[low:high, block * WIN : (block + 1) * WIN] = vectors[start : start + high - low]
    return table


def widened(table, blocks):
    wide = np.zeros(table.shape[:-1] + (padded(blocks),), np.float32)
    wide[..., : blocks * WIN] = np.tile(table, (1,) * (table.ndim - 1) + (blocks,))
    return wide


def edge_tables():
    vectors, scale = sine_basis()
    ends = np.concatenate([vectors[:8], vectors[WIN - 8 :]], 0)
    def driven_by(rows):
        return np.einsum("oa,ai,ab->iob", ends, vectors[:, rows], scale)
    return driven_by(slice(WIN - 8, WIN)), driven_by(slice(0, 9))


def coarse_inverse(blocks_down, blocks_across):
    number = blocks_down * blocks_across
    row, col = np.divmod(np.arange(number), blocks_across)
    apart = np.abs(row[:, None] - row[None, :]) + np.abs(col[:, None] - col[None, :])
    touching = (apart == 1).astype(np.float64)
    laplace = np.diag(touching.sum(1)) - touching
    return np.linalg.inv(SUBN * laplace + DAMPING * SUBN * SUBN * np.eye(number))


def halves(values):
    high = values.astype(BF16)
    return high, (values - high.astype(F32)).astype(BF16)


def dot(left, right):
    return jnp.dot(left, right, preferred_element_type=F32)


def dot_three(left, right):
    return dot(left[0], right[0]) + (dot(left[0], right[1]) + dot(left[1], right[0]))


def stacked_left(values, depth):
    wide = np.zeros((values.shape[0], depth))
    wide[:, : values.shape[1]] = values
    high = wide.astype(jnp.bfloat16)
    low = (wide - high.astype(np.float64)).astype(jnp.bfloat16)
    return np.concatenate([high, high, low], 1)


def dot_stacked(left, right):
    high, low = halves(right)
    return dot(left, jnp.concatenate([high, low, high], 0))


def iota(shape, axis):
    return lax.broadcasted_iota(jnp.int32, shape, axis)


def power(offset, kind):
    return jnp.where(kind == 0, 1.0, jnp.where(kind == 1, offset, offset * offset))


def offset_of(place):
    return (place % PIX).astype(F32) - (PIX - 1) / 2.0


def row_moments(stripe):
    shape = (3 * stripe, stripe * PIX)
    row, place = iota(shape, 0), iota(shape, 1)
    hit = place // PIX == row % stripe
    return jnp.where(hit, power(offset_of(place), row // stripe), 0.0).astype(BF16)


def column_moments(chunk):
    places = LANES // GROUP
    shape = (CHUNK, LANES)
    place, lane = iota(shape, 0), iota(shape, 1)
    kind = (lane // GROUP + (places - chunk)) % places
    hit = jnp.logical_and(place // PIX == lane % GROUP, kind < 3)
    return jnp.where(hit, power(offset_of(place), kind), 0.0).astype(BF16)


ORDER = {1: (), 2: (1,), 4: (2, 3, 1)}
CELL_ORDER = {1: (), 2: (1,), 4: (2, 1, 3)}


def swapped(count):
    return count in ORDER


def exchange(pieces, axes, count, orders):
    if not swapped(count):
        return [lax.all_to_all(pieces[0], axes, split_axis=0, concat_axis=0, tiled=True)]
    return [pieces[0]] + [
        lax.ppermute(pieces[k], axes, [(i, i ^ k) for i in range(count)]) for k in orders[count]
    ]


def piece_shapes(count, shape):
    if swapped(count):
        return [jax.ShapeDtypeStruct(shape, F32)] * count
    return [jax.ShapeDtypeStruct((count,) + shape, F32)]


def pick(index, values):
    total = values[-1]
    for step in range(len(values) - 1):
        total = jnp.where(index == step, values[step], total)
    return total


def spill_rows(blocks):
    return -(-blocks // 8) * 8


def moments_kernel(sizes, pixels, *refs):
    frames, stripe, blocks, cores, stripes = sizes
    pieces = blocks * cores
    slots = pieces if swapped(pieces) else 1
    fields, extras = refs[:slots], refs[slots : 2 * slots]
    held, arrived = refs[2 * slots :]
    width = blocks * SUBN
    places = LANES // GROUP
    span = LANES * PIX

    def copy(frame, part):
        where = (frame, slice(None), pl.ds(part * span, span))
        return pltpu.make_async_copy(pixels.at[where], held.at[where], arrived.at[frame, part])

    for frame in range(frames):
        for part in range(blocks):
            copy(frame, part).start()
    row_table = row_moments(stripe)
    col_tables = [column_moments(chunk) for chunk in range(places)]
    slot = lax.axis_index("col") * cores + lax.axis_index("sub")
    position = lax.axis_index("row") * pieces + slot
    group = iota((stripe, LANES), 1) // GROUP

    def gather(pieces, kind):
        total = pieces[-1]
        for chunk in range(places - 1):
            total = jnp.where(group == (kind + chunk) % places, pieces[chunk], total)
        return pltpu.roll(total, LANES - GROUP * kind, 1) if kind else total

    row = iota((stripe, width), 0)
    column = iota((stripe, width), 1)

    def columns_of(lines):
        high, low = halves(lines)
        pieces = []
        for chunk in range(places):
            cut = slice(chunk * CHUNK, (chunk + 1) * CHUNK)
            weights = col_tables[chunk]
            pieces.append(dot(high[:, cut], weights) + dot(low[:, cut], weights))
        plain = [piece[:stripe] for piece in pieces]
        tilted = [piece[stripe : 2 * stripe] for piece in pieces]
        bent = [piece[2 * stripe :] for piece in pieces]
        return gather(plain, 0), gather(plain, 1), gather(tilted, 0), gather(plain, 2) + gather(bent, 0)

    def finish(frame, parts):
        intensity, moment_x, moment_y, moment_two = [jnp.concatenate(kind, 1) for kind in zip(*parts)]
        inverse = 1.0 / intensity
        slope_x = moment_x * inverse
        slope_y = moment_y * inverse
        spot_size = moment_two * inverse - slope_x * slope_x - slope_y * slope_y
        mean_flux = intensity * (1.0 / (PIX * PIX))
        flow_x = jnp.where(column < width - 1, slope_x, 0.0)
        flow_y = jnp.where(position * stripe + row < stripes * stripe - 1, slope_y, 0.0)
        left = jnp.where(column > 0, pltpu.roll(flow_x, 1, 1), 0.0)
        above = pltpu.roll(flow_y, 1, 0)
        source = left - flow_x + jnp.where(row > 0, above, 0.0) - flow_y
        spill = jnp.zeros((spill_rows(blocks), LANES), F32)
        spot_row = iota(spill.shape, 0)
        for block in range(blocks):
            last = flow_y[stripe - 1 :, block * SUBN : (block + 1) * SUBN]
            spill = jnp.where(spot_row == block, last, spill)
        fluxes = [mean_flux[:, block * SUBN : (block + 1) * SUBN] for block in range(blocks)]
        spots = [spot_size[:, block * SUBN : (block + 1) * SUBN] for block in range(blocks)]
        return source, spill, fluxes, spots

    def lines_of(frame):
        for part in range(blocks):
            copy(frame, part).wait()
        return [dot(row_table, held[frame, :, pl.ds(part * span, span)]) for part in range(blocks)]

    lines = [lines_of(frame) for frame in range(frames)]
    found = [finish(frame, [columns_of(part) for part in lines[frame]]) for frame in range(frames)]
    for piece in range(pieces):
        if slots > 1:
            target = slot ^ piece
            frame, block = target % cores, target // cores
            source, spill = [pick(frame, [one[kind] for one in found]) for kind in range(2)]
            flux, spot = [pick(frame, [pick(block, one[kind]) for one in found]) for kind in range(2, 4)]
            field, extra = fields[piece], extras[piece]
        else:
            frame, block = piece % cores, piece // cores
            source, spill, flux, spot = found[frame]
            flux, spot = flux[block], spot[block]
            field, extra = fields[0].at[piece], extras[0].at[piece]
        for block in range(blocks):
            field[block * stripe : (block + 1) * stripe, :] = source[:, block * SUBN : (block + 1) * SUBN]
        field[blocks * stripe :, :] = spill
        extra[:stripe, :] = flux
        extra[stripe:, :] = spot


def pieces_of(refs, slots, count, mine, order):
    if slots > 1:
        return [(mine ^ step, ref) for step, ref in zip((0,) + tuple(order), refs)]
    return [(step, refs[0].at[step]) for step in range(count)]


def tail_rows(blocks):
    return -(-(2 * blocks + padded(blocks) // LANES) // 8) * 8


def back_of(back, side, tiles):
    depth = tiles * LANES
    start = pl.multiple_of(side * (2 * depth), LANES)
    return back[pl.ds(start, depth), :], back[pl.ds(start + depth, depth), :]


def rims_kernel(sizes, *refs):
    stripe, pieces, blocks, cores, rows = sizes
    width = blocks * SUBN
    slots = pieces if swapped(pieces) else 1
    outs = rows if swapped(rows) else 1
    fields, refs = refs[:slots], refs[slots:]
    basis, back, left, real = refs[:4]
    sent, near, lined = refs[4 : 4 + outs], refs[4 + outs + 1], refs[4 + outs + 2]
    spectrum = refs[4 + outs]
    tiles = padded(blocks) // LANES
    mine = lax.axis_index("row")
    side = lax.axis_index("col")
    slot = side * cores + lax.axis_index("sub")
    arranged = pieces_of(fields, slots, pieces, slot, CELL_ORDER.get(pieces))
    lined[SUBN:, :] = jnp.zeros((16, lined.shape[1]), F32)
    for place, field in arranged:
        for block in range(blocks):
            where = pl.ds(pl.multiple_of(place * stripe, 8), stripe)
            lined[where, block * SUBN : (block + 1) * SUBN] = field[block * stripe : (block + 1) * stripe, :]
    first = iota((8, LANES), 0) == 0
    for place, field in arranged:
        head = pl.ds(pl.multiple_of((place + 1) * stripe, 8), 8)
        for block in range(blocks):
            cut = slice(block * SUBN, (block + 1) * SUBN)
            last = field[blocks * stripe + block : blocks * stripe + block + 1, :]
            lined[head, cut] = lined[head, cut] + jnp.where(first, last, 0.0)
    source = lined[...]
    across = dot_three(halves(source), (basis[:width, :], basis[width:, :]))
    driven = dot_stacked(left[:WIN, :], across)
    response = driven * real[:WIN, :]
    spectrum[...] = response
    edges = [dot_stacked(left[WIN : WIN + 16, :], response)]
    for place, start, count in ((WIN, 0, 8), (WIN + 8 * 16, SUBN - 8, 9)):
        total = across[start : start + 1] * real[place : place + 16, :]
        for step in range(1, count):
            table = real[place + 16 * step : place + 16 * step + 16, :]
            total = total + across[start + step : start + step + 1] * table
        edges.append(total)
    rims = dot_three(halves(jnp.concatenate(edges, 0)), back_of(back, side, tiles))
    near[:8, :] = jnp.where(mine > 0, rims[24:32], 0.0)
    near[8:, :] = jnp.where(mine < rows - 1, rims[32:40], 0.0)
    tail = tail_rows(blocks)
    total = jnp.sum(source[:SUBN], 0, keepdims=True)
    place = iota((tail, LANES), 0)
    sums = jnp.zeros((tail, LANES), F32)
    for block in range(blocks):
        cut = slice(block * SUBN, (block + 1) * SUBN)
        sums = jnp.where(place == block, total[:, cut], sums)
        sums = jnp.where(place == blocks + block, source[SUBN : SUBN + 1, cut], sums)
    for tile in range(tiles):
        cut = slice(tile * LANES, (tile + 1) * LANES)
        sums = jnp.where(place == 2 * blocks + tile, across[SUBN : SUBN + 1, cut], sums)
    for target, piece in pieces_of(sent, outs, rows, mine, range(1, rows)):
        ahead = target - mine
        rim = jnp.where(ahead == -1, rims[:8], 0.0)
        rim = jnp.where(ahead == 1, rims[8:16], rim)
        rim = jnp.where(ahead == -2, rims[16:24], rim)
        rim = jnp.where(ahead == 2, rims[40:], rim)
        piece[:8, :] = rim
        piece[8 : 8 + tail, :] = sums
        if piece.shape[-2] == 8 + tail:
            continue
        for tile in range(tiles):
            cut = slice(tile * LANES, (tile + 1) * LANES)
            line = jnp.where(ahead == -1, across[:8, cut], across[SUBN - 8 : SUBN, cut])
            piece[8 + tail + 8 * tile : 16 + tail + 8 * tile, :] = line


def outputs_kernel(sizes, *refs):
    stripe, pieces, blocks, cores, rows = sizes
    slots = pieces if swapped(pieces) else 1
    extras, (mean_flux, spot_size) = refs[:slots], refs[slots:]
    slot = lax.axis_index("col") * cores + lax.axis_index("sub")
    for place, extra in pieces_of(extras, slots, pieces, slot, CELL_ORDER.get(pieces)):
        where = pl.ds(pl.multiple_of(place * stripe, 8), stripe)
        mean_flux[0, where, :] = extra[:stripe, :]
        spot_size[0, where, :] = extra[stripe:, :]


def phase_kernel(sizes, *refs):
    stripe, pieces, blocks, cores, rows = sizes
    slots = pieces if swapped(pieces) else 1
    ins = rows if swapped(rows) else 1
    received, refs = refs[:ins], refs[ins:]
    spectrum, near, back, left, real = refs[:5]
    phase = refs[5]
    tiles = padded(blocks) // LANES
    mine = lax.axis_index("row")
    side = lax.axis_index("col")
    tail = tail_rows(blocks)
    arranged = pieces_of(received, ins, rows, mine, ORDER.get(rows))

    def of_row(row, where):
        if ins == 1:
            inside = jnp.logical_and(row >= 0, row < rows)
            return jnp.where(inside, received[0][jnp.clip(row, 0, rows - 1), where, :], 0.0)
        total = jnp.zeros((where.stop - where.start, LANES), F32)
        for origin, piece in arranged[1:]:
            if piece.shape[-2] < where.stop:
                continue
            total = jnp.where(origin == row, piece[where, :], total)
        return total

    above = of_row(mine - 1, slice(0, 8 + tail + 8 * tiles))
    below = of_row(mine + 1, slice(0, 8 + tail + 8 * tiles))
    first = iota((8, LANES), 0) == 0
    top, bottom, spilt = [], [], []
    empty = [jnp.zeros((8, LANES), F32)] * tiles
    for tile in range(tiles):
        lines = slice(8 + tail + 8 * tile, 16 + tail + 8 * tile)
        top.append(above[lines])
        bottom.append(below[lines])
        start = 8 + 2 * blocks + tile
        spilt.append(jnp.where(first, above[start : start + 1], 0.0))
    across = jnp.concatenate(
        [jnp.concatenate(part, 1) for part in (top, spilt, bottom, empty)], 0
    )
    halo = left[WIN + 16 + SUBN :, : 3 * across.shape[0]]
    driven = dot_stacked(halo, across)
    response = spectrum[...] + driven * real[:WIN, :]
    reach = dot_three(halves(response), back_of(back, side, tiles))
    solved = dot_stacked(left[WIN + 16 : WIN + 16 + SUBN, :], reach)
    coarse = WIN + 17 * 16
    weighted = jnp.zeros((tail, real.shape[1]), F32)
    for origin, piece in arranged:
        count = jnp.sum(piece[8 : 8 + tail, :], 1, keepdims=True)
        weighted = weighted + count * real[pl.ds(pl.multiple_of(coarse + origin * tail, 8), tail), :]
    own = iota(weighted.shape, 1) == mine * blocks + side
    level = jnp.sum(jnp.where(own, weighted, 0.0), keepdims=True)
    solved = solved + level
    rim = slice(0, 8)
    head = near[:8, :] + above[rim] + of_row(mine - 2, rim)
    foot = near[8:, :] + below[rim] + of_row(mine + 2, rim)
    phase[0, :8, :] = solved[:8] + head
    phase[0, 8 : SUBN - 8, :] = solved[8 : SUBN - 8]
    phase[0, SUBN - 8 :, :] = solved[SUBN - 8 :] + foot


def coarse_table(blocks_down, blocks_across, tail):
    inverse = coarse_inverse(blocks_down, blocks_across)
    number = blocks_down * blocks_across
    lanes = -(-number // LANES) * LANES
    table = np.zeros((blocks_down, tail, lanes), np.float32)
    for row in range(blocks_down):
        for block in range(blocks_across):
            table[row, block, :number] = inverse[row * blocks_across + block]
            if row + 1 < blocks_down:
                table[row, blocks_across + block, :number] = inverse[(row + 1) * blocks_across + block]
    return table


def in_vmem(count):
    return [pl.BlockSpec(memory_space=pltpu.VMEM)] * count


PARAMS = pltpu.CompilerParams(vmem_limit_bytes=48 * 1024 * 1024)


def body(pixels):
    frames, pixel_rows, pixel_cols = pixels.shape
    stripe = pixel_rows // PIX
    width = pixel_cols // PIX
    rows = lax.axis_size("row")
    blocks = lax.axis_size("col")
    cores = lax.axis_size("sub")
    pieces = blocks * cores
    assert frames == cores and width == blocks * SUBN and stripe * pieces == SUBN

    field_shapes = piece_shapes(pieces, (blocks * stripe + spill_rows(blocks), LANES))
    extra_shapes = piece_shapes(pieces, (2 * stripe, SUBN))
    made = pl.pallas_call(
        functools.partial(moments_kernel, (frames, stripe, blocks, cores, rows * pieces)),
        out_shape=field_shapes + extra_shapes,
        in_specs=[pl.BlockSpec(memory_space=pltpu.HBM)],
        out_specs=in_vmem(len(field_shapes + extra_shapes)),
        scratch_shapes=[
            pltpu.VMEM((frames, pixel_rows, pixel_cols), BF16),
            pltpu.SemaphoreType.DMA((frames, blocks)),
        ],
        compiler_params=PARAMS,
        name="moments",
    )(pltpu.with_memory_space_constraint(pixels, pltpu.HBM))
    fields = exchange(made[: len(field_shapes)], ("col", "sub"), pieces, CELL_ORDER)
    extras = exchange(made[len(field_shapes) :], ("col", "sub"), pieces, CELL_ORDER)

    vectors, scale = sine_basis()
    basis = column_basis(blocks)
    full = padded(blocks)
    tiles = full // LANES
    tail = tail_rows(blocks)
    short, height = 8 + tail, 8 + tail + 8 * tiles
    halo = np.zeros((WIN, 24))
    halo[:, :9] = vectors[:, :9]
    halo[:, 16:] = vectors[:, WIN - 8 :]
    lefts = [
        stacked_left(vectors[:, MARGIN:], WIN),
        stacked_left(np.concatenate([vectors[:8], vectors[WIN - 8 :]], 0), WIN),
        stacked_left(vectors[MARGIN : MARGIN + SUBN], WIN),
        np.pad(stacked_left(halo, 32), ((0, 0), (0, 3 * WIN - 96))),
    ]
    back = constant_pair(basis.T.reshape(full, blocks, SUBN).transpose(1, 0, 2))
    tables = [widened(table, blocks).reshape(-1, full) for table in (scale,) + edge_tables()]
    coarse = coarse_table(rows, blocks, tail)
    tables.append(np.pad(coarse, ((0, 0), (0, 0), (0, full - coarse.shape[2]))).reshape(-1, full))
    wide = jnp.asarray(np.concatenate(constant_pair(basis), 0))
    back = jnp.asarray(np.concatenate(back, 1).reshape(-1, SUBN))
    left = jnp.asarray(np.concatenate(lefts, 0))
    real = jnp.asarray(np.concatenate(tables, 0).astype(np.float32))

    row_shapes = piece_shapes(rows, (height, LANES))
    if swapped(rows):
        touching = [any(abs((row ^ k) - row) == 1 for row in range(rows)) for k in range(rows)]
        row_shapes = [jax.ShapeDtypeStruct((height if one else short, LANES), F32) for one in touching]
    sizes = (stripe, pieces, blocks, cores, rows)
    *sent, spectrum, near = pl.pallas_call(
        functools.partial(rims_kernel, sizes),
        out_shape=row_shapes
        + [jax.ShapeDtypeStruct((WIN, full), F32), jax.ShapeDtypeStruct((16, SUBN), F32)],
        in_specs=in_vmem(len(fields) + 4),
        out_specs=in_vmem(len(row_shapes) + 2),
        scratch_shapes=[pltpu.VMEM((SUBN + 16, width), F32)],
        compiler_params=PARAMS,
        name="rims",
    )(*fields, wide, back, left, real)
    received = exchange(sent, ("row",), rows, ORDER)

    mean_flux, spot_size = pl.pallas_call(
        functools.partial(outputs_kernel, sizes),
        out_shape=[jax.ShapeDtypeStruct((1, SUBN, SUBN), F32)] * 2,
        in_specs=in_vmem(len(extras)),
        out_specs=in_vmem(2),
        compiler_params=PARAMS,
        name="outputs",
    )(*extras)
    phase = pl.pallas_call(
        functools.partial(phase_kernel, sizes),
        out_shape=jax.ShapeDtypeStruct((1, SUBN, SUBN), F32),
        in_specs=in_vmem(len(received) + 5),
        out_specs=pl.BlockSpec(memory_space=pltpu.VMEM),
        compiler_params=PARAMS,
        name="phase",
    )(*received, spectrum, near, back, left, real)
    return phase, mean_flux, spot_size


def solution(mesh):
    placed = P(("groups", "sub"), "row", "col")
    return jax.shard_map(
        body,
        mesh=mesh,
        in_specs=(P("groups", ("row", "col", "sub"), None),),
        out_specs=(placed, placed, placed),
        check_vma=False,
    )
```

```python
import functools
import math

import jax
import jax.numpy as jnp
import numpy as np
from jax import lax
from jax.experimental import pallas as pl
from jax.experimental.pallas import tpu as pltpu
from jax.sharding import PartitionSpec as P

PIX = 8
SUBN = 128
MARGIN = 8
WIN = SUBN + 2 * MARGIN
CHUNK = 256
LANES = 128
GROUP = CHUNK // PIX
DAMPING = 2e-05
F32 = jnp.float32
BF16 = jnp.bfloat16


def constant_pair(values):
    high = np.asarray(values).astype(jnp.bfloat16)
    low = (values - high.astype(np.float64)).astype(jnp.bfloat16)
    return high, low


def sine_basis():
    order = np.arange(1, WIN + 1, dtype=np.float64)
    vectors = np.sqrt(2.0 / (WIN + 1)) * np.sin(math.pi * order[:, None] * order[None, :] / (WIN + 1))
    spectrum = 2.0 - 2.0 * np.cos(math.pi * order / (WIN + 1))
    return vectors, 1.0 / (spectrum[:, None] + spectrum[None, :] + DAMPING)


def padded(blocks):
    return -(-blocks * WIN // LANES) * LANES


def column_basis(blocks):
    vectors, _ = sine_basis()
    table = np.zeros((blocks * SUBN, padded(blocks)))
    for block in range(blocks):
        low = max(block * SUBN - MARGIN, 0)
        high = min((block + 1) * SUBN + MARGIN, blocks * SUBN)
        start = low - (block * SUBN - MARGIN)
        table[low:high, block * WIN : (block + 1) * WIN] = vectors[start : start + high - low]
    return table


def widened(table, blocks):
    wide = np.zeros(table.shape[:-1] + (padded(blocks),), np.float32)
    wide[..., : blocks * WIN] = np.tile(table, (1,) * (table.ndim - 1) + (blocks,))
    return wide


def edge_tables():
    vectors, scale = sine_basis()
    ends = np.concatenate([vectors[:8], vectors[WIN - 8 :]], 0)
    def driven_by(rows):
        return np.einsum("oa,ai,ab->iob", ends, vectors[:, rows], scale)
    return driven_by(slice(WIN - 8, WIN)), driven_by(slice(0, 9))


def coarse_inverse(blocks_down, blocks_across):
    number = blocks_down * blocks_across
    row, col = np.divmod(np.arange(number), blocks_across)
    apart = np.abs(row[:, None] - row[None, :]) + np.abs(col[:, None] - col[None, :])
    touching = (apart == 1).astype(np.float64)
    laplace = np.diag(touching.sum(1)) - touching
    return np.linalg.inv(SUBN * laplace + DAMPING * SUBN * SUBN * np.eye(number))


def halves(values):
    high = values.astype(BF16)
    return high, (values - high.astype(F32)).astype(BF16)


def dot(left, right):
    return jnp.dot(left, right, preferred_element_type=F32)


def dot_three(left, right):
    return dot(left[0], right[0]) + (dot(left[0], right[1]) + dot(left[1], right[0]))


def stacked_left(values, depth):
    wide = np.zeros((values.shape[0], depth))
    wide[:, : values.shape[1]] = values
    high = wide.astype(jnp.bfloat16)
    low = (wide - high.astype(np.float64)).astype(jnp.bfloat16)
    return np.concatenate([high, high, low], 1)


def dot_stacked(left, right):
    high, low = halves(right)
    return dot(left, jnp.concatenate([high, low, high], 0))


def iota(shape, axis):
    return lax.broadcasted_iota(jnp.int32, shape, axis)


def power(offset, kind):
    return jnp.where(kind == 0, 1.0, jnp.where(kind == 1, offset, offset * offset))


def offset_of(place):
    return (place % PIX).astype(F32) - (PIX - 1) / 2.0


def row_moments(stripe):
    shape = (3 * stripe, stripe * PIX)
    row, place = iota(shape, 0), iota(shape, 1)
    hit = place // PIX == row % stripe
    return jnp.where(hit, power(offset_of(place), row // stripe), 0.0).astype(BF16)


def column_moments(chunk):
    places = LANES // GROUP
    shape = (CHUNK, LANES)
    place, lane = iota(shape, 0), iota(shape, 1)
    kind = (lane // GROUP + (places - chunk)) % places
    hit = jnp.logical_and(place // PIX == lane % GROUP, kind < 3)
    return jnp.where(hit, power(offset_of(place), kind), 0.0).astype(BF16)


ORDER = {1: (), 2: (1,), 4: (3, 1, 2)}
CELL_ORDER = {1: (), 2: (1,), 4: (2, 1, 3)}


def swapped(count):
    return count in ORDER


def exchange(pieces, axes, count, orders):
    if not swapped(count):
        return [lax.all_to_all(pieces[0], axes, split_axis=0, concat_axis=0, tiled=True)]
    return [pieces[0]] + [
        lax.ppermute(pieces[k], axes, [(i, i ^ k) for i in range(count)]) for k in orders[count]
    ]


def piece_shapes(count, shape):
    if swapped(count):
        return [jax.ShapeDtypeStruct(shape, F32)] * count
    return [jax.ShapeDtypeStruct((count,) + shape, F32)]


def pick(index, values):
    total = values[-1]
    for step in range(len(values) - 1):
        total = jnp.where(index == step, values[step], total)
    return total


def spill_rows(blocks):
    return -(-blocks // 8) * 8


def moments_kernel(sizes, pixels, *refs):
    frames, stripe, blocks, cores, stripes = sizes
    pieces = blocks * cores
    slots = pieces if swapped(pieces) else 1
    fields, extras = refs[:slots], refs[slots : 2 * slots]
    held, arrived = refs[2 * slots :]
    width = blocks * SUBN
    places = LANES // GROUP
    span = LANES * PIX

    def copy(frame, part):
        where = (frame, slice(None), pl.ds(part * span, span))
        return pltpu.make_async_copy(pixels.at[where], held.at[where], arrived.at[frame, part])

    for frame in range(frames):
        for part in range(blocks):
            copy(frame, part).start()
    row_table = row_moments(stripe)
    col_tables = [column_moments(chunk) for chunk in range(places)]
    slot = lax.axis_index("col") * cores + lax.axis_index("sub")
    position = lax.axis_index("row") * pieces + slot
    group = iota((stripe, LANES), 1) // GROUP

    def gather(pieces, kind):
        total = pieces[-1]
        for chunk in range(places - 1):
            total = jnp.where(group == (kind + chunk) % places, pieces[chunk], total)
        return pltpu.roll(total, LANES - GROUP * kind, 1) if kind else total

    row = iota((stripe, width), 0)
    column = iota((stripe, width), 1)

    def columns_of(lines):
        high, low = halves(lines)
        pieces = []
        for chunk in range(places):
            cut = slice(chunk * CHUNK, (chunk + 1) * CHUNK)
            weights = col_tables[chunk]
            pieces.append(dot(high[:, cut], weights) + dot(low[:, cut], weights))
        plain = [piece[:stripe] for piece in pieces]
        tilted = [piece[stripe : 2 * stripe] for piece in pieces]
        bent = [piece[2 * stripe :] for piece in pieces]
        return gather(plain, 0), gather(plain, 1), gather(tilted, 0), gather(plain, 2) + gather(bent, 0)

    def finish(frame, parts):
        intensity, moment_x, moment_y, moment_two = [jnp.concatenate(kind, 1) for kind in zip(*parts)]
        inverse = 1.0 / intensity
        slope_x = moment_x * inverse
        slope_y = moment_y * inverse
        spot_size = moment_two * inverse - slope_x * slope_x - slope_y * slope_y
        mean_flux = intensity * (1.0 / (PIX * PIX))
        flow_x = jnp.where(column < width - 1, slope_x, 0.0)
        flow_y = jnp.where(position * stripe + row < stripes * stripe - 1, slope_y, 0.0)
        left = jnp.where(column > 0, pltpu.roll(flow_x, 1, 1), 0.0)
        above = pltpu.roll(flow_y, 1, 0)
        source = left - flow_x + jnp.where(row > 0, above, 0.0) - flow_y
        spill = jnp.zeros((spill_rows(blocks), LANES), F32)
        spot_row = iota(spill.shape, 0)
        for block in range(blocks):
            last = flow_y[stripe - 1 :, block * SUBN : (block + 1) * SUBN]
            spill = jnp.where(spot_row == block, last, spill)
        fluxes = [mean_flux[:, block * SUBN : (block + 1) * SUBN] for block in range(blocks)]
        spots = [spot_size[:, block * SUBN : (block + 1) * SUBN] for block in range(blocks)]
        return source, spill, fluxes, spots

    def lines_of(frame):
        for part in range(blocks):
            copy(frame, part).wait()
        return [dot(row_table, held[frame, :, pl.ds(part * span, span)]) for part in range(blocks)]

    lines = [lines_of(frame) for frame in range(frames)]
    found = [finish(frame, [columns_of(part) for part in lines[frame]]) for frame in range(frames)]
    for piece in range(pieces):
        if slots > 1:
            target = slot ^ piece
            frame, block = target % cores, target // cores
            source, spill = [pick(frame, [one[kind] for one in found]) for kind in range(2)]
            flux, spot = [pick(frame, [pick(block, one[kind]) for one in found]) for kind in range(2, 4)]
            field, extra = fields[piece], extras[piece]
        else:
            frame, block = piece % cores, piece // cores
            source, spill, flux, spot = found[frame]
            flux, spot = flux[block], spot[block]
            field, extra = fields[0].at[piece], extras[0].at[piece]
        for block in range(blocks):
            field[block * stripe : (block + 1) * stripe, :] = source[:, block * SUBN : (block + 1) * SUBN]
        field[blocks * stripe :, :] = spill
        extra[:stripe, :] = flux
        extra[stripe:, :] = spot


def pieces_of(refs, slots, count, mine, order):
    if slots > 1:
        return [(mine ^ step, ref) for step, ref in zip((0,) + tuple(order), refs)]
    return [(step, refs[0].at[step]) for step in range(count)]


def tail_rows(blocks):
    return -(-(2 * blocks + padded(blocks) // LANES) // 8) * 8


def back_of(back, side, tiles):
    depth = tiles * LANES
    start = pl.multiple_of(side * (2 * depth), LANES)
    return back[pl.ds(start, depth), :], back[pl.ds(start + depth, depth), :]


def rims_kernel(sizes, *refs):
    stripe, pieces, blocks, cores, rows = sizes
    width = blocks * SUBN
    slots = pieces if swapped(pieces) else 1
    outs = rows if swapped(rows) else 1
    fields, refs = refs[:slots], refs[slots:]
    basis, back, left, real = refs[:4]
    sent, near, lined = refs[4 : 4 + outs], refs[4 + outs + 1], refs[4 + outs + 2]
    spectrum = refs[4 + outs]
    tiles = padded(blocks) // LANES
    mine = lax.axis_index("row")
    side = lax.axis_index("col")
    slot = side * cores + lax.axis_index("sub")
    arranged = pieces_of(fields, slots, pieces, slot, CELL_ORDER.get(pieces))
    lined[SUBN:, :] = jnp.zeros((16, lined.shape[1]), F32)
    for place, field in arranged:
        for block in range(blocks):
            where = pl.ds(pl.multiple_of(place * stripe, 8), stripe)
            lined[where, block * SUBN : (block + 1) * SUBN] = field[block * stripe : (block + 1) * stripe, :]
    first = iota((8, LANES), 0) == 0
    for place, field in arranged:
        head = pl.ds(pl.multiple_of((place + 1) * stripe, 8), 8)
        for block in range(blocks):
            cut = slice(block * SUBN, (block + 1) * SUBN)
            last = field[blocks * stripe + block : blocks * stripe + block + 1, :]
            lined[head, cut] = lined[head, cut] + jnp.where(first, last, 0.0)
    source = lined[...]
    across = dot_three(halves(source), (basis[:width, :], basis[width:, :]))
    driven = dot_stacked(left[:WIN, :], across)
    response = driven * real[:WIN, :]
    spectrum[...] = response
    edges = [dot_stacked(left[WIN : WIN + 16, :], response)]
    for place, start, count in ((WIN, 0, 8), (WIN + 8 * 16, SUBN - 8, 9)):
        total = across[start : start + 1] * real[place : place + 16, :]
        for step in range(1, count):
            table = real[place + 16 * step : place + 16 * step + 16, :]
            total = total + across[start + step : start + step + 1] * table
        edges.append(total)
    rims = dot_three(halves(jnp.concatenate(edges, 0)), back_of(back, side, tiles))
    near[:8, :] = jnp.where(mine > 0, rims[24:32], 0.0)
    near[8:, :] = jnp.where(mine < rows - 1, rims[32:40], 0.0)
    tail = tail_rows(blocks)
    total = jnp.sum(source[:SUBN], 0, keepdims=True)
    place = iota((tail, LANES), 0)
    sums = jnp.zeros((tail, LANES), F32)
    for block in range(blocks):
        cut = slice(block * SUBN, (block + 1) * SUBN)
        sums = jnp.where(place == block, total[:, cut], sums)
        sums = jnp.where(place == blocks + block, source[SUBN : SUBN + 1, cut], sums)
    for tile in range(tiles):
        cut = slice(tile * LANES, (tile + 1) * LANES)
        sums = jnp.where(place == 2 * blocks + tile, across[SUBN : SUBN + 1, cut], sums)
    for target, piece in pieces_of(sent, outs, rows, mine, range(1, rows)):
        ahead = target - mine
        rim = jnp.where(ahead == -1, rims[:8], 0.0)
        rim = jnp.where(ahead == 1, rims[8:16], rim)
        rim = jnp.where(ahead == -2, rims[16:24], rim)
        rim = jnp.where(ahead == 2, rims[40:], rim)
        piece[:8, :] = rim
        piece[8 : 8 + tail, :] = sums
        if piece.shape[-2] == 8 + tail:
            continue
        for tile in range(tiles):
            cut = slice(tile * LANES, (tile + 1) * LANES)
            line = jnp.where(ahead == -1, across[:8, cut], across[SUBN - 8 : SUBN, cut])
            piece[8 + tail + 8 * tile : 16 + tail + 8 * tile, :] = line


def outputs_kernel(sizes, *refs):
    stripe, pieces, blocks, cores, rows = sizes
    slots = pieces if swapped(pieces) else 1
    extras, (mean_flux, spot_size) = refs[:slots], refs[slots:]
    slot = lax.axis_index("col") * cores + lax.axis_index("sub")
    for place, extra in pieces_of(extras, slots, pieces, slot, CELL_ORDER.get(pieces)):
        where = pl.ds(pl.multiple_of(place * stripe, 8), stripe)
        mean_flux[0, where, :] = extra[:stripe, :]
        spot_size[0, where, :] = extra[stripe:, :]


def phase_kernel(sizes, *refs):
    stripe, pieces, blocks, cores, rows = sizes
    slots = pieces if swapped(pieces) else 1
    ins = rows if swapped(rows) else 1
    received, refs = refs[:ins], refs[ins:]
    spectrum, near, back, left, real = refs[:5]
    phase = refs[5]
    tiles = padded(blocks) // LANES
    mine = lax.axis_index("row")
    side = lax.axis_index("col")
    tail = tail_rows(blocks)
    arranged = pieces_of(received, ins, rows, mine, ORDER.get(rows))

    def of_row(row, where):
        if ins == 1:
            inside = jnp.logical_and(row >= 0, row < rows)
            return jnp.where(inside, received[0][jnp.clip(row, 0, rows - 1), where, :], 0.0)
        total = jnp.zeros((where.stop - where.start, LANES), F32)
        for origin, piece in arranged[1:]:
            if piece.shape[-2] < where.stop:
                continue
            total = jnp.where(origin == row, piece[where, :], total)
        return total

    above = of_row(mine - 1, slice(0, 8 + tail + 8 * tiles))
    below = of_row(mine + 1, slice(0, 8 + tail + 8 * tiles))
    first = iota((8, LANES), 0) == 0
    top, bottom, spilt = [], [], []
    empty = [jnp.zeros((8, LANES), F32)] * tiles
    for tile in range(tiles):
        lines = slice(8 + tail + 8 * tile, 16 + tail + 8 * tile)
        top.append(above[lines])
        bottom.append(below[lines])
        start = 8 + 2 * blocks + tile
        spilt.append(jnp.where(first, above[start : start + 1], 0.0))
    across = jnp.concatenate(
        [jnp.concatenate(part, 1) for part in (top, spilt, bottom, empty)], 0
    )
    halo = left[WIN + 16 + SUBN :, : 3 * across.shape[0]]
    driven = dot_stacked(halo, across)
    response = spectrum[...] + driven * real[:WIN, :]
    reach = dot_three(halves(response), back_of(back, side, tiles))
    solved = dot_stacked(left[WIN + 16 : WIN + 16 + SUBN, :], reach)
    coarse = WIN + 17 * 16
    weighted = jnp.zeros((tail, real.shape[1]), F32)
    for origin, piece in arranged:
        count = jnp.sum(piece[8 : 8 + tail, :], 1, keepdims=True)
        weighted = weighted + count * real[pl.ds(pl.multiple_of(coarse + origin * tail, 8), tail), :]
    own = iota(weighted.shape, 1) == mine * blocks + side
    level = jnp.sum(jnp.where(own, weighted, 0.0), keepdims=True)
    solved = solved + level
    rim = slice(0, 8)
    head = near[:8, :] + above[rim] + of_row(mine - 2, rim)
    foot = near[8:, :] + below[rim] + of_row(mine + 2, rim)
    phase[0, :8, :] = solved[:8] + head
    phase[0, 8 : SUBN - 8, :] = solved[8 : SUBN - 8]
    phase[0, SUBN - 8 :, :] = solved[SUBN - 8 :] + foot


def coarse_table(blocks_down, blocks_across, tail):
    inverse = coarse_inverse(blocks_down, blocks_across)
    number = blocks_down * blocks_across
    lanes = -(-number // LANES) * LANES
    table = np.zeros((blocks_down, tail, lanes), np.float32)
    for row in range(blocks_down):
        for block in range(blocks_across):
            table[row, block, :number] = inverse[row * blocks_across + block]
            if row + 1 < blocks_down:
                table[row, blocks_across + block, :number] = inverse[(row + 1) * blocks_across + block]
    return table


def in_vmem(count):
    return [pl.BlockSpec(memory_space=pltpu.VMEM)] * count


PARAMS = pltpu.CompilerParams(vmem_limit_bytes=48 * 1024 * 1024)


def body(pixels):
    frames, pixel_rows, pixel_cols = pixels.shape
    stripe = pixel_rows // PIX
    width = pixel_cols // PIX
    rows = lax.axis_size("row")
    blocks = lax.axis_size("col")
    cores = lax.axis_size("sub")
    pieces = blocks * cores
    assert frames == cores and width == blocks * SUBN and stripe * pieces == SUBN

    field_shapes = piece_shapes(pieces, (blocks * stripe + spill_rows(blocks), LANES))
    extra_shapes = piece_shapes(pieces, (2 * stripe, SUBN))
    made = pl.pallas_call(
        functools.partial(moments_kernel, (frames, stripe, blocks, cores, rows * pieces)),
        out_shape=field_shapes + extra_shapes,
        in_specs=[pl.BlockSpec(memory_space=pltpu.HBM)],
        out_specs=in_vmem(len(field_shapes + extra_shapes)),
        scratch_shapes=[
            pltpu.VMEM((frames, pixel_rows, pixel_cols), BF16),
            pltpu.SemaphoreType.DMA((frames, blocks)),
        ],
        compiler_params=PARAMS,
        name="moments",
    )(pltpu.with_memory_space_constraint(pixels, pltpu.HBM))
    fields = exchange(made[: len(field_shapes)], ("col", "sub"), pieces, CELL_ORDER)
    extras = exchange(made[len(field_shapes) :], ("col", "sub"), pieces, CELL_ORDER)

    vectors, scale = sine_basis()
    basis = column_basis(blocks)
    full = padded(blocks)
    tiles = full // LANES
    tail = tail_rows(blocks)
    short, height = 8 + tail, 8 + tail + 8 * tiles
    halo = np.zeros((WIN, 24))
    halo[:, :9] = vectors[:, :9]
    halo[:, 16:] = vectors[:, WIN - 8 :]
    lefts = [
        stacked_left(vectors[:, MARGIN:], WIN),
        stacked_left(np.concatenate([vectors[:8], vectors[WIN - 8 :]], 0), WIN),
        stacked_left(vectors[MARGIN : MARGIN + SUBN], WIN),
        np.pad(stacked_left(halo, 32), ((0, 0), (0, 3 * WIN - 96))),
    ]
    back = constant_pair(basis.T.reshape(full, blocks, SUBN).transpose(1, 0, 2))
    tables = [widened(table, blocks).reshape(-1, full) for table in (scale,) + edge_tables()]
    coarse = coarse_table(rows, blocks, tail)
    tables.append(np.pad(coarse, ((0, 0), (0, 0), (0, full - coarse.shape[2]))).reshape(-1, full))
    wide = jnp.asarray(np.concatenate(constant_pair(basis), 0))
    back = jnp.asarray(np.concatenate(back, 1).reshape(-1, SUBN))
    left = jnp.asarray(np.concatenate(lefts, 0))
    real = jnp.asarray(np.concatenate(tables, 0).astype(np.float32))

    row_shapes = piece_shapes(rows, (height, LANES))
    if swapped(rows):
        touching = [any(abs((row ^ k) - row) == 1 for row in range(rows)) for k in range(rows)]
        row_shapes = [jax.ShapeDtypeStruct((height if one else short, LANES), F32) for one in touching]
    sizes = (stripe, pieces, blocks, cores, rows)
    *sent, spectrum, near = pl.pallas_call(
        functools.partial(rims_kernel, sizes),
        out_shape=row_shapes
        + [jax.ShapeDtypeStruct((WIN, full), F32), jax.ShapeDtypeStruct((16, SUBN), F32)],
        in_specs=in_vmem(len(fields) + 4),
        out_specs=in_vmem(len(row_shapes) + 2),
        scratch_shapes=[pltpu.VMEM((SUBN + 16, width), F32)],
        compiler_params=PARAMS,
        name="rims",
    )(*fields, wide, back, left, real)
    received = exchange(sent, ("row",), rows, ORDER)

    mean_flux, spot_size = pl.pallas_call(
        functools.partial(outputs_kernel, sizes),
        out_shape=[jax.ShapeDtypeStruct((1, SUBN, SUBN), F32)] * 2,
        in_specs=in_vmem(len(extras)),
        out_specs=in_vmem(2),
        compiler_params=PARAMS,
        name="outputs",
    )(*extras)
    phase = pl.pallas_call(
        functools.partial(phase_kernel, sizes),
        out_shape=jax.ShapeDtypeStruct((1, SUBN, SUBN), F32),
        in_specs=in_vmem(len(received) + 5),
        out_specs=pl.BlockSpec(memory_space=pltpu.VMEM),
        compiler_params=PARAMS,
        name="phase",
    )(*received, spectrum, near, back, left, real)
    return phase, mean_flux, spot_size


def solution(mesh):
    placed = P(("groups", "sub"), "row", "col")
    return jax.shard_map(
        body,
        mesh=mesh,
        in_specs=(P("groups", ("row", "col", "sub"), None),),
        out_specs=(placed, placed, placed),
        check_vma=False,
    )
```
